512 devices in a mesh: seq: 128 (over z, y, core), head: 4 (over x).
Axes of the slice: x: 4, y: 8, z: 8, core: 2. Of those that a mesh axis runs over, the one named last changes fastest.
Arguments:
- hidden_states: bfloat16 [32768, 1536], P('seq', 'head'), may hold values from -60 to 60
- feature_q: bfloat16 [1536, 384], P(None, 'head'), may hold values from -0.15625 to 0.15625
- feature_k: bfloat16 [1536, 384], P(None, 'head'), may hold values from -0.15625 to 0.15625
- value_w: bfloat16 [1536, 1536], P(None, 'head'), may hold values from -0.15625 to 0.15625
- window_q: bfloat16 [1536, 1536], P(None, 'head'), may hold values from -0.15625 to 0.15625
- window_k: bfloat16 [1536, 1536], P(None, 'head'), may hold values from -0.15625 to 0.15625
- norm_gain: float32 [1536], P('head'), may hold values from 0.5 to 1.5
Outputs:
- mixed: bfloat16 [32768, 1536], P('seq', 'head')
The draws below stay inside these ranges and needn't reach their ends.
All inputs are finite; a program needn't handle non-finite values.
Results may differ from the reference program's by a relative error of at most 0.007.
Values may be sent and summed in bfloat16 or wider, within the bound.
No kernel may reach another device: no remote copies, remote signals or barrier semaphores. Data moves between devices by JAX's collectives and lax.ppermute only.
A program may use at most 128 MiB of HBM per device.

```python
import jax
import jax.numpy as jnp
from jax import lax

D = 1536
HEADS = 24
FK = 16
HV = 64
WINDOW_HEAD_SIZE = 64
WIN = 64
TOK_DEV = 256
FEAT = 273
SEQ = 32768


def draw_hidden_states(key, part):
    first = jax.random.fold_in(jax.random.fold_in(key, 17), 0)
    base = jnp.clip(jax.random.normal(first, (SEQ, D), jnp.float32), -6.0, 6.0)
    return base.astype(jnp.bfloat16)


def level_of(rng, dims, shards, least, largest):
    def one(dim, parts):
        draws = jax.random.uniform(jax.random.fold_in(jax.random.fold_in(rng, 6), dim), (parts,), jnp.float32, least / len(shards), largest / len(shards))
        return jnp.repeat(jnp.exp(draws), dims[dim] // parts).reshape((-1,) + (1,) * (len(dims) - dim - 1))

    loudness = one(*shards[0])
    for cut in shards[1:]:
        loudness = loudness * one(*cut)
    return loudness


def bell_draw(stream_key, dims, deviation, reach, cuts=(), kind=jnp.bfloat16):
    drawn = jax.random.normal(stream_key, dims, jnp.float32) * deviation
    if len(cuts) > 0:
        drawn = level_of(stream_key, dims, cuts, -0.22, 0.18) * drawn
    return jnp.clip(drawn, min=-reach, max=reach).astype(kind)


def setup_inputs(seed: int = 0) -> dict:
    splits = jax.random.split(jax.random.key(seed), 8)
    return {
        "hidden_states": draw_hidden_states(jax.random.fold_in(splits[7], 71), 0),
        "feature_q": bell_draw(splits[1], (D, HEADS * FK), D ** -0.5, 0.15625, ((1, 4),)),
        "feature_k": bell_draw(splits[2], (D, HEADS * FK), D ** -0.5, 0.15625, ((1, 4),)),
        "value_w": bell_draw(splits[3], (D, HEADS * HV), D ** -0.5, 0.15625, ((1, 4),)),
        "window_q": bell_draw(splits[4], (D, HEADS * WINDOW_HEAD_SIZE), D ** -0.5, 0.15625, ((1, 4),)),
        "window_k": bell_draw(splits[5], (D, HEADS * WINDOW_HEAD_SIZE), D ** -0.5, 0.15625, ((1, 4),)),
        "norm_gain": jnp.clip(1.0 + 0.1 * jax.random.normal(splits[6], (HEADS * HV,), jnp.float32), 0.5, 1.5),
    }


HIGH_ACCURACY = lax.Precision.HIGHEST

def expand(x):
    lead = x.shape[:-1]
    width = x.shape[-1]
    ones = jnp.ones(lead + (1,), jnp.float32)
    quad = (x[..., :, None] * x[..., None, :]).reshape(lead + (width * width,)) * 0.5 ** 0.5
    return jnp.concatenate([ones, x, quad], axis=-1)

def reference(hidden_states, feature_q, feature_k, value_w, window_q, window_k, norm_gain):
    count = SEQ // TOK_DEV
    blocks = hidden_states.reshape(count, TOK_DEV, D)
    order = jnp.arange(count, dtype=jnp.int32)

    def step(carry, item):
        state, prev_keys, prev_values = carry
        block, index = item
        offset = index * TOK_DEV
        query = (jnp.dot(block, feature_q, preferred_element_type=jnp.float32) * FK ** (-0.25)).reshape(TOK_DEV, HEADS, FK)
        key = (jnp.dot(block, feature_k, preferred_element_type=jnp.float32) * FK ** (-0.25)).reshape(TOK_DEV, HEADS, FK)
        values = jnp.dot(block, value_w, preferred_element_type=jnp.float32).astype(jnp.bfloat16)
        wquery = jnp.dot(block, window_q, preferred_element_type=jnp.float32).astype(jnp.bfloat16)
        wkey = jnp.dot(block, window_k, preferred_element_type=jnp.float32).astype(jnp.bfloat16)
        value3 = values.reshape(TOK_DEV, HEADS, HV).astype(jnp.float32)
        inner = jnp.einsum('lhf,mhf->hlm', query, key, precision=HIGH_ACCURACY)
        kernel = 1.0 + inner + 0.5 * inner * inner
        rows_i = jnp.arange(TOK_DEV, dtype=jnp.int32)
        causal = rows_i[:, None] >= rows_i[None, :]
        kernel = jnp.where(causal[None], kernel, 0.0).astype(jnp.bfloat16)
        intra = jnp.einsum('hlm,mhv->lhv', kernel.astype(jnp.float32), value3, precision=HIGH_ACCURACY)
        phi_q = expand(query)
        phi_k = expand(key)
        cross = jnp.einsum('lhf,fhv->lhv', phi_q, state, precision=HIGH_ACCURACY)
        linear = intra + cross
        scale = lax.rsqrt(lax.optimization_barrier(jnp.mean(linear * linear, axis=-1, keepdims=True)) + 1e-05)
        normed = linear * scale * norm_gain.reshape(HEADS, HV)
        key_rows_full = jnp.concatenate([prev_keys, wkey], axis=0).reshape(TOK_DEV + WIN, HEADS, WINDOW_HEAD_SIZE).astype(jnp.float32)
        values_all = jnp.concatenate([prev_values, values], axis=0).reshape(TOK_DEV + WIN, HEADS, HV).astype(jnp.float32)
        query_weight3 = wquery.reshape(TOK_DEV, HEADS, WINDOW_HEAD_SIZE).astype(jnp.float32)
        window_logits = jnp.einsum('qxo,bxo->xqb', query_weight3, key_rows_full, precision=HIGH_ACCURACY) * WINDOW_HEAD_SIZE ** (-0.5)
        query_pos = offset + rows_i[:, None]
        key_pos = offset - WIN + jnp.arange(TOK_DEV + WIN, dtype=jnp.int32)[None, :]
        valid = (key_pos <= query_pos) & (key_pos > query_pos - WIN) & (key_pos >= 0)
        window_logits = jnp.where(valid[None], window_logits, -1e+30)
        top = lax.optimization_barrier(jnp.max(window_logits, axis=-1, keepdims=True))
        expw = jnp.exp(window_logits - top)
        weights = (expw / lax.optimization_barrier(jnp.sum(expw, axis=-1, keepdims=True))).astype(jnp.bfloat16)
        window = jnp.einsum('hlm,mhv->lhv', weights.astype(jnp.float32), values_all, precision=HIGH_ACCURACY)
        mixed = (normed + window).astype(jnp.bfloat16).reshape(TOK_DEV, HEADS * HV)
        new_state = state + jnp.einsum('lhf,lhv->fhv', phi_k, value3, precision=HIGH_ACCURACY)
        return ((new_state, wkey[TOK_DEV - WIN:], values[TOK_DEV - WIN:]), mixed)
    init = (jnp.zeros((FEAT, HEADS, HV), jnp.float32), jnp.zeros((WIN, HEADS * WINDOW_HEAD_SIZE), jnp.bfloat16), jnp.zeros((WIN, HEADS * HV), jnp.bfloat16))
    carry, outputs = lax.scan(step, init, (blocks, order))
    return outputs.reshape(SEQ, HEADS * HV)
```

```python
import functools

import jax
import jax.numpy as jnp
from jax import lax
from jax.experimental import pallas as pl
from jax.experimental.pallas import tpu as pltpu
from jax.sharding import Mesh
from jax.sharding import PartitionSpec as P

FK = 16
HV = 64
WIN = 64
ROLLS = 8
BLOCKS = ROLLS + 2
PAIR_ROWS = BLOCKS * FK
SEQ = ("seq_0", "seq_1", "seq_2")
PLANE = ("seq_1", "seq_2")
F32 = jnp.float32
BF16 = jnp.bfloat16
NT = (((1,), (1,)), ((), ()))
VMEM_BYTES = 40 << 20


def dot(a, b):
    return jnp.dot(a, b, preferred_element_type=F32)


def project_transposed(w_ref, x_ref, rows, chunks):
    depth = x_ref.shape[1]
    total = None
    for c in range(chunks):
        part = lax.dot_general(
            w_ref[:, c * depth : (c + 1) * depth],
            x_ref[c * rows : (c + 1) * rows, :],
            NT,
            preferred_element_type=F32,
        )
        total = part if total is None else total + part
    return total * FK ** (-0.25)


def project(x_ref, w_ref, rows, chunks):
    depth = x_ref.shape[1]
    total = None
    for c in range(chunks):
        part = dot(x_ref[c * rows : (c + 1) * rows, :], w_ref[c * depth : (c + 1) * depth, :])
        total = part if total is None else total + part
    return total


def features(xt, weight, one):
    total, tokens = xt.shape
    x3 = xt.reshape(total // FK, FK, tokens)
    blocks = [(xt * xt * weight).astype(BF16)]
    for d in range(1, ROLLS):
        rolled = jnp.concatenate([x3[:, d:], x3[:, :d]], axis=1)
        blocks.append((x3 * rolled).reshape(total, tokens).astype(BF16))
    blocks.append(xt.astype(BF16))
    half = x3[:, : FK // 2] * x3[:, FK // 2 :]
    mixed = jnp.concatenate([half, jnp.full_like(half, one)], axis=1)
    blocks.append(mixed.reshape(total, tokens).astype(BF16))
    return blocks


def low_half(shape):
    return lax.broadcasted_iota(jnp.int32, shape, len(shape) - 1) < HV


def state_kernel(rows, chunks, x_ref, wk_ref, wv_ref, state_ref, kt_ref, v_ref):
    v = project(x_ref, wv_ref, rows, chunks).astype(BF16)
    v_ref[...] = v
    kt = project_transposed(wk_ref, x_ref, rows, chunks)
    kt_ref[...] = kt
    blocks = features(kt, 1.0, 1.0)
    pairs = v.shape[1] // 128
    for p in range(pairs):
        left = jnp.concatenate([b[32 * p : 32 * p + 32] for b in blocks], axis=0)
        both = dot(left, v[:, 128 * p : 128 * p + 128]).reshape(BLOCKS, 2, FK, 128)
        one = jnp.where(low_half((BLOCKS, FK, 128)), both[:, 0], both[:, 1])
        state_ref[PAIR_ROWS * p : PAIR_ROWS * (p + 1), :] = one.reshape(PAIR_ROWS, 128).astype(BF16)
    used = PAIR_ROWS * pairs
    state_ref[used:, :] = jnp.zeros((state_ref.shape[0] - used, 128), BF16)


def window_project_kernel(rows, chunks, x_ref, wq_ref, wk_ref, v_ref, oq_ref, ok_ref, halo_ref):
    oq_ref[...] = project(x_ref, wq_ref, rows, chunks).astype(BF16)
    keys = project(x_ref, wk_ref, rows, chunks).astype(BF16)
    ok_ref[...] = keys
    width = keys.shape[1]
    halo_ref[:, :width] = keys[rows - WIN :]
    halo_ref[:, width:] = v_ref[rows - WIN :, :]


def intra_kernel(rows, chunks, x_ref, wq_ref, kt_ref, v_ref, intra_ref, phi_ref):
    qt = project_transposed(wq_ref, x_ref, rows, chunks)
    blocks = features(qt, 0.5, 1.0 / (FK // 2))
    heads = qt.shape[0] // FK
    pad = jnp.zeros((384 - 2 * PAIR_ROWS, rows), F32)
    kt = kt_ref[...]
    q_hi = qt.astype(BF16).astype(F32)
    q_lo = qt - q_hi
    k_hi = kt.astype(BF16).astype(F32)
    k_lo = kt - k_hi
    zero = jnp.zeros((128 - 3 * FK, rows), F32)
    t = lax.broadcasted_iota(jnp.int32, (rows, rows), 0)
    s = lax.broadcasted_iota(jnp.int32, (rows, rows), 1)
    causal = t >= s
    for p in range(heads // 2):
        phi = jnp.concatenate([b[32 * p : 32 * p + 32].astype(F32) for b in blocks] + [pad], axis=0)
        phi_ref[:, 384 * p : 384 * (p + 1)] = phi.T.astype(BF16)
        vp = v_ref[:, 128 * p : 128 * p + 128]
        outs = []
        for h in (2 * p, 2 * p + 1):
            at = slice(FK * h, FK * (h + 1))
            left = jnp.concatenate([q_hi[at], q_hi[at], q_lo[at], zero], axis=0).T.astype(BF16)
            right = jnp.concatenate([k_hi[at], k_lo[at], k_hi[at], zero], axis=0).astype(BF16)
            a = dot(left, right)
            kern = jnp.where(causal, 1.0 + a + 0.5 * a * a, 0.0).astype(BF16)
            outs.append(dot(kern, vp))
        intra_ref[:, 128 * p : 128 * p + 128] = jnp.where(low_half((rows, 128)), outs[0], outs[1])


def window_kernel(rows, first_ref, q_ref, k_ref, v_ref, halo_ref, out_ref):
    width = k_ref.shape[1]
    first = first_ref[0]
    row = lax.broadcasted_iota(jnp.int32, (2 * WIN, 2 * WIN), 0) % WIN
    col = lax.broadcasted_iota(jnp.int32, (2 * WIN, 2 * WIN), 1)
    band = (col <= row + WIN) & (col > row)
    for t in range(rows // WIN):
        valid = band & ((col >= WIN) | (first == 0)) if t == 0 else band
        for p in range(width // 128):
            at = slice(128 * p, 128 * p + 128)
            if t == 0:
                keys = jnp.concatenate([halo_ref[:, at], k_ref[:WIN, at]], axis=0)
                vals = jnp.concatenate(
                    [halo_ref[:, width + 128 * p : width + 128 * p + 128], v_ref[:WIN, at]], axis=0
                )
            else:
                keys = k_ref[WIN * (t - 1) : WIN * (t + 1), at]
                vals = v_ref[WIN * (t - 1) : WIN * (t + 1), at]
            q = q_ref[WIN * t : WIN * (t + 1), at]
            low = low_half((WIN, 128))
            none = jnp.zeros_like(q)
            both = jnp.concatenate([jnp.where(low, q, none), jnp.where(low, none, q)], axis=0)
            logits = lax.dot_general(both, keys, NT, preferred_element_type=F32) * HV ** (-0.5)
            logits = jnp.where(valid, logits, -1e30)
            top = jnp.max(logits, axis=-1, keepdims=True)
            expw = jnp.exp(logits - top)
            weights = (expw / jnp.sum(expw, axis=-1, keepdims=True)).astype(BF16)
            mixed = dot(weights, vals)
            out_ref[WIN * t : WIN * (t + 1), at] = jnp.where(low, mixed[:WIN], mixed[WIN:])


def prefix_kernel(plane_ref, slices_ref, totals_ref, out_ref):
    plane = plane_ref[0]
    run = jnp.zeros(totals_ref.shape[1:], F32)
    for z in range(totals_ref.shape[0]):
        run = run + jnp.where(z < plane, totals_ref[z], 0.0)
    for i in range(slices_ref.shape[0]):
        out_ref[i] = run.astype(BF16)
        run = run + slices_ref[i].astype(F32)


def final_kernel(rows, state_ref, phi_ref, intra_ref, window_ref, gain_ref, out_ref):
    low_state = low_half((BLOCKS, FK, 128))
    i = lax.broadcasted_iota(jnp.int32, (256, 128), 0) % 128
    j = lax.broadcasted_iota(jnp.int32, (256, 128), 1)
    ones = jnp.where((i < HV) == (j < HV), 1.0 / HV, 0.0).astype(BF16)
    for p in range(intra_ref.shape[1] // 128):
        at = slice(128 * p, 128 * p + 128)
        state = state_ref[PAIR_ROWS * p : PAIR_ROWS * (p + 1), :].reshape(BLOCKS, FK, 128)
        none = jnp.zeros_like(state)
        even = jnp.where(low_state, state, none)[:, None]
        odd = jnp.where(low_state, none, state)[:, None]
        right = jnp.concatenate([even, odd], axis=1).reshape(2 * PAIR_ROWS, 128)
        right = jnp.concatenate([right, jnp.zeros((384 - 2 * PAIR_ROWS, 128), BF16)], axis=0)
        linear = intra_ref[:, at] + dot(phi_ref[:, 384 * p : 384 * (p + 1)], right)
        square = linear * linear
        hi = square.astype(BF16)
        lo = (square - hi.astype(F32)).astype(BF16)
        mean = dot(jnp.concatenate([hi, lo], axis=1), ones)
        normed = linear * lax.rsqrt(mean + 1e-5) * gain_ref[:, at]
        out_ref[:, at] = (normed + window_ref[:, at]).astype(BF16)


def call(kernel, outs, args, flops, scalars=0):
    outs = [jax.ShapeDtypeStruct(s, d) for s, d in outs]
    size = sum(a.size * a.dtype.itemsize for a in list(args) + outs)
    specs = [pl.BlockSpec(memory_space=pltpu.SMEM)] * scalars
    specs += [pl.BlockSpec(memory_space=pltpu.VMEM)] * (len(args) - scalars)
    return pl.pallas_call(
        kernel,
        out_shape=outs,
        in_specs=specs,
        out_specs=[pl.BlockSpec(memory_space=pltpu.VMEM)] * len(outs),
        compiler_params=pltpu.CompilerParams(vmem_limit_bytes=VMEM_BYTES),
        cost_estimate=pl.CostEstimate(flops=flops, bytes_accessed=size, transcendentals=0),
    )(*args)


def exchange(x, axis):
    return lax.all_to_all(x, axis, split_axis=0, concat_axis=0, tiled=True)


def body(hidden_states, feature_q, feature_k, value_w, window_q, window_k, norm_gain):
    rows = hidden_states.shape[0]
    chunks = lax.axis_size("head")
    width = value_w.shape[1]
    model = value_w.shape[0]
    few = feature_k.shape[1]
    planes, members = lax.axis_size("seq_0"), lax.axis_size("seq_1") * lax.axis_size("seq_2")
    plane = lax.axis_index("seq_0").astype(jnp.int32).reshape(1)
    first = (lax.axis_index(SEQ) == 0).astype(jnp.int32).reshape(1)
    piece = FK * members
    held = -(-PAIR_ROWS * width // (128 * piece)) * piece

    whole = lax.all_gather(hidden_states, "head", tiled=True)
    state, kt, v = call(
        functools.partial(state_kernel, rows, chunks),
        [((held, 128), BF16), ((few, rows), F32), ((rows, width), BF16)],
        [whole, feature_k.T, value_w],
        2 * rows * model * (few + width),
    )
    slices = exchange(state.reshape(members, held // members, 128), PLANE)
    wq, wk, halo = call(
        functools.partial(window_project_kernel, rows, chunks),
        [((rows, width), BF16), ((rows, width), BF16), ((WIN, 2 * width), BF16)],
        [whole, window_q, window_k, v],
        4 * rows * model * width,
    )
    devices = lax.axis_size(SEQ)
    halo = lax.ppermute(halo, SEQ, [(i, i + 1) for i in range(devices - 1)])
    total = jnp.sum(slices.astype(F32), axis=0)
    totals = exchange(jnp.broadcast_to(total, (planes, *total.shape)), "seq_0")
    intra, phi = call(
        functools.partial(intra_kernel, rows, chunks),
        [((rows, width), F32), ((rows, 3 * width), BF16)],
        [whole, feature_q.T, kt, v],
        2 * rows * model * few + 8 * rows * rows * width,
    )
    (before,) = call(
        prefix_kernel, [(slices.shape, BF16)], [plane, slices, totals], 10 * slices.size, 1
    )
    prefix = exchange(before, PLANE).reshape(held, 128)
    (window,) = call(
        functools.partial(window_kernel, rows),
        [((rows, width), F32)],
        [first, wq, wk, v, halo],
        16 * rows * WIN * width,
        1,
    )
    (mixed,) = call(
        functools.partial(final_kernel, rows),
        [((rows, width), BF16)],
        [prefix, phi, intra, window, norm_gain.reshape(1, width)],
        4 * rows * 384 * width,
    )
    return mixed


def solution(mesh):
    split = Mesh(
        mesh.devices.reshape(8, 8, 2, mesh.shape["head"]), ("seq_0", "seq_1", "seq_2", "head")
    )
    placed = (
        P(SEQ, "head"),
        P(None, "head"),
        P(None, "head"),
        P(None, "head"),
        P(None, "head"),
        P(None, "head"),
        P("head"),
    )
    return jax.shard_map(
        body, mesh=split, in_specs=placed, out_specs=P(SEQ, "head"), check_vma=False
    )
```

```python
import functools

import jax
import jax.numpy as jnp
from jax import lax
from jax.experimental import pallas as pl
from jax.experimental.pallas import tpu as pltpu
from jax.sharding import Mesh
from jax.sharding import PartitionSpec as P

FK = 16
HV = 64
WIN = 64
ROLLS = 8
BLOCKS = ROLLS + 2
PAIR_ROWS = BLOCKS * FK
SEQ = ("seq_0", "seq_1", "seq_2")
PLANE = ("seq_1", "seq_2")
F32 = jnp.float32
BF16 = jnp.bfloat16
NT = (((1,), (1,)), ((), ()))


def dot(a, b):
    return jnp.dot(a, b, preferred_element_type=F32)


def project_transposed(w_ref, x_ref, rows, chunks):
    depth = x_ref.shape[1]
    total = None
    for c in range(chunks):
        part = lax.dot_general(
            w_ref[:, c * depth : (c + 1) * depth],
            x_ref[c * rows : (c + 1) * rows, :],
            NT,
            preferred_element_type=F32,
        )
        total = part if total is None else total + part
    return total * FK ** (-0.25)


def project(x_ref, w_ref, rows, chunks):
    depth = x_ref.shape[1]
    total = None
    for c in range(chunks):
        part = dot(x_ref[c * rows : (c + 1) * rows, :], w_ref[c * depth : (c + 1) * depth, :])
        total = part if total is None else total + part
    return total


def features(xt, weight, one):
    total, tokens = xt.shape
    x3 = xt.reshape(total // FK, FK, tokens)
    blocks = [(xt * xt * weight).astype(BF16)]
    for d in range(1, ROLLS):
        rolled = jnp.concatenate([x3[:, d:], x3[:, :d]], axis=1)
        blocks.append((x3 * rolled).reshape(total, tokens).astype(BF16))
    blocks.append(xt.astype(BF16))
    half = x3[:, : FK // 2] * x3[:, FK // 2 :]
    mixed = jnp.concatenate([half, jnp.full_like(half, one)], axis=1)
    blocks.append(mixed.reshape(total, tokens).astype(BF16))
    return blocks


def low_half(shape):
    return lax.broadcasted_iota(jnp.int32, shape, len(shape) - 1) < HV


def state_kernel(rows, chunks, x_ref, wk_ref, wv_hbm, state_hbm, v_hbm, wv_ref, state_ref, v_ref, wv_sem, out_sem):
    depth = x_ref.shape[1]
    loads = []
    for c in range(chunks):
        at = pl.ds(c * depth, depth)
        loads.append(pltpu.make_async_copy(wv_hbm.at[at], wv_ref.at[at], wv_sem.at[c]))
        loads[c].start()
    blocks = features(project_transposed(wk_ref, x_ref, rows, chunks), 1.0, 1.0)
    total = None
    for c in range(chunks):
        loads[c].wait()
        part = dot(x_ref[c * rows : (c + 1) * rows, :], wv_ref[c * depth : (c + 1) * depth, :])
        total = part if total is None else total + part
    v = total.astype(BF16)
    v_ref[...] = v
    stores = [pltpu.make_async_copy(v_ref, v_hbm, out_sem.at[0])]
    stores[0].start()
    pairs = v.shape[1] // 128
    used = PAIR_ROWS * pairs
    state_ref[used:, :] = jnp.zeros((state_ref.shape[0] - used, 128), BF16)
    for p in range(pairs):
        left = jnp.concatenate([b[32 * p : 32 * p + 32] for b in blocks], axis=0)
        both = dot(left, v[:, 128 * p : 128 * p + 128]).reshape(BLOCKS, 2, FK, 128)
        one = jnp.where(low_half((BLOCKS, FK, 128)), both[:, 0], both[:, 1])
        state_ref[PAIR_ROWS * p : PAIR_ROWS * (p + 1), :] = one.reshape(PAIR_ROWS, 128).astype(BF16)
        size = PAIR_ROWS if p + 1 < pairs else state_ref.shape[0] - PAIR_ROWS * p
        at = pl.ds(PAIR_ROWS * p, size)
        stores.append(pltpu.make_async_copy(state_ref.at[at], state_hbm.at[at], out_sem.at[p + 1]))
        stores[p + 1].start()
    for store in stores:
        store.wait()


def window_band():
    row = lax.broadcasted_iota(jnp.int32, (2 * WIN, 2 * WIN), 0) % WIN
    col = lax.broadcasted_iota(jnp.int32, (2 * WIN, 2 * WIN), 1)
    return (col <= row + WIN) & (col > row), col


def window_tile(q, keys, vals, valid):
    low = low_half((WIN, 128))
    none = jnp.zeros_like(q)
    both = jnp.concatenate([jnp.where(low, q, none), jnp.where(low, none, q)], axis=0)
    logits = lax.dot_general(both, keys, NT, preferred_element_type=F32) * HV ** (-0.5)
    logits = jnp.where(valid, logits, -1e30)
    top = jnp.max(logits, axis=-1, keepdims=True)
    expw = jnp.exp(logits - top)
    weights = (expw / jnp.sum(expw, axis=-1, keepdims=True)).astype(BF16)
    mixed = dot(weights, vals)
    return jnp.where(low, mixed[:WIN], mixed[WIN:])


def window_kernel(rows, chunks, x_ref, wq_ref, wk_ref, v_ref, out_ref, head_ref, halo_ref):
    queries = project(x_ref, wq_ref, rows, chunks).astype(BF16)
    keys = project(x_ref, wk_ref, rows, chunks).astype(BF16)
    width = keys.shape[1]
    halo_ref[:, :width] = keys[rows - WIN :]
    halo_ref[:, width:] = v_ref[rows - WIN :, :]
    head_ref[:, :width] = queries[:WIN]
    head_ref[:, width : 2 * width] = keys[:WIN]
    head_ref[:, 2 * width :] = v_ref[:WIN, :]
    band, _ = window_band()
    for t in range(1, rows // WIN):
        for p in range(width // 128):
            at = slice(128 * p, 128 * p + 128)
            seen = slice(WIN * (t - 1), WIN * (t + 1))
            out_ref[WIN * (t - 1) : WIN * t, at] = window_tile(
                queries[WIN * t : WIN * (t + 1), at], keys[seen, at], v_ref[seen, at], band
            )


def first_window_kernel(first_ref, head_ref, halo_ref, out_ref):
    width = out_ref.shape[1]
    band, col = window_band()
    valid = band & ((col >= WIN) | (first_ref[0] == 0))
    for p in range(width // 128):
        at, at2, at3 = (slice(n * width + 128 * p, n * width + 128 * p + 128) for n in range(3))
        keys = jnp.concatenate([halo_ref[:, at], head_ref[:, at2]], axis=0)
        vals = jnp.concatenate([halo_ref[:, at2], head_ref[:, at3]], axis=0)
        out_ref[:, at] = window_tile(head_ref[:, at], keys, vals, valid)


def intra_kernel(rows, chunks, x_ref, wq_ref, wk_ref, v_ref, intra_ref, phi_ref):
    qt = project_transposed(wq_ref, x_ref, rows, chunks)
    kt = project_transposed(wk_ref, x_ref, rows, chunks)
    blocks = features(qt, 0.5, 1.0 / (FK // 2))
    heads = qt.shape[0] // FK
    pad = jnp.zeros((384 - 2 * PAIR_ROWS, rows), F32)
    q_hi = qt.astype(BF16).astype(F32)
    q_lo = qt - q_hi
    k_hi = kt.astype(BF16).astype(F32)
    k_lo = kt - k_hi
    zero = jnp.zeros((128 - 3 * FK, rows), F32)
    t = lax.broadcasted_iota(jnp.int32, (rows, rows), 0)
    s = lax.broadcasted_iota(jnp.int32, (rows, rows), 1)
    causal = t >= s
    for p in range(heads // 2):
        phi = jnp.concatenate([b[32 * p : 32 * p + 32].astype(F32) for b in blocks] + [pad], axis=0)
        phi_ref[:, 384 * p : 384 * (p + 1)] = phi.T.astype(BF16)
        vp = v_ref[:, 128 * p : 128 * p + 128]
        outs = []
        for h in (2 * p, 2 * p + 1):
            at = slice(FK * h, FK * (h + 1))
            left = jnp.concatenate([q_hi[at], q_hi[at], q_lo[at], zero], axis=0).T.astype(BF16)
            right = jnp.concatenate([k_hi[at], k_lo[at], k_hi[at], zero], axis=0).astype(BF16)
            a = dot(left, right)
            kern = jnp.where(causal, 1.0 + a + 0.5 * a * a, 0.0).astype(BF16)
            outs.append(dot(kern, vp))
        intra_ref[:, 128 * p : 128 * p + 128] = jnp.where(low_half((rows, 128)), outs[0], outs[1])


def total_kernel(slices_ref, out_ref):
    total = slices_ref[0].astype(F32)
    for i in range(1, slices_ref.shape[0]):
        total = total + slices_ref[i].astype(F32)
    for z in range(out_ref.shape[0]):
        out_ref[z] = total


def prefix_kernel(plane_ref, slices_ref, totals_ref, out_ref):
    plane = plane_ref[0]
    run = jnp.zeros(totals_ref.shape[1:], F32)
    for z in range(totals_ref.shape[0]):
        run = run + jnp.where(z < plane, totals_ref[z], 0.0)
    for i in range(slices_ref.shape[0]):
        out_ref[i] = run.astype(BF16)
        run = run + slices_ref[i].astype(F32)


def final_kernel(rows, state_ref, phi_ref, intra_ref, first_ref, window_ref, gain_ref, out_ref):
    low_state = low_half((BLOCKS, FK, 128))
    i = lax.broadcasted_iota(jnp.int32, (256, 128), 0) % 128
    j = lax.broadcasted_iota(jnp.int32, (256, 128), 1)
    ones = jnp.where((i < HV) == (j < HV), 1.0 / HV, 0.0).astype(BF16)
    for p in range(intra_ref.shape[1] // 128):
        at = slice(128 * p, 128 * p + 128)
        state = state_ref[PAIR_ROWS * p : PAIR_ROWS * (p + 1), :].reshape(BLOCKS, FK, 128)
        none = jnp.zeros_like(state)
        even = jnp.where(low_state, state, none)[:, None]
        odd = jnp.where(low_state, none, state)[:, None]
        right = jnp.concatenate([even, odd], axis=1).reshape(2 * PAIR_ROWS, 128)
        right = jnp.concatenate([right, jnp.zeros((384 - 2 * PAIR_ROWS, 128), BF16)], axis=0)
        linear = intra_ref[:, at] + dot(phi_ref[:, 384 * p : 384 * (p + 1)], right)
        square = linear * linear
        hi = square.astype(BF16)
        lo = (square - hi.astype(F32)).astype(BF16)
        mean = dot(jnp.concatenate([hi, lo], axis=1), ones)
        normed = linear * lax.rsqrt(mean + 1e-5) * gain_ref[:, at]
        out_ref[:WIN, at] = (normed[:WIN] + first_ref[:, at]).astype(BF16)
        out_ref[WIN:, at] = (normed[WIN:] + window_ref[:, at]).astype(BF16)


def call(kernel, outs, args, flops, scratch=(), vmem=12):
    arrays = [a if space is pltpu.SMEM else pltpu.with_memory_space_constraint(a, space) for a, space in args]
    size = sum(a.size * a.dtype.itemsize for a in arrays)

    def spec(space):
        return pl.BlockSpec(memory_space=pltpu.VMEM if space is pltpu.HBM and not scratch else space)

    return pl.pallas_call(
        kernel,
        out_shape=[space(shape, dtype) for shape, dtype, space in outs],
        in_specs=[spec(space) for _, space in args],
        out_specs=[spec(space) for _, _, space in outs],
        scratch_shapes=list(scratch),
        compiler_params=pltpu.CompilerParams(vmem_limit_bytes=vmem << 20),
        cost_estimate=pl.CostEstimate(flops=flops, bytes_accessed=size, transcendentals=0),
    )(*arrays)


def exchange(x, axis):
    return lax.all_to_all(x, axis, split_axis=0, concat_axis=0, tiled=True)


def body(hidden_states, feature_q, feature_k, value_w, window_q, window_k, norm_gain):
    rows = hidden_states.shape[0]
    chunks = lax.axis_size("head")
    width = value_w.shape[1]
    model = value_w.shape[0]
    few = feature_k.shape[1]
    planes, members = lax.axis_size("seq_0"), lax.axis_size("seq_1") * lax.axis_size("seq_2")
    plane = lax.axis_index("seq_0").astype(jnp.int32).reshape(1)
    first = (lax.axis_index(SEQ) == 0).astype(jnp.int32).reshape(1)
    piece = FK * members
    held = -(-PAIR_ROWS * width // (128 * piece)) * piece

    pairs = width // 128
    vmem, hbm, smem = pltpu.VMEM, pltpu.HBM, pltpu.SMEM

    whole = lax.all_gather(hidden_states, "head", tiled=True)
    state, v = call(
        functools.partial(state_kernel, rows, chunks),
        [((held, 128), BF16, hbm), ((rows, width), BF16, hbm)],
        [(whole, vmem), (feature_k.T, vmem), (value_w, hbm)],
        2 * rows * model * (few + width),
        scratch=[
            pltpu.VMEM((model, width), BF16),
            pltpu.VMEM((held, 128), BF16),
            pltpu.VMEM((rows, width), BF16),
            pltpu.SemaphoreType.DMA((chunks,)),
            pltpu.SemaphoreType.DMA((pairs + 1,)),
        ],
    )
    slices = exchange(state.reshape(members, held // members, 128), PLANE)
    window, head, halo = call(
        functools.partial(window_kernel, rows, chunks),
        [((rows - WIN, width), F32, hbm), ((WIN, 3 * width), BF16, hbm), ((WIN, 2 * width), BF16, hbm)],
        [(whole, vmem), (window_q, vmem), (window_k, vmem), (v, hbm)],
        4 * rows * model * width + 12 * rows * WIN * width,
    )
    slices, window, head, halo = lax.optimization_barrier((slices, window, head, halo))
    devices = lax.axis_size(SEQ)
    halo = lax.ppermute(halo, SEQ, [(i, i + 1) for i in range(devices - 1)])
    (totals,) = call(
        total_kernel, [((planes, *slices.shape[1:]), F32, hbm)], [(slices, vmem)], slices.size
    )
    totals = exchange(totals, "seq_0")
    intra, phi = call(
        functools.partial(intra_kernel, rows, chunks),
        [((rows, width), F32, vmem), ((rows, 3 * width), BF16, vmem)],
        [(whole, vmem), (feature_q.T, vmem), (feature_k.T, vmem), (v, hbm)],
        4 * rows * model * few + 8 * rows * rows * width,
    )
    totals, intra, phi = lax.optimization_barrier((totals, intra, phi))
    (before,) = call(
        prefix_kernel,
        [(slices.shape, BF16, hbm)],
        [(plane, smem), (slices, vmem), (totals, vmem)],
        10 * slices.size,
    )
    prefix = exchange(before, PLANE).reshape(held, 128)
    (early,) = call(
        first_window_kernel,
        [((WIN, width), F32, vmem)],
        [(first, smem), (head, vmem), (halo, vmem)],
        4 * WIN * WIN * width,
    )
    gain = norm_gain.reshape(1, width)
    (mixed,) = call(
        functools.partial(final_kernel, rows),
        [((rows, width), BF16, hbm)],
        [(a, vmem) for a in (prefix, phi, intra, early, window, gain)],
        4 * rows * 384 * width,
    )
    return mixed


def solution(mesh):
    split = Mesh(
        mesh.devices.reshape(8, 8, 2, mesh.shape["head"]), ("seq_0", "seq_1", "seq_2", "head")
    )
    placed = (
        P(SEQ, "head"),
        P(None, "head"),
        P(None, "head"),
        P(None, "head"),
        P(None, "head"),
        P(None, "head"),
        P("head"),
    )
    return jax.shard_map(
        body, mesh=split, in_specs=placed, out_specs=P(SEQ, "head"), check_vma=False
    )
```

```python
import functools

import jax
import jax.numpy as jnp
from jax import lax
from jax.experimental import pallas as pl
from jax.experimental.pallas import tpu as pltpu
from jax.sharding import Mesh
from jax.sharding import PartitionSpec as P

FK = 16
HV = 64
WIN = 64
ROLLS = 8
BLOCKS = ROLLS + 2
PAIR_ROWS = BLOCKS * FK
SEQ = ("seq_0", "seq_1", "seq_2")
PLANE = ("seq_1", "seq_2")
F32 = jnp.float32
BF16 = jnp.bfloat16
FLOPS_PER_NS = 1_000_000
NT = (((1,), (1,)), ((), ()))


def dot(a, b):
    return jnp.dot(a, b, preferred_element_type=F32)


def project_transposed(w_ref, x_ref, rows, chunks):
    depth = x_ref.shape[1]
    total = None
    for c in range(chunks):
        part = lax.dot_general(
            w_ref[:, c * depth : (c + 1) * depth],
            x_ref[c * rows : (c + 1) * rows, :],
            NT,
            preferred_element_type=F32,
        )
        total = part if total is None else total + part
    return total * FK ** (-0.25)


def project(x_ref, w_ref, rows, chunks):
    depth = x_ref.shape[1]
    total = None
    for c in range(chunks):
        part = dot(x_ref[c * rows : (c + 1) * rows, :], w_ref[c * depth : (c + 1) * depth, :])
        total = part if total is None else total + part
    return total


def features(xt, weight, one):
    total, tokens = xt.shape
    x3 = xt.reshape(total // FK, FK, tokens)
    blocks = [(xt * xt * weight).astype(BF16)]
    for d in range(1, ROLLS):
        rolled = jnp.concatenate([x3[:, d:], x3[:, :d]], axis=1)
        blocks.append((x3 * rolled).reshape(total, tokens).astype(BF16))
    blocks.append(xt.astype(BF16))
    half = x3[:, : FK // 2] * x3[:, FK // 2 :]
    mixed = jnp.concatenate([half, jnp.full_like(half, one)], axis=1)
    blocks.append(mixed.reshape(total, tokens).astype(BF16))
    return blocks


def low_half(shape):
    return lax.broadcasted_iota(jnp.int32, shape, len(shape) - 1) < HV


def feature_kernel(rows, chunks, x_ref, wk_ref, left_ref):
    blocks = features(project_transposed(wk_ref, x_ref, rows, chunks), 1.0, 1.0)
    for p in range(left_ref.shape[0]):
        for n, block in enumerate(blocks):
            left_ref[p, 32 * n : 32 * (n + 1), :] = block[32 * p : 32 * p + 32]


def state_kernel(rows, chunks, x_ref, wv_ref, left_ref, state_ref, v_ref):
    v = project(x_ref, wv_ref, rows, chunks).astype(BF16)
    v_ref[...] = v
    pairs = v.shape[1] // 128
    for p in range(pairs):
        both = dot(left_ref[p], v[:, 128 * p : 128 * p + 128]).reshape(BLOCKS, 2, FK, 128)
        one = jnp.where(low_half((BLOCKS, FK, 128)), both[:, 0], both[:, 1])
        state_ref[PAIR_ROWS * p : PAIR_ROWS * (p + 1), :] = one.reshape(PAIR_ROWS, 128).astype(BF16)
    used = PAIR_ROWS * pairs
    state_ref[used:, :] = jnp.zeros((state_ref.shape[0] - used, 128), BF16)


def window_project_kernel(rows, chunks, x_ref, wq_ref, wk_ref, v_ref, oq_ref, ok_ref, halo_ref):
    oq_ref[...] = project(x_ref, wq_ref, rows, chunks).astype(BF16)
    keys = project(x_ref, wk_ref, rows, chunks).astype(BF16)
    ok_ref[...] = keys
    width = keys.shape[1]
    halo_ref[:, :width] = keys[rows - WIN :]
    halo_ref[:, width:] = v_ref[rows - WIN :, :]


def window_kernel(rows, first_ref, q_ref, k_ref, v_ref, halo_ref, out_ref):
    width = k_ref.shape[1]
    row = lax.broadcasted_iota(jnp.int32, (2 * WIN, 2 * WIN), 0) % WIN
    col = lax.broadcasted_iota(jnp.int32, (2 * WIN, 2 * WIN), 1)
    band = (col <= row + WIN) & (col > row)
    low = low_half((WIN, 128))
    tiles = [(t, p) for t in range(rows // WIN) for p in range(width // 128)]

    def seen(ref, t, p, shift):
        at = slice(128 * p, 128 * p + 128)
        if t > 0:
            return ref[WIN * (t - 1) : WIN * (t + 1), at]
        return jnp.concatenate(
            [halo_ref[:, shift + 128 * p : shift + 128 * p + 128], ref[:WIN, at]], axis=0
        )

    logits = []
    for t, p in tiles:
        q = q_ref[WIN * t : WIN * (t + 1), 128 * p : 128 * p + 128]
        none = jnp.zeros_like(q)
        both = jnp.concatenate([jnp.where(low, q, none), jnp.where(low, none, q)], axis=0)
        score = lax.dot_general(both, seen(k_ref, t, p, 0), NT, preferred_element_type=F32)
        valid = band & ((col >= WIN) | (first_ref[0] == 0)) if t == 0 else band
        logits.append(jnp.where(valid, score * HV ** (-0.5), -1e30))
    logits = jnp.concatenate(logits, axis=0)
    expw = jnp.exp(logits - jnp.max(logits, axis=-1, keepdims=True))
    weights = (expw / jnp.sum(expw, axis=-1, keepdims=True)).astype(BF16)
    for n, (t, p) in enumerate(tiles):
        mixed = dot(weights[2 * WIN * n : 2 * WIN * (n + 1)], seen(v_ref, t, p, width))
        out_ref[WIN * t : WIN * (t + 1), 128 * p : 128 * p + 128] = jnp.where(low, mixed[:WIN], mixed[WIN:])


def intra_kernel(rows, chunks, x_ref, wq_ref, wk_ref, v_ref, intra_ref, phi_ref):
    qt = project_transposed(wq_ref, x_ref, rows, chunks)
    kt = project_transposed(wk_ref, x_ref, rows, chunks)
    blocks = features(qt, 0.5, 1.0 / (FK // 2))
    heads = qt.shape[0] // FK
    pad = jnp.zeros((384 - 2 * PAIR_ROWS, rows), F32)
    q_hi = qt.astype(BF16).astype(F32)
    q_lo = qt - q_hi
    k_hi = kt.astype(BF16).astype(F32)
    k_lo = kt - k_hi
    zero = jnp.zeros((128 - 3 * FK, rows), F32)
    t = lax.broadcasted_iota(jnp.int32, (rows, rows), 0)
    s = lax.broadcasted_iota(jnp.int32, (rows, rows), 1)
    causal = t >= s
    for p in range(heads // 2):
        phi = jnp.concatenate([b[32 * p : 32 * p + 32].astype(F32) for b in blocks] + [pad], axis=0)
        phi_ref[:, 384 * p : 384 * (p + 1)] = phi.T.astype(BF16)
        vp = v_ref[:, 128 * p : 128 * p + 128]
        outs = []
        for h in (2 * p, 2 * p + 1):
            at = slice(FK * h, FK * (h + 1))
            left = jnp.concatenate([q_hi[at], q_hi[at], q_lo[at], zero], axis=0).T.astype(BF16)
            right = jnp.concatenate([k_hi[at], k_lo[at], k_hi[at], zero], axis=0).astype(BF16)
            a = dot(left, right)
            kern = jnp.where(causal, 1.0 + a + 0.5 * a * a, 0.0).astype(BF16)
            outs.append(dot(kern, vp))
        intra_ref[:, 128 * p : 128 * p + 128] = jnp.where(low_half((rows, 128)), outs[0], outs[1])


def prefix_kernel(plane_ref, slices_ref, totals_ref, out_ref):
    plane = plane_ref[0]
    run = jnp.zeros(totals_ref.shape[1:], F32)
    for z in range(totals_ref.shape[0]):
        run = run + jnp.where(z < plane, totals_ref[z], 0.0)
    for i in range(slices_ref.shape[0]):
        out_ref[i] = run.astype(BF16)
        run = run + slices_ref[i].astype(F32)


def final_kernel(rows, state_ref, phi_ref, intra_ref, window_ref, gain_ref, out_ref):
    low_state = low_half((BLOCKS, FK, 128))
    i = lax.broadcasted_iota(jnp.int32, (256, 128), 0) % 128
    j = lax.broadcasted_iota(jnp.int32, (256, 128), 1)
    ones = jnp.where((i < HV) == (j < HV), 1.0 / HV, 0.0).astype(BF16)
    for p in range(intra_ref.shape[1] // 128):
        at = slice(128 * p, 128 * p + 128)
        state = state_ref[PAIR_ROWS * p : PAIR_ROWS * (p + 1), :].reshape(BLOCKS, FK, 128)
        none = jnp.zeros_like(state)
        even = jnp.where(low_state, state, none)[:, None]
        odd = jnp.where(low_state, none, state)[:, None]
        right = jnp.concatenate([even, odd], axis=1).reshape(2 * PAIR_ROWS, 128)
        right = jnp.concatenate([right, jnp.zeros((384 - 2 * PAIR_ROWS, 128), BF16)], axis=0)
        linear = intra_ref[:, at] + dot(phi_ref[:, 384 * p : 384 * (p + 1)], right)
        square = linear * linear
        hi = square.astype(BF16)
        lo = (square - hi.astype(F32)).astype(BF16)
        mean = dot(jnp.concatenate([hi, lo], axis=1), ones)
        normed = linear * lax.rsqrt(mean + 1e-5) * gain_ref[at].reshape(1, 128)
        out_ref[:, at] = (normed + window_ref[:, at]).astype(BF16)


def call(kernel, outs, args, nanoseconds, vmem=12):
    arrays = [a if space is pltpu.SMEM else pltpu.with_memory_space_constraint(a, space) for a, space in args]
    spaces = [space for _, space in args]

    def spec(space):
        return pl.BlockSpec(memory_space=pltpu.SMEM if space is pltpu.SMEM else pltpu.VMEM)

    return pl.pallas_call(
        kernel,
        out_shape=[space(shape, dtype) for shape, dtype, space in outs],
        in_specs=[spec(space) for space in spaces],
        out_specs=[spec(space) for _, _, space in outs],
        compiler_params=pltpu.CompilerParams(vmem_limit_bytes=vmem << 20),
        cost_estimate=pl.CostEstimate(
            flops=nanoseconds * FLOPS_PER_NS, bytes_accessed=0, transcendentals=0
        ),
    )(*arrays)


def exchange(x, axis):
    return lax.all_to_all(x, axis, split_axis=0, concat_axis=0, tiled=True)


def body(hidden_states, feature_q, feature_k, value_w, window_q, window_k, norm_gain):
    rows = hidden_states.shape[0]
    chunks = lax.axis_size("head")
    width = value_w.shape[1]
    model = value_w.shape[0]
    few = feature_k.shape[1]
    planes, members = lax.axis_size("seq_0"), lax.axis_size("seq_1") * lax.axis_size("seq_2")
    plane = lax.axis_index("seq_0").astype(jnp.int32).reshape(1)
    first = (lax.axis_index(SEQ) == 0).astype(jnp.int32).reshape(1)
    piece = FK * members
    held = -(-PAIR_ROWS * width // (128 * piece)) * piece

    pairs = width // 128
    vmem, hbm, smem = pltpu.VMEM, pltpu.HBM, pltpu.SMEM

    whole = lax.all_gather(hidden_states, "head", tiled=True)
    whole, plane, first = lax.optimization_barrier((whole, plane, first))
    (left,) = call(
        functools.partial(feature_kernel, rows, chunks),
        [((pairs, 2 * PAIR_ROWS, rows), BF16, vmem)],
        [(whole, vmem), (feature_k.T, vmem)],
        900,
    )
    state, v = call(
        functools.partial(state_kernel, rows, chunks),
        [((held, 128), BF16, vmem), ((rows, width), BF16, hbm)],
        [(whole, vmem), (value_w, vmem), (left, vmem)],
        1000,
    )
    slices = exchange(state.reshape(members, held // members, 128), PLANE)
    slices, v = lax.optimization_barrier((slices, v))
    total = jnp.sum(slices.astype(F32), axis=0)
    totals = exchange(jnp.broadcast_to(total, (planes, *total.shape)), "seq_0")
    wq, wk, halo = call(
        functools.partial(window_project_kernel, rows, chunks),
        [((rows, width), BF16, hbm), ((rows, width), BF16, hbm), ((WIN, 2 * width), BF16, hbm)],
        [(whole, vmem), (window_q, vmem), (window_k, vmem), (v, hbm)],
        1700,
    )
    devices = lax.axis_size(SEQ)
    halo = lax.ppermute(halo, SEQ, [(i, i + 1) for i in range(devices - 1)])
    intra, phi = call(
        functools.partial(intra_kernel, rows, chunks),
        [((rows, width), F32, vmem), ((rows, 3 * width), BF16, vmem)],
        [(whole, vmem), (feature_q.T, hbm), (feature_k.T, hbm), (v, hbm)],
        2200,
    )
    totals, wq, wk, halo, intra, phi = lax.optimization_barrier((totals, wq, wk, halo, intra, phi))
    (before,) = call(
        prefix_kernel,
        [(slices.shape, BF16, hbm)],
        [(plane, smem), (slices, vmem), (totals, vmem)],
        1000,
    )
    prefix = exchange(before, PLANE).reshape(held, 128)
    (window,) = call(
        functools.partial(window_kernel, rows),
        [((rows, width), F32, vmem)],
        [(first, smem), (wq, hbm), (wk, hbm), (v, hbm), (halo, vmem)],
        3000,
    )
    (mixed,) = call(
        functools.partial(final_kernel, rows),
        [((rows, width), BF16, hbm)],
        [(a, vmem) for a in (prefix, phi, intra, window, norm_gain)],
        1400,
    )
    return mixed


def solution(mesh):
    split = Mesh(
        mesh.devices.reshape(8, 8, 2, mesh.shape["head"]), ("seq_0", "seq_1", "seq_2", "head")
    )
    placed = (
        P(SEQ, "head"),
        P(None, "head"),
        P(None, "head"),
        P(None, "head"),
        P(None, "head"),
        P(None, "head"),
        P("head"),
    )
    return jax.shard_map(
        body, mesh=split, in_specs=placed, out_specs=P(SEQ, "head"), check_vma=False
    )
```

```python
import functools

import jax
import jax.numpy as jnp
from jax import lax
from jax.experimental import pallas as pl
from jax.experimental.pallas import tpu as pltpu
from jax.sharding import Mesh
from jax.sharding import PartitionSpec as P

FK = 16
HV = 64
WIN = 64
ROLLS = 8
BLOCKS = ROLLS + 2
PAIR_ROWS = BLOCKS * FK
SEQ = ("seq_0", "seq_1", "seq_2")
PLANE = ("seq_1", "seq_2")
F32 = jnp.float32
BF16 = jnp.bfloat16
FLOPS_PER_NS = 1_000_000
NT = (((1,), (1,)), ((), ()))


def dot(a, b):
    return jnp.dot(a, b, preferred_element_type=F32)


def project_transposed(w_ref, x_ref, rows, chunks):
    depth = x_ref.shape[1]
    total = None
    for c in range(chunks):
        part = lax.dot_general(
            w_ref[:, c * depth : (c + 1) * depth],
            x_ref[c * rows : (c + 1) * rows, :],
            NT,
            preferred_element_type=F32,
        )
        total = part if total is None else total + part
    return total * FK ** (-0.25)


def project(x_ref, w_ref, rows, chunks):
    depth = x_ref.shape[1]
    total = None
    for c in range(chunks):
        part = dot(x_ref[c * rows : (c + 1) * rows, :], w_ref[c * depth : (c + 1) * depth, :])
        total = part if total is None else total + part
    return total


def features(xt, weight, one):
    total, tokens = xt.shape
    x3 = xt.reshape(total // FK, FK, tokens)
    blocks = [(xt * xt * weight).astype(BF16)]
    for d in range(1, ROLLS):
        rolled = jnp.concatenate([x3[:, d:], x3[:, :d]], axis=1)
        blocks.append((x3 * rolled).reshape(total, tokens).astype(BF16))
    blocks.append(xt.astype(BF16))
    half = x3[:, : FK // 2] * x3[:, FK // 2 :]
    mixed = jnp.concatenate([half, jnp.full_like(half, one)], axis=1)
    blocks.append(mixed.reshape(total, tokens).astype(BF16))
    return blocks


def low_half(shape):
    return lax.broadcasted_iota(jnp.int32, shape, len(shape) - 1) < HV


def state_kernel(
    rows, chunks, x_ref, wk_hbm, wv_hbm, state_ref, v_hbm, wk_ref, wv_ref, v_ref, wk_sem, wv_sem, v_sem
):
    load = pltpu.make_async_copy(wk_hbm, wk_ref, wk_sem)
    load.start()
    parts = wv_sem.shape[0]
    piece = wv_ref.shape[0] // parts
    loads = []
    for n in range(parts):
        at = pl.ds(n * piece, piece)
        loads.append(pltpu.make_async_copy(wv_hbm.at[at], wv_ref.at[at], wv_sem.at[n]))
        loads[n].start()
    load.wait()
    blocks = features(project_transposed(wk_ref, x_ref, rows, chunks), 1.0, 1.0)
    depth = x_ref.shape[1]
    total = None
    for c in range(chunks):
        for n in range(c * parts // chunks, (c + 1) * parts // chunks):
            loads[n].wait()
        part = dot(x_ref[c * rows : (c + 1) * rows, :], wv_ref[c * depth : (c + 1) * depth, :])
        total = part if total is None else total + part
    v = total.astype(BF16)
    v_ref[...] = v
    store = pltpu.make_async_copy(v_ref, v_hbm, v_sem)
    store.start()
    pairs = v.shape[1] // 128
    for p in range(pairs):
        left = jnp.concatenate([b[32 * p : 32 * p + 32] for b in blocks], axis=0)
        both = dot(left, v[:, 128 * p : 128 * p + 128]).reshape(BLOCKS, 2, FK, 128)
        one = jnp.where(low_half((BLOCKS, FK, 128)), both[:, 0], both[:, 1])
        state_ref[PAIR_ROWS * p : PAIR_ROWS * (p + 1), :] = one.reshape(PAIR_ROWS, 128).astype(BF16)
    used = PAIR_ROWS * pairs
    state_ref[used:, :] = jnp.zeros((state_ref.shape[0] - used, 128), BF16)
    store.wait()


def window_key_kernel(rows, chunks, x_ref, w_ref, v_ref, out_ref, halo_ref):
    keys = project(x_ref, w_ref, rows, chunks).astype(BF16)
    out_ref[...] = keys
    width = keys.shape[1]
    halo_ref[:, :width] = keys[rows - WIN :]
    halo_ref[:, width:] = v_ref[rows - WIN :, :]


def window_query_kernel(rows, chunks, x_ref, w_ref, out_ref):
    out_ref[...] = project(x_ref, w_ref, rows, chunks).astype(BF16)


def window_kernel(rows, first_ref, q_ref, k_ref, v_ref, halo_ref, out_ref):
    width = k_ref.shape[1]
    row = lax.broadcasted_iota(jnp.int32, (2 * WIN, 2 * WIN), 0) % WIN
    col = lax.broadcasted_iota(jnp.int32, (2 * WIN, 2 * WIN), 1)
    band = (col <= row + WIN) & (col > row)
    low = low_half((WIN, 128))
    tiles = [(t, p) for t in range(rows // WIN) for p in range(width // 128)]

    def seen(ref, t, p, shift):
        at = slice(128 * p, 128 * p + 128)
        if t > 0:
            return ref[WIN * (t - 1) : WIN * (t + 1), at]
        return jnp.concatenate(
            [halo_ref[:, shift + 128 * p : shift + 128 * p + 128], ref[:WIN, at]], axis=0
        )

    logits = []
    for t, p in tiles:
        q = q_ref[WIN * t : WIN * (t + 1), 128 * p : 128 * p + 128]
        none = jnp.zeros_like(q)
        both = jnp.concatenate([jnp.where(low, q, none), jnp.where(low, none, q)], axis=0)
        score = lax.dot_general(both, seen(k_ref, t, p, 0), NT, preferred_element_type=F32)
        valid = band & ((col >= WIN) | (first_ref[0] == 0)) if t == 0 else band
        logits.append(jnp.where(valid, score * HV ** (-0.5), -1e30))
    logits = jnp.concatenate(logits, axis=0)
    expw = jnp.exp(logits - jnp.max(logits, axis=-1, keepdims=True))
    weights = (expw / jnp.sum(expw, axis=-1, keepdims=True)).astype(BF16)
    for n, (t, p) in enumerate(tiles):
        mixed = dot(weights[2 * WIN * n : 2 * WIN * (n + 1)], seen(v_ref, t, p, width))
        out_ref[WIN * t : WIN * (t + 1), 128 * p : 128 * p + 128] = jnp.where(low, mixed[:WIN], mixed[WIN:])


def intra_kernel(rows, chunks, x_ref, wq_ref, wk_ref, v_ref, intra_ref, phi_ref):
    qt = project_transposed(wq_ref, x_ref, rows, chunks)
    kt = project_transposed(wk_ref, x_ref, rows, chunks)
    blocks = features(qt, 0.5, 1.0 / (FK // 2))
    heads = qt.shape[0] // FK
    pad = jnp.zeros((384 - 2 * PAIR_ROWS, rows), F32)
    q_hi = qt.astype(BF16).astype(F32)
    q_lo = qt - q_hi
    k_hi = kt.astype(BF16).astype(F32)
    k_lo = kt - k_hi
    zero = jnp.zeros((128 - 3 * FK, rows), F32)
    t = lax.broadcasted_iota(jnp.int32, (rows, rows), 0)
    s = lax.broadcasted_iota(jnp.int32, (rows, rows), 1)
    causal = t >= s
    for p in range(heads // 2):
        phi = jnp.concatenate([b[32 * p : 32 * p + 32].astype(F32) for b in blocks] + [pad], axis=0)
        phi_ref[:, 384 * p : 384 * (p + 1)] = phi.T.astype(BF16)
        vp = v_ref[:, 128 * p : 128 * p + 128]
        outs = []
        for h in (2 * p, 2 * p + 1):
            at = slice(FK * h, FK * (h + 1))
            left = jnp.concatenate([q_hi[at], q_hi[at], q_lo[at], zero], axis=0).T.astype(BF16)
            right = jnp.concatenate([k_hi[at], k_lo[at], k_hi[at], zero], axis=0).astype(BF16)
            a = dot(left, right)
            kern = jnp.where(causal, 1.0 + a + 0.5 * a * a, 0.0).astype(BF16)
            outs.append(dot(kern, vp))
        intra_ref[:, 128 * p : 128 * p + 128] = jnp.where(low_half((rows, 128)), outs[0], outs[1])


def prefix_kernel(plane_ref, slices_ref, totals_ref, out_ref):
    plane = plane_ref[0]
    run = jnp.zeros(totals_ref.shape[1:], F32)
    for z in range(totals_ref.shape[0]):
        run = run + jnp.where(z < plane, totals_ref[z], 0.0)
    for i in range(slices_ref.shape[0]):
        out_ref[i] = run.astype(BF16)
        run = run + slices_ref[i].astype(F32)


def final_kernel(rows, state_ref, phi_ref, intra_ref, window_ref, gain_ref, out_ref):
    low_state = low_half((BLOCKS, FK, 128))
    i = lax.broadcasted_iota(jnp.int32, (256, 128), 0) % 128
    j = lax.broadcasted_iota(jnp.int32, (256, 128), 1)
    ones = jnp.where((i < HV) == (j < HV), 1.0 / HV, 0.0).astype(BF16)
    for p in range(intra_ref.shape[1] // 128):
        at = slice(128 * p, 128 * p + 128)
        state = state_ref[PAIR_ROWS * p : PAIR_ROWS * (p + 1), :].reshape(BLOCKS, FK, 128)
        none = jnp.zeros_like(state)
        even = jnp.where(low_state, state, none)[:, None]
        odd = jnp.where(low_state, none, state)[:, None]
        right = jnp.concatenate([even, odd], axis=1).reshape(2 * PAIR_ROWS, 128)
        right = jnp.concatenate([right, jnp.zeros((384 - 2 * PAIR_ROWS, 128), BF16)], axis=0)
        linear = intra_ref[:, at] + dot(phi_ref[:, 384 * p : 384 * (p + 1)], right)
        square = linear * linear
        hi = square.astype(BF16)
        lo = (square - hi.astype(F32)).astype(BF16)
        mean = dot(jnp.concatenate([hi, lo], axis=1), ones)
        normed = linear * lax.rsqrt(mean + 1e-5) * gain_ref[at].reshape(1, 128)
        out_ref[:, at] = (normed + window_ref[:, at]).astype(BF16)


def call(kernel, outs, args, nanoseconds, scratch=(), vmem=12):
    arrays = [a if space is pltpu.SMEM else pltpu.with_memory_space_constraint(a, space) for a, space in args]
    spaces = [space for _, space in args]
    size = sum(a.size * a.dtype.itemsize for a in arrays)

    def spec(space):
        return pl.BlockSpec(memory_space=pltpu.VMEM if space is pltpu.HBM and not scratch else space)

    return pl.pallas_call(
        kernel,
        out_shape=[space(shape, dtype) for shape, dtype, space in outs],
        in_specs=[spec(space) for space in spaces],
        out_specs=[spec(space) for _, _, space in outs],
        scratch_shapes=list(scratch),
        compiler_params=pltpu.CompilerParams(vmem_limit_bytes=vmem << 20),
        cost_estimate=pl.CostEstimate(
            flops=nanoseconds * FLOPS_PER_NS, bytes_accessed=size, transcendentals=0
        ),
    )(*arrays)


def exchange(x, axis):
    return lax.all_to_all(x, axis, split_axis=0, concat_axis=0, tiled=True)


def body(hidden_states, feature_q, feature_k, value_w, window_q, window_k, norm_gain):
    rows = hidden_states.shape[0]
    chunks = lax.axis_size("head")
    width = value_w.shape[1]
    model = value_w.shape[0]
    few = feature_k.shape[1]
    planes, members = lax.axis_size("seq_0"), lax.axis_size("seq_1") * lax.axis_size("seq_2")
    plane = lax.axis_index("seq_0").astype(jnp.int32).reshape(1)
    first = (lax.axis_index(SEQ) == 0).astype(jnp.int32).reshape(1)
    piece = FK * members
    held = -(-PAIR_ROWS * width // (128 * piece)) * piece

    vmem, hbm, smem = pltpu.VMEM, pltpu.HBM, pltpu.SMEM

    whole = lax.all_gather(hidden_states, "head", tiled=True)
    whole, plane, first = lax.optimization_barrier((whole, plane, first))
    state, v = call(
        functools.partial(state_kernel, rows, chunks),
        [((held, 128), BF16, vmem), ((rows, width), BF16, hbm)],
        [(whole, vmem), (feature_k.T, hbm), (value_w, hbm)],
        2200,
        scratch=[
            pltpu.VMEM((few, model), BF16),
            pltpu.VMEM((model, width), BF16),
            pltpu.VMEM((rows, width), BF16),
            pltpu.SemaphoreType.DMA(()),
            pltpu.SemaphoreType.DMA((2 * chunks,)),
            pltpu.SemaphoreType.DMA(()),
        ],
    )
    slices = exchange(state.reshape(members, held // members, 128), PLANE)
    slices, v = lax.optimization_barrier((slices, v))
    total = jnp.sum(slices.astype(F32), axis=0)
    totals = exchange(jnp.broadcast_to(total, (planes, *total.shape)), "seq_0")
    wk, halo = call(
        functools.partial(window_key_kernel, rows, chunks),
        [((rows, width), BF16, hbm), ((WIN, 2 * width), BF16, hbm)],
        [(whole, vmem), (window_k, vmem), (v, hbm)],
        1500,
    )
    devices = lax.axis_size(SEQ)
    halo = lax.ppermute(halo, SEQ, [(i, i + 1) for i in range(devices - 1)])
    (wq,) = call(
        functools.partial(window_query_kernel, rows, chunks),
        [((rows, width), BF16, hbm)],
        [(whole, vmem), (window_q, vmem)],
        1200,
    )
    totals, wq, wk, halo, v = lax.optimization_barrier((totals, wq, wk, halo, v))
    (before,) = call(
        prefix_kernel,
        [(slices.shape, BF16, hbm)],
        [(plane, smem), (slices, vmem), (totals, vmem)],
        1000,
    )
    prefix = exchange(before, PLANE).reshape(held, 128)
    intra, phi = call(
        functools.partial(intra_kernel, rows, chunks),
        [((rows, width), F32, vmem), ((rows, 3 * width), BF16, vmem)],
        [(whole, vmem), (feature_q.T, hbm), (feature_k.T, hbm), (v, hbm)],
        2200,
    )
    (window,) = call(
        functools.partial(window_kernel, rows),
        [((rows, width), F32, vmem)],
        [(first, smem), (wq, hbm), (wk, hbm), (v, hbm), (halo, vmem)],
        3000,
    )
    (mixed,) = call(
        functools.partial(final_kernel, rows),
        [((rows, width), BF16, hbm)],
        [(a, vmem) for a in (prefix, phi, intra, window, norm_gain)],
        1400,
    )
    return mixed


def solution(mesh):
    split = Mesh(
        mesh.devices.reshape(8, 8, 2, mesh.shape["head"]), ("seq_0", "seq_1", "seq_2", "head")
    )
    placed = (
        P(SEQ, "head"),
        P(None, "head"),
        P(None, "head"),
        P(None, "head"),
        P(None, "head"),
        P(None, "head"),
        P("head"),
    )
    return jax.shard_map(
        body, mesh=split, in_specs=placed, out_specs=P(SEQ, "head"), check_vma=False
    )
```

```python
import functools

import jax
import jax.numpy as jnp
from jax import lax
from jax.experimental import pallas as pl
from jax.experimental.pallas import tpu as pltpu
from jax.sharding import Mesh
from jax.sharding import PartitionSpec as P

FK = 16
HV = 64
WIN = 64
ROLLS = 8
BLOCKS = ROLLS + 2
PAIR_ROWS = BLOCKS * FK
SEQ = ("seq_0", "seq_1", "seq_2")
PLANE = ("seq_1", "seq_2")
F32 = jnp.float32
BF16 = jnp.bfloat16
FLOPS_PER_NS = 1_000_000
NT = (((1,), (1,)), ((), ()))


def dot(a, b):
    return jnp.dot(a, b, preferred_element_type=F32)


def project_transposed(w_ref, x_ref, rows, chunks):
    depth = x_ref.shape[1]
    total = None
    for c in range(chunks):
        part = lax.dot_general(
            w_ref[:, c * depth : (c + 1) * depth],
            x_ref[c * rows : (c + 1) * rows, :],
            NT,
            preferred_element_type=F32,
        )
        total = part if total is None else total + part
    return total * FK ** (-0.25)


def project(x_ref, w_ref, rows, chunks):
    depth = x_ref.shape[1]
    total = None
    for c in range(chunks):
        part = dot(x_ref[c * rows : (c + 1) * rows, :], w_ref[c * depth : (c + 1) * depth, :])
        total = part if total is None else total + part
    return total


def features(xt, weight, one):
    total, tokens = xt.shape
    x3 = xt.reshape(total // FK, FK, tokens)
    blocks = [(xt * xt * weight).astype(BF16)]
    for d in range(1, ROLLS):
        rolled = jnp.concatenate([x3[:, d:], x3[:, :d]], axis=1)
        blocks.append((x3 * rolled).reshape(total, tokens).astype(BF16))
    blocks.append(xt.astype(BF16))
    half = x3[:, : FK // 2] * x3[:, FK // 2 :]
    mixed = jnp.concatenate([half, jnp.full_like(half, one)], axis=1)
    blocks.append(mixed.reshape(total, tokens).astype(BF16))
    return blocks


def low_half(shape):
    return lax.broadcasted_iota(jnp.int32, shape, len(shape) - 1) < HV


def mean_kernel(out_ref):
    i = lax.broadcasted_iota(jnp.int32, out_ref.shape, 0) % 128
    j = lax.broadcasted_iota(jnp.int32, out_ref.shape, 1)
    out_ref[...] = jnp.where((i < HV) == (j < HV), 1.0 / HV, 0.0).astype(BF16)


def state_kernel(rows, chunks, x_ref, wk_ref, wv_ref, state_ref, v_hbm, v_ref, v_sem):
    v = project(x_ref, wv_ref, rows, chunks).astype(BF16)
    v_ref[...] = v
    store = pltpu.make_async_copy(v_ref, v_hbm, v_sem)
    store.start()
    blocks = features(project_transposed(wk_ref, x_ref, rows, chunks), 1.0, 1.0)
    pairs = v.shape[1] // 128
    for p in range(pairs):
        left = jnp.concatenate([b[32 * p : 32 * p + 32] for b in blocks], axis=0)
        both = dot(left, v[:, 128 * p : 128 * p + 128]).reshape(BLOCKS, 2, FK, 128)
        one = jnp.where(low_half((BLOCKS, FK, 128)), both[:, 0], both[:, 1])
        state_ref[PAIR_ROWS * p : PAIR_ROWS * (p + 1), :] = one.reshape(PAIR_ROWS, 128).astype(BF16)
    used = PAIR_ROWS * pairs
    state_ref[used:, :] = jnp.zeros((state_ref.shape[0] - used, 128), BF16)
    store.wait()


def window_key_kernel(rows, chunks, x_ref, w_ref, v_ref, out_ref, halo_ref):
    keys = project(x_ref, w_ref, rows, chunks).astype(BF16)
    out_ref[...] = keys
    width = keys.shape[1]
    halo_ref[:, :width] = keys[rows - WIN :]
    halo_ref[:, width:] = v_ref[rows - WIN :, :]


def window_query_kernel(rows, chunks, x_ref, w_ref, out_ref):
    out_ref[...] = project(x_ref, w_ref, rows, chunks).astype(BF16)


def window_kernel(rows, first_ref, q_ref, k_ref, v_ref, halo_ref, out_ref):
    width = k_ref.shape[1]
    row = lax.broadcasted_iota(jnp.int32, (2 * WIN, 2 * WIN), 0) % WIN
    col = lax.broadcasted_iota(jnp.int32, (2 * WIN, 2 * WIN), 1)
    band = (col <= row + WIN) & (col > row)
    low = low_half((WIN, 128))
    tiles = [(t, p) for t in range(rows // WIN) for p in range(width // 128)]

    def seen(ref, t, p, shift):
        at = slice(128 * p, 128 * p + 128)
        if t > 0:
            return ref[WIN * (t - 1) : WIN * (t + 1), at]
        return jnp.concatenate(
            [halo_ref[:, shift + 128 * p : shift + 128 * p + 128], ref[:WIN, at]], axis=0
        )

    logits = []
    for t, p in tiles:
        q = q_ref[WIN * t : WIN * (t + 1), 128 * p : 128 * p + 128]
        none = jnp.zeros_like(q)
        both = jnp.concatenate([jnp.where(low, q, none), jnp.where(low, none, q)], axis=0)
        score = lax.dot_general(both, seen(k_ref, t, p, 0), NT, preferred_element_type=F32)
        valid = band & ((col >= WIN) | (first_ref[0] == 0)) if t == 0 else band
        logits.append(jnp.where(valid, score * HV ** (-0.5), -1e30))
    logits = jnp.concatenate(logits, axis=0)
    expw = jnp.exp(logits - jnp.max(logits, axis=-1, keepdims=True))
    weights = (expw / jnp.sum(expw, axis=-1, keepdims=True)).astype(BF16)
    for n, (t, p) in enumerate(tiles):
        mixed = dot(weights[2 * WIN * n : 2 * WIN * (n + 1)], seen(v_ref, t, p, width))
        out_ref[WIN * t : WIN * (t + 1), 128 * p : 128 * p + 128] = jnp.where(low, mixed[:WIN], mixed[WIN:])


def intra_kernel(rows, chunks, x_ref, wq_ref, wk_ref, v_ref, intra_ref, phi_ref):
    qt = project_transposed(wq_ref, x_ref, rows, chunks)
    kt = project_transposed(wk_ref, x_ref, rows, chunks)
    blocks = features(qt, 0.5, 1.0 / (FK // 2))
    heads = qt.shape[0] // FK
    pad = jnp.zeros((384 - 2 * PAIR_ROWS, rows), F32)
    q_hi = qt.astype(BF16).astype(F32)
    q_lo = qt - q_hi
    k_hi = kt.astype(BF16).astype(F32)
    k_lo = kt - k_hi
    zero = jnp.zeros((128 - 3 * FK, rows), F32)
    t = lax.broadcasted_iota(jnp.int32, (rows, rows), 0)
    s = lax.broadcasted_iota(jnp.int32, (rows, rows), 1)
    causal = t >= s
    for p in range(heads // 2):
        phi = jnp.concatenate([b[32 * p : 32 * p + 32].astype(F32) for b in blocks] + [pad], axis=0)
        phi_ref[:, 384 * p : 384 * (p + 1)] = phi.T.astype(BF16)
        vp = v_ref[:, 128 * p : 128 * p + 128]
        outs = []
        for h in (2 * p, 2 * p + 1):
            at = slice(FK * h, FK * (h + 1))
            left = jnp.concatenate([q_hi[at], q_hi[at], q_lo[at], zero], axis=0).T.astype(BF16)
            right = jnp.concatenate([k_hi[at], k_lo[at], k_hi[at], zero], axis=0).astype(BF16)
            a = dot(left, right)
            kern = jnp.where(causal, 1.0 + a + 0.5 * a * a, 0.0).astype(BF16)
            outs.append(dot(kern, vp))
        intra_ref[:, 128 * p : 128 * p + 128] = jnp.where(low_half((rows, 128)), outs[0], outs[1])


def prefix_kernel(plane_ref, slices_ref, totals_ref, out_ref):
    plane = plane_ref[0]
    run = jnp.zeros(totals_ref.shape[1:], F32)
    for z in range(totals_ref.shape[0]):
        run = run + jnp.where(z < plane, totals_ref[z].astype(F32), 0.0)
    for i in range(slices_ref.shape[0]):
        out_ref[i] = run.astype(BF16)
        run = run + slices_ref[i].astype(F32)


def final_kernel(rows, state_ref, phi_ref, intra_ref, window_ref, gain_ref, mean_ref, out_ref):
    low_state = low_half((BLOCKS, FK, 128))
    for p in range(intra_ref.shape[1] // 128):
        at = slice(128 * p, 128 * p + 128)
        state = state_ref[PAIR_ROWS * p : PAIR_ROWS * (p + 1), :].reshape(BLOCKS, FK, 128)
        none = jnp.zeros_like(state)
        even = jnp.where(low_state, state, none)[:, None]
        odd = jnp.where(low_state, none, state)[:, None]
        right = jnp.concatenate([even, odd], axis=1).reshape(2 * PAIR_ROWS, 128)
        right = jnp.concatenate([right, jnp.zeros((384 - 2 * PAIR_ROWS, 128), BF16)], axis=0)
        linear = intra_ref[:, at] + dot(phi_ref[:, 384 * p : 384 * (p + 1)], right)
        square = linear * linear
        hi = square.astype(BF16)
        lo = (square - hi.astype(F32)).astype(BF16)
        mean = dot(jnp.concatenate([hi, lo], axis=1), mean_ref[...])
        normed = linear * lax.rsqrt(mean + 1e-5) * gain_ref[at].reshape(1, 128)
        out_ref[:, at] = (normed + window_ref[:, at]).astype(BF16)


def call(kernel, outs, args, nanoseconds, scratch=(), vmem=12):
    arrays = [a if space is pltpu.SMEM else pltpu.with_memory_space_constraint(a, space) for a, space in args]
    spaces = [space for _, space in args]
    size = sum(a.size * a.dtype.itemsize for a in arrays)

    def spec(space):
        return pl.BlockSpec(memory_space=pltpu.VMEM if space is pltpu.HBM and not scratch else space)

    return pl.pallas_call(
        kernel,
        out_shape=[space(shape, dtype) for shape, dtype, space in outs],
        in_specs=[spec(space) for space in spaces],
        out_specs=[spec(space) for _, _, space in outs],
        scratch_shapes=list(scratch),
        compiler_params=pltpu.CompilerParams(vmem_limit_bytes=vmem << 20),
        cost_estimate=pl.CostEstimate(
            flops=nanoseconds * FLOPS_PER_NS, bytes_accessed=size, transcendentals=0
        ),
    )(*arrays)


def exchange(x, axis):
    return lax.all_to_all(x, axis, split_axis=0, concat_axis=0, tiled=True)


def body(hidden_states, feature_q, feature_k, value_w, window_q, window_k, norm_gain):
    rows = hidden_states.shape[0]
    chunks = lax.axis_size("head")
    width = value_w.shape[1]
    model = value_w.shape[0]
    few = feature_k.shape[1]
    planes, members = lax.axis_size("seq_0"), lax.axis_size("seq_1") * lax.axis_size("seq_2")
    plane = lax.axis_index("seq_0").astype(jnp.int32).reshape(1)
    first = (lax.axis_index(SEQ) == 0).astype(jnp.int32).reshape(1)
    piece = FK * members
    held = -(-PAIR_ROWS * width // (128 * piece)) * piece

    vmem, hbm, smem = pltpu.VMEM, pltpu.HBM, pltpu.SMEM

    (mean,) = call(mean_kernel, [((256, 128), BF16, vmem)], [], 1000)
    hidden_states, mean, plane, first = lax.optimization_barrier((hidden_states, mean, plane, first))
    whole = lax.all_gather(hidden_states, "head", tiled=True)
    state, v = call(
        functools.partial(state_kernel, rows, chunks),
        [((held, 128), BF16, vmem), ((rows, width), BF16, hbm)],
        [(whole, vmem), (feature_k.T, vmem), (value_w, vmem)],
        1500,
        scratch=[pltpu.VMEM((rows, width), BF16), pltpu.SemaphoreType.DMA(())],
    )
    slices = exchange(state.reshape(members, held // members, 128), PLANE)
    slices, v = lax.optimization_barrier((slices, v))
    total = jnp.sum(slices.astype(F32), axis=0).astype(BF16)
    totals = exchange(jnp.broadcast_to(total, (planes, *total.shape)), "seq_0")
    wk, halo = call(
        functools.partial(window_key_kernel, rows, chunks),
        [((rows, width), BF16, hbm), ((WIN, 2 * width), BF16, hbm)],
        [(whole, vmem), (window_k, vmem), (v, hbm)],
        1500,
    )
    devices = lax.axis_size(SEQ)
    halo = lax.ppermute(halo, SEQ, [(i, i + 1) for i in range(devices - 1)])
    (wq,) = call(
        functools.partial(window_query_kernel, rows, chunks),
        [((rows, width), BF16, hbm)],
        [(whole, vmem), (window_q, vmem)],
        1200,
    )
    totals, wq, wk, halo, v = lax.optimization_barrier((totals, wq, wk, halo, v))
    (before,) = call(
        prefix_kernel,
        [(slices.shape, BF16, hbm)],
        [(plane, smem), (slices, vmem), (totals, vmem)],
        1000,
    )
    prefix = exchange(before, PLANE).reshape(held, 128)
    intra, phi = call(
        functools.partial(intra_kernel, rows, chunks),
        [((rows, width), F32, vmem), ((rows, 3 * width), BF16, vmem)],
        [(whole, vmem), (feature_q.T, hbm), (feature_k.T, hbm), (v, hbm)],
        2200,
    )
    (window,) = call(
        functools.partial(window_kernel, rows),
        [((rows, width), F32, vmem)],
        [(first, smem), (wq, hbm), (wk, hbm), (v, hbm), (halo, vmem)],
        3000,
    )
    (mixed,) = call(
        functools.partial(final_kernel, rows),
        [((rows, width), BF16, hbm)],
        [(a, vmem) for a in (prefix, phi, intra, window, norm_gain, mean)],
        1400,
    )
    return mixed


def solution(mesh):
    split = Mesh(
        mesh.devices.reshape(8, 8, 2, mesh.shape["head"]), ("seq_0", "seq_1", "seq_2", "head")
    )
    placed = (
        P(SEQ, "head"),
        P(None, "head"),
        P(None, "head"),
        P(None, "head"),
        P(None, "head"),
        P(None, "head"),
        P("head"),
    )
    return jax.shard_map(
        body, mesh=split, in_specs=placed, out_specs=P(SEQ, "head"), check_vma=False
    )
```

```python
import functools

import jax
import jax.numpy as jnp
from jax import lax
from jax.experimental import pallas as pl
from jax.experimental.pallas import tpu as pltpu
from jax.sharding import Mesh
from jax.sharding import PartitionSpec as P

FK = 16
HV = 64
WIN = 64
ROLLS = 8
BLOCKS = ROLLS + 2
PAIR_ROWS = BLOCKS * FK
SEQ = ("seq_0", "seq_1", "seq_2")
PLANE = ("seq_1", "seq_2")
F32 = jnp.float32
BF16 = jnp.bfloat16
FLOPS_PER_NS = 1_000_000
NT = (((1,), (1,)), ((), ()))


def dot(a, b):
    return jnp.dot(a, b, preferred_element_type=F32)


def project_transposed(w_ref, x_ref, rows, chunks):
    depth = x_ref.shape[1]
    total = None
    for c in range(chunks):
        part = lax.dot_general(
            w_ref[:, c * depth : (c + 1) * depth],
            x_ref[c * rows : (c + 1) * rows, :],
            NT,
            preferred_element_type=F32,
        )
        total = part if total is None else total + part
    return total * FK ** (-0.25)


def project(x_ref, w_ref, rows, chunks):
    depth = x_ref.shape[1]
    total = None
    for c in range(chunks):
        part = dot(x_ref[c * rows : (c + 1) * rows, :], w_ref[c * depth : (c + 1) * depth, :])
        total = part if total is None else total + part
    return total


def features(xt, weight, one):
    total, tokens = xt.shape
    x3 = xt.reshape(total // FK, FK, tokens)
    blocks = [(xt * xt * weight).astype(BF16)]
    for d in range(1, ROLLS):
        rolled = jnp.concatenate([x3[:, d:], x3[:, :d]], axis=1)
        blocks.append((x3 * rolled).reshape(total, tokens).astype(BF16))
    blocks.append(xt.astype(BF16))
    half = x3[:, : FK // 2] * x3[:, FK // 2 :]
    mixed = jnp.concatenate([half, jnp.full_like(half, one)], axis=1)
    blocks.append(mixed.reshape(total, tokens).astype(BF16))
    return blocks


def low_half(shape):
    return lax.broadcasted_iota(jnp.int32, shape, len(shape) - 1) < HV


def mean_kernel(out_ref):
    i = lax.broadcasted_iota(jnp.int32, out_ref.shape, 0) % 128
    j = lax.broadcasted_iota(jnp.int32, out_ref.shape, 1)
    out_ref[...] = jnp.where((i < HV) == (j < HV), 1.0 / HV, 0.0).astype(BF16)


def state_kernel(rows, chunks, x_ref, wk_ref, wv_ref, state_ref, v_hbm, v_ref, v_sem):
    v = project(x_ref, wv_ref, rows, chunks).astype(BF16)
    v_ref[...] = v
    store = pltpu.make_async_copy(v_ref, v_hbm, v_sem)
    store.start()
    blocks = features(project_transposed(wk_ref, x_ref, rows, chunks), 1.0, 1.0)
    pairs = v.shape[1] // 128
    for p in range(pairs):
        left = jnp.concatenate([b[32 * p : 32 * p + 32] for b in blocks], axis=0)
        both = dot(left, v[:, 128 * p : 128 * p + 128]).reshape(BLOCKS, 2, FK, 128)
        one = jnp.where(low_half((BLOCKS, FK, 128)), both[:, 0], both[:, 1])
        state_ref[PAIR_ROWS * p : PAIR_ROWS * (p + 1), :] = one.reshape(PAIR_ROWS, 128).astype(BF16)
    used = PAIR_ROWS * pairs
    state_ref[used:, :] = jnp.zeros((state_ref.shape[0] - used, 128), BF16)
    store.wait()


def window_tiles(tiles, valid):
    low = low_half((WIN, 128))
    logits = []
    for q, keys, _ in tiles:
        none = jnp.zeros_like(q)
        both = jnp.concatenate([jnp.where(low, q, none), jnp.where(low, none, q)], axis=0)
        score = lax.dot_general(both, keys, NT, preferred_element_type=F32)
        logits.append(jnp.where(valid, score * HV ** (-0.5), -1e30))
    logits = jnp.concatenate(logits, axis=0)
    expw = jnp.exp(logits - jnp.max(logits, axis=-1, keepdims=True))
    weights = (expw / jnp.sum(expw, axis=-1, keepdims=True)).astype(BF16)
    outs = []
    for n, (_, _, vals) in enumerate(tiles):
        mixed = dot(weights[2 * WIN * n : 2 * WIN * (n + 1)], vals)
        outs.append(jnp.where(low, mixed[:WIN], mixed[WIN:]))
    return outs


def window_band():
    row = lax.broadcasted_iota(jnp.int32, (2 * WIN, 2 * WIN), 0) % WIN
    col = lax.broadcasted_iota(jnp.int32, (2 * WIN, 2 * WIN), 1)
    return (col <= row + WIN) & (col > row), col


def window_kernel(rows, chunks, x_ref, wq_ref, wk_ref, v_ref, out_ref, head_ref, halo_ref):
    keys = project(x_ref, wk_ref, rows, chunks).astype(BF16)
    queries = project(x_ref, wq_ref, rows, chunks).astype(BF16)
    width = keys.shape[1]
    halo_ref[:, :width] = keys[rows - WIN :]
    halo_ref[:, width:] = v_ref[rows - WIN :, :]
    head_ref[:, :width] = queries[:WIN]
    head_ref[:, width : 2 * width] = keys[:WIN]
    head_ref[:, 2 * width :] = v_ref[:WIN, :]
    band, _ = window_band()
    places = [(t, p) for t in range(1, rows // WIN) for p in range(width // 128)]
    tiles = []
    for t, p in places:
        at, seen = slice(128 * p, 128 * p + 128), slice(WIN * (t - 1), WIN * (t + 1))
        tiles.append((queries[WIN * t : WIN * (t + 1), at], keys[seen, at], v_ref[seen, at]))
    for (t, p), out in zip(places, window_tiles(tiles, band)):
        out_ref[WIN * (t - 1) : WIN * t, 128 * p : 128 * p + 128] = out


def first_window_kernel(first_ref, head_ref, halo_ref, out_ref):
    width = out_ref.shape[1]
    band, col = window_band()
    valid = band & ((col >= WIN) | (first_ref[0] == 0))
    tiles = []
    for p in range(width // 128):
        at, at2, at3 = (slice(n * width + 128 * p, n * width + 128 * p + 128) for n in range(3))
        keys = jnp.concatenate([halo_ref[:, at], head_ref[:, at2]], axis=0)
        vals = jnp.concatenate([halo_ref[:, at2], head_ref[:, at3]], axis=0)
        tiles.append((head_ref[:, at], keys, vals))
    for p, out in enumerate(window_tiles(tiles, valid)):
        out_ref[:, 128 * p : 128 * p + 128] = out


def intra_kernel(rows, chunks, x_ref, wq_ref, wk_ref, v_ref, intra_ref, phi_ref):
    qt = project_transposed(wq_ref, x_ref, rows, chunks)
    kt = project_transposed(wk_ref, x_ref, rows, chunks)
    blocks = features(qt, 0.5, 1.0 / (FK // 2))
    heads = qt.shape[0] // FK
    pad = jnp.zeros((384 - 2 * PAIR_ROWS, rows), F32)
    q_hi = qt.astype(BF16).astype(F32)
    q_lo = qt - q_hi
    k_hi = kt.astype(BF16).astype(F32)
    k_lo = kt - k_hi
    zero = jnp.zeros((128 - 3 * FK, rows), F32)
    t = lax.broadcasted_iota(jnp.int32, (rows, rows), 0)
    s = lax.broadcasted_iota(jnp.int32, (rows, rows), 1)
    causal = t >= s
    for p in range(heads // 2):
        phi = jnp.concatenate([b[32 * p : 32 * p + 32].astype(F32) for b in blocks] + [pad], axis=0)
        phi_ref[:, 384 * p : 384 * (p + 1)] = phi.T.astype(BF16)
        vp = v_ref[:, 128 * p : 128 * p + 128]
        outs = []
        for h in (2 * p, 2 * p + 1):
            at = slice(FK * h, FK * (h + 1))
            left = jnp.concatenate([q_hi[at], q_hi[at], q_lo[at], zero], axis=0).T.astype(BF16)
            right = jnp.concatenate([k_hi[at], k_lo[at], k_hi[at], zero], axis=0).astype(BF16)
            a = dot(left, right)
            kern = jnp.where(causal, 1.0 + a + 0.5 * a * a, 0.0).astype(BF16)
            outs.append(dot(kern, vp))
        intra_ref[:, 128 * p : 128 * p + 128] = jnp.where(low_half((rows, 128)), outs[0], outs[1])


def prefix_kernel(plane_ref, slices_ref, totals_ref, out_ref):
    plane = plane_ref[0]
    run = jnp.zeros(totals_ref.shape[1:], F32)
    for z in range(totals_ref.shape[0]):
        run = run + jnp.where(z < plane, totals_ref[z].astype(F32), 0.0)
    for i in range(slices_ref.shape[0]):
        out_ref[i] = run.astype(BF16)
        run = run + slices_ref[i].astype(F32)


def final_kernel(
    rows, state_ref, phi_ref, intra_ref, early_ref, window_ref, gain_ref, mean_ref, out_hbm, out_ref, sem
):
    stores = []
    low_state = low_half((BLOCKS, FK, 128))
    for p in range(intra_ref.shape[1] // 128):
        at = slice(128 * p, 128 * p + 128)
        state = state_ref[PAIR_ROWS * p : PAIR_ROWS * (p + 1), :].reshape(BLOCKS, FK, 128)
        none = jnp.zeros_like(state)
        even = jnp.where(low_state, state, none)[:, None]
        odd = jnp.where(low_state, none, state)[:, None]
        right = jnp.concatenate([even, odd], axis=1).reshape(2 * PAIR_ROWS, 128)
        right = jnp.concatenate([right, jnp.zeros((384 - 2 * PAIR_ROWS, 128), BF16)], axis=0)
        linear = intra_ref[:, at] + dot(phi_ref[:, 384 * p : 384 * (p + 1)], right)
        square = linear * linear
        hi = square.astype(BF16)
        lo = (square - hi.astype(F32)).astype(BF16)
        mean = dot(jnp.concatenate([hi, lo], axis=1), mean_ref[...])
        normed = linear * lax.rsqrt(mean + 1e-5) * gain_ref[at].reshape(1, 128)
        out_ref[p, :WIN, :] = (normed[:WIN] + early_ref[:, at]).astype(BF16)
        out_ref[p, WIN:, :] = (normed[WIN:] + window_ref[:, at]).astype(BF16)
        stores.append(pltpu.make_async_copy(out_ref.at[p], out_hbm.at[:, at], sem.at[p]))
        stores[p].start()
    for store in stores:
        store.wait()


def call(kernel, outs, args, nanoseconds, scratch=(), vmem=12):
    arrays = [a if space is pltpu.SMEM else pltpu.with_memory_space_constraint(a, space) for a, space in args]
    spaces = [space for _, space in args]
    size = sum(a.size * a.dtype.itemsize for a in arrays)

    def spec(space):
        return pl.BlockSpec(memory_space=pltpu.VMEM if space is pltpu.HBM and not scratch else space)

    return pl.pallas_call(
        kernel,
        out_shape=[space(shape, dtype) for shape, dtype, space in outs],
        in_specs=[spec(space) for space in spaces],
        out_specs=[spec(space) for _, _, space in outs],
        scratch_shapes=list(scratch),
        compiler_params=pltpu.CompilerParams(vmem_limit_bytes=vmem << 20),
        cost_estimate=pl.CostEstimate(
            flops=nanoseconds * FLOPS_PER_NS, bytes_accessed=size, transcendentals=0
        ),
    )(*arrays)


def exchange(x, axis):
    return lax.all_to_all(x, axis, split_axis=0, concat_axis=0, tiled=True)


def body(hidden_states, feature_q, feature_k, value_w, window_q, window_k, norm_gain):
    rows = hidden_states.shape[0]
    chunks = lax.axis_size("head")
    width = value_w.shape[1]
    model = value_w.shape[0]
    few = feature_k.shape[1]
    planes, members = lax.axis_size("seq_0"), lax.axis_size("seq_1") * lax.axis_size("seq_2")
    plane = lax.axis_index("seq_0").astype(jnp.int32).reshape(1)
    first = (lax.axis_index(SEQ) == 0).astype(jnp.int32).reshape(1)
    piece = FK * members
    held = -(-PAIR_ROWS * width // (128 * piece)) * piece

    vmem, hbm, smem = pltpu.VMEM, pltpu.HBM, pltpu.SMEM

    (mean,) = call(mean_kernel, [((256, 128), BF16, vmem)], [], 200)
    hidden_states, mean, plane, first = lax.optimization_barrier((hidden_states, mean, plane, first))
    whole = lax.all_gather(hidden_states, "head", tiled=True)
    state, v = call(
        functools.partial(state_kernel, rows, chunks),
        [((held, 128), BF16, vmem), ((rows, width), BF16, hbm)],
        [(whole, vmem), (feature_k.T, vmem), (value_w, vmem)],
        1500,
        scratch=[pltpu.VMEM((rows, width), BF16), pltpu.SemaphoreType.DMA(())],
    )
    slices = exchange(state.reshape(members, held // members, 128), PLANE)
    slices, v = lax.optimization_barrier((slices, v))
    total = jnp.sum(slices.astype(F32), axis=0).astype(BF16)
    totals = exchange(jnp.broadcast_to(total, (planes, *total.shape)), "seq_0")
    window, head, halo = call(
        functools.partial(window_kernel, rows, chunks),
        [((rows - WIN, width), F32, hbm), ((WIN, 3 * width), BF16, hbm), ((WIN, 2 * width), BF16, hbm)],
        [(whole, vmem), (window_q, vmem), (window_k, vmem), (v, hbm)],
        3500,
    )
    intra, phi = call(
        functools.partial(intra_kernel, rows, chunks),
        [((rows, width), F32, vmem), ((rows, 3 * width), BF16, vmem)],
        [(whole, vmem), (feature_q.T, hbm), (feature_k.T, hbm), (v, hbm)],
        2200,
    )
    totals, window, head, halo, intra, phi = lax.optimization_barrier(
        (totals, window, head, halo, intra, phi)
    )
    (before,) = call(
        prefix_kernel,
        [(slices.shape, BF16, hbm)],
        [(plane, smem), (slices, vmem), (totals, vmem)],
        1000,
    )
    prefix = exchange(before, PLANE).reshape(held, 128)
    devices = lax.axis_size(SEQ)
    halo = lax.ppermute(halo, SEQ, [(i, i + 1) for i in range(devices - 1)])
    (early,) = call(
        first_window_kernel,
        [((WIN, width), F32, vmem)],
        [(first, smem), (head, vmem), (halo, vmem)],
        1000,
    )
    (mixed,) = call(
        functools.partial(final_kernel, rows),
        [((rows, width), BF16, hbm)],
        [(a, vmem) for a in (prefix, phi, intra, early, window, norm_gain, mean)],
        1400,
        scratch=[pltpu.VMEM((width // 128, rows, 128), BF16), pltpu.SemaphoreType.DMA((width // 128,))],
    )
    return mixed


def solution(mesh):
    split = Mesh(
        mesh.devices.reshape(8, 8, 2, mesh.shape["head"]), ("seq_0", "seq_1", "seq_2", "head")
    )
    placed = (
        P(SEQ, "head"),
        P(None, "head"),
        P(None, "head"),
        P(None, "head"),
        P(None, "head"),
        P(None, "head"),
        P("head"),
    )
    return jax.shard_map(
        body, mesh=split, in_specs=placed, out_specs=P(SEQ, "head"), check_vma=False
    )
```

```python
import functools

import jax
import jax.numpy as jnp
from jax import lax
from jax.experimental import pallas as pl
from jax.experimental.pallas import tpu as pltpu
from jax.sharding import Mesh
from jax.sharding import PartitionSpec as P

FK = 16
HV = 64
WIN = 64
ROLLS = 8
BLOCKS = ROLLS + 2
PAIR_ROWS = BLOCKS * FK
SEQ = ("seq_0", "seq_1", "seq_2")
PLANE = ("seq_1", "seq_2")
F32 = jnp.float32
BF16 = jnp.bfloat16
FLOPS_PER_NS = 1_000_000
NT = (((1,), (1,)), ((), ()))


def dot(a, b):
    return jnp.dot(a, b, preferred_element_type=F32)


def project_transposed(w_ref, x_ref, rows, chunks):
    depth = x_ref.shape[1]
    total = None
    for c in range(chunks):
        part = lax.dot_general(
            w_ref[:, c * depth : (c + 1) * depth],
            x_ref[c * rows : (c + 1) * rows, :],
            NT,
            preferred_element_type=F32,
        )
        total = part if total is None else total + part
    return total * FK ** (-0.25)


def project(x_ref, w_ref, rows, chunks):
    depth = x_ref.shape[1]
    total = None
    for c in range(chunks):
        part = dot(x_ref[c * rows : (c + 1) * rows, :], w_ref[c * depth : (c + 1) * depth, :])
        total = part if total is None else total + part
    return total


def features(xt, weight, one):
    total, tokens = xt.shape
    x3 = xt.reshape(total // FK, FK, tokens)
    blocks = [(xt * xt * weight).astype(BF16)]
    for d in range(1, ROLLS):
        rolled = jnp.concatenate([x3[:, d:], x3[:, :d]], axis=1)
        blocks.append((x3 * rolled).reshape(total, tokens).astype(BF16))
    blocks.append(xt.astype(BF16))
    half = x3[:, : FK // 2] * x3[:, FK // 2 :]
    mixed = jnp.concatenate([half, jnp.full_like(half, one)], axis=1)
    blocks.append(mixed.reshape(total, tokens).astype(BF16))
    return blocks


def low_half(shape):
    return lax.broadcasted_iota(jnp.int32, shape, len(shape) - 1) < HV


def mean_kernel(out_ref):
    i = lax.broadcasted_iota(jnp.int32, out_ref.shape, 0) % 128
    j = lax.broadcasted_iota(jnp.int32, out_ref.shape, 1)
    out_ref[...] = jnp.where((i < HV) == (j < HV), 1.0 / HV, 0.0).astype(BF16)


def state_kernel(rows, chunks, x_ref, wk_ref, wv_ref, state_ref, v_hbm, v_ref, v_sem):
    v = project(x_ref, wv_ref, rows, chunks).astype(BF16)
    v_ref[...] = v
    store = pltpu.make_async_copy(v_ref, v_hbm, v_sem)
    store.start()
    blocks = features(project_transposed(wk_ref, x_ref, rows, chunks), 1.0, 1.0)
    pairs = v.shape[1] // 128
    for p in range(pairs):
        left = jnp.concatenate([b[32 * p : 32 * p + 32] for b in blocks], axis=0)
        both = dot(left, v[:, 128 * p : 128 * p + 128]).reshape(BLOCKS, 2, FK, 128)
        one = jnp.where(low_half((BLOCKS, FK, 128)), both[:, 0], both[:, 1])
        state_ref[PAIR_ROWS * p : PAIR_ROWS * (p + 1), :] = one.reshape(PAIR_ROWS, 128).astype(BF16)
    used = PAIR_ROWS * pairs
    state_ref[used:, :] = jnp.zeros((state_ref.shape[0] - used, 128), BF16)
    store.wait()


def window_tiles(tiles, valid):
    low = low_half((WIN, 128))
    logits = []
    for q, keys, _ in tiles:
        none = jnp.zeros_like(q)
        both = jnp.concatenate([jnp.where(low, q, none), jnp.where(low, none, q)], axis=0)
        score = lax.dot_general(both, keys, NT, preferred_element_type=F32)
        logits.append(jnp.where(valid, score * HV ** (-0.5), -1e30))
    logits = jnp.concatenate(logits, axis=0)
    expw = jnp.exp(logits - jnp.max(logits, axis=-1, keepdims=True))
    weights = (expw / jnp.sum(expw, axis=-1, keepdims=True)).astype(BF16)
    outs = []
    for n, (_, _, vals) in enumerate(tiles):
        mixed = dot(weights[2 * WIN * n : 2 * WIN * (n + 1)], vals)
        outs.append(jnp.where(low, mixed[:WIN], mixed[WIN:]))
    return outs


def window_band():
    row = lax.broadcasted_iota(jnp.int32, (2 * WIN, 2 * WIN), 0) % WIN
    col = lax.broadcasted_iota(jnp.int32, (2 * WIN, 2 * WIN), 1)
    return (col <= row + WIN) & (col > row), col


def window_kernel(rows, chunks, x_ref, wq_ref, wk_ref, v_ref, out_ref, head_ref, halo_ref):
    keys = project(x_ref, wk_ref, rows, chunks).astype(BF16)
    queries = project(x_ref, wq_ref, rows, chunks).astype(BF16)
    width = keys.shape[1]
    halo_ref[:, :width] = keys[rows - WIN :]
    halo_ref[:, width:] = v_ref[rows - WIN :, :]
    head_ref[:, :width] = queries[:WIN]
    head_ref[:, width : 2 * width] = keys[:WIN]
    head_ref[:, 2 * width :] = v_ref[:WIN, :]
    band, _ = window_band()
    places = [(t, p) for t in range(1, rows // WIN) for p in range(width // 128)]
    tiles = []
    for t, p in places:
        at, seen = slice(128 * p, 128 * p + 128), slice(WIN * (t - 1), WIN * (t + 1))
        tiles.append((queries[WIN * t : WIN * (t + 1), at], keys[seen, at], v_ref[seen, at]))
    for (t, p), out in zip(places, window_tiles(tiles, band)):
        out_ref[WIN * (t - 1) : WIN * t, 128 * p : 128 * p + 128] = out


def first_window_kernel(first_ref, head_ref, halo_ref, out_ref):
    width = out_ref.shape[1]
    band, col = window_band()
    valid = band & ((col >= WIN) | (first_ref[0] == 0))
    tiles = []
    for p in range(width // 128):
        at, at2, at3 = (slice(n * width + 128 * p, n * width + 128 * p + 128) for n in range(3))
        keys = jnp.concatenate([halo_ref[:, at], head_ref[:, at2]], axis=0)
        vals = jnp.concatenate([halo_ref[:, at2], head_ref[:, at3]], axis=0)
        tiles.append((head_ref[:, at], keys, vals))
    for p, out in enumerate(window_tiles(tiles, valid)):
        out_ref[:, 128 * p : 128 * p + 128] = out


def intra_kernel(rows, chunks, x_ref, wq_ref, wk_ref, v_ref, intra_ref, phi_ref):
    qt = project_transposed(wq_ref, x_ref, rows, chunks)
    kt = project_transposed(wk_ref, x_ref, rows, chunks)
    blocks = features(qt, 0.5, 1.0 / (FK // 2))
    heads = qt.shape[0] // FK
    pad = jnp.zeros((384 - 2 * PAIR_ROWS, rows), F32)
    q_hi = qt.astype(BF16).astype(F32)
    q_lo = qt - q_hi
    k_hi = kt.astype(BF16).astype(F32)
    k_lo = kt - k_hi
    zero = jnp.zeros((128 - 3 * FK, rows), F32)
    t = lax.broadcasted_iota(jnp.int32, (rows, rows), 0)
    s = lax.broadcasted_iota(jnp.int32, (rows, rows), 1)
    causal = t >= s
    for p in range(heads // 2):
        phi = jnp.concatenate([b[32 * p : 32 * p + 32].astype(F32) for b in blocks] + [pad], axis=0)
        phi_ref[:, 384 * p : 384 * (p + 1)] = phi.T.astype(BF16)
        vp = v_ref[:, 128 * p : 128 * p + 128]
        outs = []
        for h in (2 * p, 2 * p + 1):
            at = slice(FK * h, FK * (h + 1))
            left = jnp.concatenate([q_hi[at], q_hi[at], q_lo[at], zero], axis=0).T.astype(BF16)
            right = jnp.concatenate([k_hi[at], k_lo[at], k_hi[at], zero], axis=0).astype(BF16)
            a = dot(left, right)
            kern = jnp.where(causal, 1.0 + a + 0.5 * a * a, 0.0).astype(BF16)
            outs.append(dot(kern, vp))
        intra_ref[:, 128 * p : 128 * p + 128] = jnp.where(low_half((rows, 128)), outs[0], outs[1])


def total_kernel(slices_ref, out_hbm, total_ref, sem):
    total = slices_ref[0].astype(F32)
    for i in range(1, slices_ref.shape[0]):
        total = total + slices_ref[i].astype(F32)
    total_ref[...] = total.astype(BF16)
    stores = [pltpu.make_async_copy(total_ref, out_hbm.at[z], sem.at[z]) for z in range(out_hbm.shape[0])]
    for store in stores:
        store.start()
    for store in stores:
        store.wait()


def prefix_kernel(plane_ref, slices_ref, totals_ref, out_hbm, out_ref, sem):
    plane = plane_ref[0]
    run = jnp.zeros(totals_ref.shape[1:], F32)
    for z in range(totals_ref.shape[0]):
        run = run + jnp.where(z < plane, totals_ref[z].astype(F32), 0.0)
    stores = []
    each = slices_ref.shape[0] // sem.shape[0]
    for n in range(sem.shape[0]):
        for i in range(each * n, each * (n + 1)):
            out_ref[i] = run.astype(BF16)
            run = run + slices_ref[i].astype(F32)
        at = pl.ds(each * n, each)
        stores.append(pltpu.make_async_copy(out_ref.at[at], out_hbm.at[at], sem.at[n]))
        stores[n].start()
    for store in stores:
        store.wait()


def final_kernel(
    rows, state_ref, phi_ref, intra_ref, early_ref, window_ref, gain_ref, mean_ref, out_hbm, out_ref, sem
):
    low_state = low_half((BLOCKS, FK, 128))
    pairs = [slice(128 * p, 128 * p + 128) for p in range(intra_ref.shape[1] // 128)]
    linears, squares = [], []
    for p, at in enumerate(pairs):
        state = state_ref[PAIR_ROWS * p : PAIR_ROWS * (p + 1), :].reshape(BLOCKS, FK, 128)
        none = jnp.zeros_like(state)
        even = jnp.where(low_state, state, none)[:, None]
        odd = jnp.where(low_state, none, state)[:, None]
        right = jnp.concatenate([even, odd], axis=1).reshape(2 * PAIR_ROWS, 128)
        right = jnp.concatenate([right, jnp.zeros((384 - 2 * PAIR_ROWS, 128), BF16)], axis=0)
        linears.append(intra_ref[:, at] + dot(phi_ref[:, 384 * p : 384 * (p + 1)], right))
    for linear in linears:
        square = linear * linear
        hi = square.astype(BF16)
        lo = (square - hi.astype(F32)).astype(BF16)
        squares.append(dot(jnp.concatenate([hi, lo], axis=1), mean_ref[...]))
    stores = []
    for p, at in enumerate(pairs):
        normed = linears[p] * lax.rsqrt(squares[p] + 1e-5) * gain_ref[at].reshape(1, 128)
        out_ref[p, :WIN, :] = (normed[:WIN] + early_ref[:, at]).astype(BF16)
        out_ref[p, WIN:, :] = (normed[WIN:] + window_ref[:, at]).astype(BF16)
        stores.append(pltpu.make_async_copy(out_ref.at[p], out_hbm.at[:, at], sem.at[p]))
        stores[p].start()
    for store in stores:
        store.wait()


def call(kernel, outs, args, nanoseconds, scratch=(), vmem=12):
    arrays = [a if space is pltpu.SMEM else pltpu.with_memory_space_constraint(a, space) for a, space in args]
    spaces = [space for _, space in args]
    size = sum(a.size * a.dtype.itemsize for a in arrays)

    def spec(space):
        return pl.BlockSpec(memory_space=pltpu.VMEM if space is pltpu.HBM and not scratch else space)

    return pl.pallas_call(
        kernel,
        out_shape=[space(shape, dtype) for shape, dtype, space in outs],
        in_specs=[spec(space) for space in spaces],
        out_specs=[spec(space) for _, _, space in outs],
        scratch_shapes=list(scratch),
        compiler_params=pltpu.CompilerParams(vmem_limit_bytes=vmem << 20),
        cost_estimate=pl.CostEstimate(
            flops=nanoseconds * FLOPS_PER_NS, bytes_accessed=size, transcendentals=0
        ),
    )(*arrays)


def exchange(x, axis):
    return lax.all_to_all(x, axis, split_axis=0, concat_axis=0, tiled=True)


def body(hidden_states, feature_q, feature_k, value_w, window_q, window_k, norm_gain):
    rows = hidden_states.shape[0]
    chunks = lax.axis_size("head")
    width = value_w.shape[1]
    model = value_w.shape[0]
    few = feature_k.shape[1]
    planes, members = lax.axis_size("seq_0"), lax.axis_size("seq_1") * lax.axis_size("seq_2")
    plane = lax.axis_index("seq_0").astype(jnp.int32).reshape(1)
    first = (lax.axis_index(SEQ) == 0).astype(jnp.int32).reshape(1)
    piece = FK * members
    held = -(-PAIR_ROWS * width // (128 * piece)) * piece

    vmem, hbm, smem = pltpu.VMEM, pltpu.HBM, pltpu.SMEM

    (mean,) = call(mean_kernel, [((256, 128), BF16, vmem)], [], 200)
    hidden_states, mean, plane, first = lax.optimization_barrier((hidden_states, mean, plane, first))
    whole = lax.all_gather(hidden_states, "head", tiled=True)
    state, v = call(
        functools.partial(state_kernel, rows, chunks),
        [((held, 128), BF16, vmem), ((rows, width), BF16, hbm)],
        [(whole, vmem), (feature_k.T, vmem), (value_w, vmem)],
        1500,
        scratch=[pltpu.VMEM((rows, width), BF16), pltpu.SemaphoreType.DMA(())],
    )
    slices = exchange(state.reshape(members, held // members, 128), PLANE)
    slices, v = lax.optimization_barrier((slices, v))
    piece_shape = slices.shape[1:]
    (totals,) = call(
        total_kernel,
        [((planes, *piece_shape), BF16, hbm)],
        [(slices, vmem)],
        600,
        scratch=[pltpu.VMEM(piece_shape, BF16), pltpu.SemaphoreType.DMA((planes,))],
    )
    totals = exchange(totals, "seq_0")
    window, head, halo = call(
        functools.partial(window_kernel, rows, chunks),
        [((rows - WIN, width), F32, hbm), ((WIN, 3 * width), BF16, hbm), ((WIN, 2 * width), BF16, hbm)],
        [(whole, vmem), (window_q, vmem), (window_k, vmem), (v, hbm)],
        3500,
    )
    intra, phi = call(
        functools.partial(intra_kernel, rows, chunks),
        [((rows, width), F32, vmem), ((rows, 3 * width), BF16, vmem)],
        [(whole, vmem), (feature_q.T, hbm), (feature_k.T, hbm), (v, hbm)],
        2200,
    )
    totals, window, head, halo, intra, phi = lax.optimization_barrier(
        (totals, window, head, halo, intra, phi)
    )
    (before,) = call(
        prefix_kernel,
        [(slices.shape, BF16, hbm)],
        [(plane, smem), (slices, vmem), (totals, vmem)],
        1000,
        scratch=[pltpu.VMEM(slices.shape, BF16), pltpu.SemaphoreType.DMA((4,))],
    )
    prefix = exchange(before, PLANE).reshape(held, 128)
    devices = lax.axis_size(SEQ)
    halo = lax.ppermute(halo, SEQ, [(i, i + 1) for i in range(devices - 1)])
    (early,) = call(
        first_window_kernel,
        [((WIN, width), F32, vmem)],
        [(first, smem), (head, vmem), (halo, vmem)],
        1000,
    )
    (mixed,) = call(
        functools.partial(final_kernel, rows),
        [((rows, width), BF16, hbm)],
        [(a, vmem) for a in (prefix, phi, intra, early, window, norm_gain, mean)],
        1400,
        scratch=[pltpu.VMEM((width // 128, rows, 128), BF16), pltpu.SemaphoreType.DMA((width // 128,))],
    )
    return mixed


def solution(mesh):
    split = Mesh(
        mesh.devices.reshape(8, 8, 2, mesh.shape["head"]), ("seq_0", "seq_1", "seq_2", "head")
    )
    placed = (
        P(SEQ, "head"),
        P(None, "head"),
        P(None, "head"),
        P(None, "head"),
        P(None, "head"),
        P(None, "head"),
        P("head"),
    )
    return jax.shard_map(
        body, mesh=split, in_specs=placed, out_specs=P(SEQ, "head"), check_vma=False
    )
```

```python
import functools

import jax
import jax.numpy as jnp
from jax import lax
from jax.experimental import pallas as pl
from jax.experimental.pallas import tpu as pltpu
from jax.sharding import Mesh
from jax.sharding import PartitionSpec as P

FK = 16
HV = 64
WIN = 64
ROLLS = 8
BLOCKS = ROLLS + 2
PAIR_ROWS = BLOCKS * FK
SEQ = ("seq_0", "seq_1", "seq_2")
PLANE = ("seq_1", "seq_2")
F32 = jnp.float32
BF16 = jnp.bfloat16
SHRINK = 2.0**-30
FLOPS_PER_NS = 1_000_000
NT = (((1,), (1,)), ((), ()))


def dot(a, b):
    return jnp.dot(a, b, preferred_element_type=F32)


def project_transposed(w_ref, x_ref, rows, chunks):
    depth = x_ref.shape[1]
    total = None
    for c in range(chunks):
        part = lax.dot_general(
            w_ref[:, c * depth : (c + 1) * depth],
            x_ref[c * rows : (c + 1) * rows, :],
            NT,
            preferred_element_type=F32,
        )
        total = part if total is None else total + part
    return total * FK ** (-0.25)


def project(x_ref, w_ref, rows, chunks):
    depth = x_ref.shape[1]
    total = None
    for c in range(chunks):
        part = dot(x_ref[c * rows : (c + 1) * rows, :], w_ref[c * depth : (c + 1) * depth, :])
        total = part if total is None else total + part
    return total


def features(xt, weight, one):
    total, tokens = xt.shape
    x3 = xt.reshape(total // FK, FK, tokens)
    blocks = [(xt * xt * weight).astype(BF16)]
    for d in range(1, ROLLS):
        rolled = jnp.concatenate([x3[:, d:], x3[:, :d]], axis=1)
        blocks.append((x3 * rolled).reshape(total, tokens).astype(BF16))
    blocks.append(xt.astype(BF16))
    half = x3[:, : FK // 2] * x3[:, FK // 2 :]
    mixed = jnp.concatenate([half, jnp.full_like(half, one)], axis=1)
    blocks.append(mixed.reshape(total, tokens).astype(BF16))
    return blocks


def low_half(shape):
    return lax.broadcasted_iota(jnp.int32, shape, len(shape) - 1) < HV


def mean_kernel(out_ref):
    i = lax.broadcasted_iota(jnp.int32, out_ref.shape, 0) % 128
    j = lax.broadcasted_iota(jnp.int32, out_ref.shape, 1)
    out_ref[...] = jnp.where((i < HV) == (j < HV), 1.0 / HV, 0.0).astype(BF16)


def state_kernel(rows, chunks, x_ref, wk_ref, wv_ref, state_ref, v_hbm, v_ref, v_sem):
    kt = project_transposed(wk_ref, x_ref, rows, chunks)
    v = project(x_ref, wv_ref, rows, chunks).astype(BF16)
    blocks = features(kt, 1.0, 1.0)
    pairs = v.shape[1] // 128
    lefts = [jnp.concatenate([b[32 * p : 32 * p + 32] for b in blocks], axis=0) for p in range(pairs)]
    v_ref[...] = v
    store = pltpu.make_async_copy(v_ref, v_hbm, v_sem)
    store.start()
    for p in range(pairs):
        both = dot(lefts[p], v[:, 128 * p : 128 * p + 128]).reshape(BLOCKS, 2, FK, 128)
        one = jnp.where(low_half((BLOCKS, FK, 128)), both[:, 0], both[:, 1])
        state_ref[PAIR_ROWS * p : PAIR_ROWS * (p + 1), :] = one.reshape(PAIR_ROWS, 128).astype(BF16)
    used = PAIR_ROWS * pairs
    state_ref[used:, :] = jnp.zeros((state_ref.shape[0] - used, 128), BF16)
    store.wait()


def window_tiles(tiles, valid):
    low = low_half((WIN, 128))
    logits = []
    for q, keys, _ in tiles:
        none = jnp.zeros_like(q)
        both = jnp.concatenate([jnp.where(low, q, none), jnp.where(low, none, q)], axis=0)
        score = lax.dot_general(both, keys, NT, preferred_element_type=F32)
        logits.append(jnp.where(valid, score * HV ** (-0.5), -1e30))
    logits = jnp.concatenate(logits, axis=0)
    expw = jnp.exp(logits - jnp.max(logits, axis=-1, keepdims=True))
    weights = (expw / jnp.sum(expw, axis=-1, keepdims=True)).astype(BF16)
    outs = []
    for n, (_, _, vals) in enumerate(tiles):
        mixed = dot(weights[2 * WIN * n : 2 * WIN * (n + 1)], vals)
        outs.append(jnp.where(low, mixed[:WIN], mixed[WIN:]))
    return outs


def window_band():
    row = lax.broadcasted_iota(jnp.int32, (2 * WIN, 2 * WIN), 0) % WIN
    col = lax.broadcasted_iota(jnp.int32, (2 * WIN, 2 * WIN), 1)
    return (col <= row + WIN) & (col > row), col


def window_kernel(rows, chunks, x_ref, wq_ref, wk_ref, v_ref, out_ref, head_ref, halo_ref):
    keys = project(x_ref, wk_ref, rows, chunks).astype(BF16)
    queries = project(x_ref, wq_ref, rows, chunks).astype(BF16)
    width = keys.shape[1]
    halo_ref[:, :width] = keys[rows - WIN :]
    halo_ref[:, width:] = v_ref[rows - WIN :, :]
    head_ref[:, :width] = queries[:WIN]
    head_ref[:, width : 2 * width] = keys[:WIN]
    head_ref[:, 2 * width :] = v_ref[:WIN, :]
    band, _ = window_band()
    places = [(t, p) for t in range(1, rows // WIN) for p in range(width // 128)]
    tiles = []
    for t, p in places:
        at, seen = slice(128 * p, 128 * p + 128), slice(WIN * (t - 1), WIN * (t + 1))
        tiles.append((queries[WIN * t : WIN * (t + 1), at], keys[seen, at], v_ref[seen, at]))
    for (t, p), out in zip(places, window_tiles(tiles, band)):
        out_ref[WIN * (t - 1) : WIN * t, 128 * p : 128 * p + 128] = out


def first_window_kernel(first_ref, head_ref, halo_ref, out_ref):
    width = out_ref.shape[1]
    band, col = window_band()
    valid = band & ((col >= WIN) | (first_ref[0] == 0))
    tiles = []
    for p in range(width // 128):
        at, at2, at3 = (slice(n * width + 128 * p, n * width + 128 * p + 128) for n in range(3))
        keys = jnp.concatenate([halo_ref[:, at], head_ref[:, at2]], axis=0)
        vals = jnp.concatenate([halo_ref[:, at2], head_ref[:, at3]], axis=0)
        tiles.append((head_ref[:, at], keys, vals))
    for p, out in enumerate(window_tiles(tiles, valid)):
        out_ref[:, 128 * p : 128 * p + 128] = out


def intra_kernel(rows, chunks, x_ref, wq_ref, wk_ref, v_ref, intra_ref, phi_ref):
    qt = project_transposed(wq_ref, x_ref, rows, chunks)
    kt = project_transposed(wk_ref, x_ref, rows, chunks)
    blocks = features(qt, 0.5, 1.0 / (FK // 2))
    heads = qt.shape[0] // FK
    pad = jnp.zeros((384 - 2 * PAIR_ROWS, rows), F32)
    q_hi = qt.astype(BF16).astype(F32)
    q_lo = qt - q_hi
    k_hi = kt.astype(BF16).astype(F32)
    k_lo = kt - k_hi
    zero = jnp.zeros((128 - 3 * FK, rows), F32)
    t = lax.broadcasted_iota(jnp.int32, (rows, rows), 0)
    s = lax.broadcasted_iota(jnp.int32, (rows, rows), 1)
    causal = t >= s
    for p in range(heads // 2):
        phi = jnp.concatenate([b[32 * p : 32 * p + 32].astype(F32) for b in blocks] + [pad], axis=0)
        phi_ref[:, 384 * p : 384 * (p + 1)] = phi.T.astype(BF16)
        vp = v_ref[:, 128 * p : 128 * p + 128]
        outs = []
        for h in (2 * p, 2 * p + 1):
            at = slice(FK * h, FK * (h + 1))
            left = jnp.concatenate([q_hi[at], q_hi[at], q_lo[at], zero], axis=0).T.astype(BF16)
            right = jnp.concatenate([k_hi[at], k_lo[at], k_hi[at], zero], axis=0).astype(BF16)
            a = dot(left, right)
            kern = jnp.where(causal, 1.0 + a + 0.5 * a * a, 0.0).astype(BF16)
            outs.append(dot(kern, vp))
        intra_ref[:, 128 * p : 128 * p + 128] = jnp.where(low_half((rows, 128)), outs[0], outs[1])


def total_kernel(slices_ref, out_hbm, total_ref, sem):
    total = slices_ref[0].astype(F32)
    for i in range(1, slices_ref.shape[0]):
        total = total + slices_ref[i].astype(F32)
    total_ref[...] = total.astype(BF16)
    stores = [pltpu.make_async_copy(total_ref, out_hbm.at[z], sem.at[z]) for z in range(out_hbm.shape[0])]
    for store in stores:
        store.start()
    for store in stores:
        store.wait()


def prefix_kernel(plane_ref, slices_ref, totals_ref, out_hbm, out_ref, sem):
    plane = plane_ref[0]
    run = jnp.zeros(totals_ref.shape[1:], F32)
    for z in range(totals_ref.shape[0]):
        run = run + jnp.where(z < plane, totals_ref[z].astype(F32), 0.0)
    stores = []
    each = slices_ref.shape[0] // sem.shape[0]
    for n in range(sem.shape[0]):
        for i in range(each * n, each * (n + 1)):
            out_ref[i] = run.astype(BF16)
            run = run + slices_ref[i].astype(F32)
        at = pl.ds(each * n, each)
        stores.append(pltpu.make_async_copy(out_ref.at[at], out_hbm.at[at], sem.at[n]))
        stores[n].start()
    for store in stores:
        store.wait()


def final_kernel(
    rows, state_ref, phi_ref, intra_ref, early_ref, window_ref, gain_ref, mean_ref, out_hbm, out_ref, sem
):
    low_state = low_half((BLOCKS, FK, 128))
    pairs = [slice(128 * p, 128 * p + 128) for p in range(intra_ref.shape[1] // 128)]
    linears, squares = [], []
    for p, at in enumerate(pairs):
        state = state_ref[PAIR_ROWS * p : PAIR_ROWS * (p + 1), :].reshape(BLOCKS, FK, 128)
        none = jnp.zeros_like(state)
        even = jnp.where(low_state, state, none)[:, None]
        odd = jnp.where(low_state, none, state)[:, None]
        right = jnp.concatenate([even, odd], axis=1).reshape(2 * PAIR_ROWS, 128)
        right = jnp.concatenate([right, jnp.zeros((384 - 2 * PAIR_ROWS, 128), BF16)], axis=0)
        linears.append(intra_ref[:, at] + dot(phi_ref[:, 384 * p : 384 * (p + 1)], right))
    for linear in linears:
        square = (linear * SHRINK) * (linear * SHRINK)
        hi = square.astype(BF16)
        lo = (square - hi.astype(F32)).astype(BF16)
        squares.append(dot(jnp.concatenate([hi, lo], axis=1), mean_ref[...]))
    stores = []
    for p, at in enumerate(pairs):
        scale = lax.rsqrt(squares[p] + 1e-5 * SHRINK * SHRINK) * SHRINK
        normed = linears[p] * scale * gain_ref[at].reshape(1, 128)
        out_ref[p, :WIN, :] = (normed[:WIN] + early_ref[:, at]).astype(BF16)
        out_ref[p, WIN:, :] = (normed[WIN:] + window_ref[:, at]).astype(BF16)
        stores.append(pltpu.make_async_copy(out_ref.at[p], out_hbm.at[:, at], sem.at[p]))
        stores[p].start()
    for store in stores:
        store.wait()


def call(kernel, outs, args, nanoseconds, scratch=(), vmem=12):
    arrays = [a if space is pltpu.SMEM else pltpu.with_memory_space_constraint(a, space) for a, space in args]
    spaces = [space for _, space in args]
    size = sum(a.size * a.dtype.itemsize for a in arrays)

    def spec(space):
        return pl.BlockSpec(memory_space=pltpu.VMEM if space is pltpu.HBM and not scratch else space)

    return pl.pallas_call(
        kernel,
        out_shape=[space(shape, dtype) for shape, dtype, space in outs],
        in_specs=[spec(space) for space in spaces],
        out_specs=[spec(space) for _, _, space in outs],
        scratch_shapes=list(scratch),
        compiler_params=pltpu.CompilerParams(vmem_limit_bytes=vmem << 20),
        cost_estimate=pl.CostEstimate(
            flops=nanoseconds * FLOPS_PER_NS, bytes_accessed=size, transcendentals=0
        ),
    )(*arrays)


def exchange(x, axis):
    return lax.all_to_all(x, axis, split_axis=0, concat_axis=0, tiled=True)


def body(hidden_states, feature_q, feature_k, value_w, window_q, window_k, norm_gain):
    rows = hidden_states.shape[0]
    chunks = lax.axis_size("head")
    width = value_w.shape[1]
    model = value_w.shape[0]
    few = feature_k.shape[1]
    planes, members = lax.axis_size("seq_0"), lax.axis_size("seq_1") * lax.axis_size("seq_2")
    plane = lax.axis_index("seq_0").astype(jnp.int32).reshape(1)
    first = (lax.axis_index(SEQ) == 0).astype(jnp.int32).reshape(1)
    piece = FK * members
    held = -(-PAIR_ROWS * width // (128 * piece)) * piece

    vmem, hbm, smem = pltpu.VMEM, pltpu.HBM, pltpu.SMEM

    (mean,) = call(mean_kernel, [((256, 128), BF16, vmem)], [], 200)
    hidden_states, mean, plane, first = lax.optimization_barrier((hidden_states, mean, plane, first))
    whole = lax.all_gather(hidden_states, "head", tiled=True)
    state, v = call(
        functools.partial(state_kernel, rows, chunks),
        [((held, 128), BF16, vmem), ((rows, width), BF16, hbm)],
        [(whole, vmem), (feature_k.T, vmem), (value_w, vmem)],
        1500,
        scratch=[pltpu.VMEM((rows, width), BF16), pltpu.SemaphoreType.DMA(())],
    )
    slices = exchange(state.reshape(members, held // members, 128), PLANE)
    slices, v = lax.optimization_barrier((slices, v))
    piece_shape = slices.shape[1:]
    (totals,) = call(
        total_kernel,
        [((planes, *piece_shape), BF16, hbm)],
        [(slices, vmem)],
        600,
        scratch=[pltpu.VMEM(piece_shape, BF16), pltpu.SemaphoreType.DMA((planes,))],
    )
    totals = exchange(totals, "seq_0")
    window, head, halo = call(
        functools.partial(window_kernel, rows, chunks),
        [((rows - WIN, width), F32, hbm), ((WIN, 3 * width), BF16, hbm), ((WIN, 2 * width), BF16, hbm)],
        [(whole, vmem), (window_q, vmem), (window_k, vmem), (v, hbm)],
        3500,
    )
    intra, phi = call(
        functools.partial(intra_kernel, rows, chunks),
        [((rows, width), F32, vmem), ((rows, 3 * width), BF16, vmem)],
        [(whole, vmem), (feature_q.T, hbm), (feature_k.T, hbm), (v, hbm)],
        2200,
    )
    totals, window, head, halo, intra, phi = lax.optimization_barrier(
        (totals, window, head, halo, intra, phi)
    )
    (before,) = call(
        prefix_kernel,
        [(slices.shape, BF16, hbm)],
        [(plane, smem), (slices, vmem), (totals, vmem)],
        1000,
        scratch=[pltpu.VMEM(slices.shape, BF16), pltpu.SemaphoreType.DMA((4,))],
    )
    prefix = exchange(before, PLANE).reshape(held, 128)
    devices = lax.axis_size(SEQ)
    halo = lax.ppermute(halo, SEQ, [(i, i + 1) for i in range(devices - 1)])
    (early,) = call(
        first_window_kernel,
        [((WIN, width), F32, vmem)],
        [(first, smem), (head, vmem), (halo, vmem)],
        1000,
    )
    (mixed,) = call(
        functools.partial(final_kernel, rows),
        [((rows, width), BF16, hbm)],
        [(a, vmem) for a in (prefix, phi, intra, early, window, norm_gain, mean)],
        1400,
        scratch=[pltpu.VMEM((width // 128, rows, 128), BF16), pltpu.SemaphoreType.DMA((width // 128,))],
    )
    return mixed


def solution(mesh):
    split = Mesh(
        mesh.devices.reshape(8, 8, 2, mesh.shape["head"]), ("seq_0", "seq_1", "seq_2", "head")
    )
    placed = (
        P(SEQ, "head"),
        P(None, "head"),
        P(None, "head"),
        P(None, "head"),
        P(None, "head"),
        P(None, "head"),
        P("head"),
    )
    return jax.shard_map(
        body, mesh=split, in_specs=placed, out_specs=P(SEQ, "head"), check_vma=False
    )
```

```python
import functools

import jax
import jax.numpy as jnp
from jax import lax
from jax.experimental import pallas as pl
from jax.experimental.pallas import tpu as pltpu
from jax.sharding import Mesh
from jax.sharding import PartitionSpec as P

FK = 16
HV = 64
WIN = 64
ROLLS = 8
BLOCKS = ROLLS + 2
PAIR_ROWS = BLOCKS * FK
SEQ = ("seq_0", "seq_1", "seq_2")
PLANE = ("seq_1", "seq_2")
F32 = jnp.float32
BF16 = jnp.bfloat16
SHRINK = 2.0**-30
FLOPS_PER_NS = 1_000_000
NT = (((1,), (1,)), ((), ()))


def dot(a, b):
    return jnp.dot(a, b, preferred_element_type=F32)


def project_transposed(w_ref, x_ref, rows, chunks):
    depth = x_ref.shape[1]
    total = None
    for c in range(chunks):
        part = lax.dot_general(
            w_ref[:, c * depth : (c + 1) * depth],
            x_ref[c * rows : (c + 1) * rows, :],
            NT,
            preferred_element_type=F32,
        )
        total = part if total is None else total + part
    return total * FK ** (-0.25)


def project(x_ref, w_ref, rows, chunks):
    depth = x_ref.shape[1]
    total = None
    for c in range(chunks):
        part = dot(x_ref[c * rows : (c + 1) * rows, :], w_ref[c * depth : (c + 1) * depth, :])
        total = part if total is None else total + part
    return total


def features(xt, weight, one):
    total, tokens = xt.shape
    x3 = xt.reshape(total // FK, FK, tokens)
    blocks = [(xt * xt * weight).astype(BF16)]
    for d in range(1, ROLLS):
        rolled = jnp.concatenate([x3[:, d:], x3[:, :d]], axis=1)
        blocks.append((x3 * rolled).reshape(total, tokens).astype(BF16))
    blocks.append(xt.astype(BF16))
    half = x3[:, : FK // 2] * x3[:, FK // 2 :]
    mixed = jnp.concatenate([half, jnp.full_like(half, one)], axis=1)
    blocks.append(mixed.reshape(total, tokens).astype(BF16))
    return blocks


def low_half(shape):
    return lax.broadcasted_iota(jnp.int32, shape, len(shape) - 1) < HV


def mean_kernel(out_ref):
    i = lax.broadcasted_iota(jnp.int32, out_ref.shape, 0) % 128
    j = lax.broadcasted_iota(jnp.int32, out_ref.shape, 1)
    out_ref[...] = jnp.where((i < HV) == (j < HV), 1.0 / HV, 0.0).astype(BF16)


def whole_rows(x_ref, rows, chunks):
    return jnp.concatenate([x_ref[c * rows : (c + 1) * rows, :] for c in range(chunks)], axis=1)


def state_kernel(rows, chunks, x_ref, wk_ref, wv_ref, state_ref, v_hbm, v_ref, left_ref, v_sem):
    x = whole_rows(x_ref, rows, chunks)
    kt = lax.dot_general(wk_ref[...], x, NT, preferred_element_type=F32) * FK ** (-0.25)
    v_ref[...] = dot(x, wv_ref[...]).astype(BF16)
    store = pltpu.make_async_copy(v_ref, v_hbm, v_sem)
    store.start()
    blocks = features(kt, 1.0, 1.0)
    pairs = left_ref.shape[0]
    for p in range(pairs):
        for n, block in enumerate(blocks):
            left_ref[p, 32 * n : 32 * (n + 1), :] = block[32 * p : 32 * p + 32]
    for p in range(pairs):
        both = dot(left_ref[p], v_ref[:, 128 * p : 128 * p + 128]).reshape(BLOCKS, 2, FK, 128)
        one = jnp.where(low_half((BLOCKS, FK, 128)), both[:, 0], both[:, 1])
        state_ref[PAIR_ROWS * p : PAIR_ROWS * (p + 1), :] = one.reshape(PAIR_ROWS, 128).astype(BF16)
    used = PAIR_ROWS * pairs
    state_ref[used:, :] = jnp.zeros((state_ref.shape[0] - used, 128), BF16)
    store.wait()


def window_tiles(tiles, valid):
    low = low_half((WIN, 128))
    logits = []
    for q, keys, _ in tiles:
        none = jnp.zeros_like(q)
        both = jnp.concatenate([jnp.where(low, q, none), jnp.where(low, none, q)], axis=0)
        score = lax.dot_general(both, keys, NT, preferred_element_type=F32)
        logits.append(jnp.where(valid, score * HV ** (-0.5), -1e30))
    logits = jnp.concatenate(logits, axis=0)
    expw = jnp.exp(logits - jnp.max(logits, axis=-1, keepdims=True))
    weights = (expw / jnp.sum(expw, axis=-1, keepdims=True)).astype(BF16)
    outs = []
    for n, (_, _, vals) in enumerate(tiles):
        mixed = dot(weights[2 * WIN * n : 2 * WIN * (n + 1)], vals)
        outs.append(jnp.where(low, mixed[:WIN], mixed[WIN:]))
    return outs


def window_band():
    row = lax.broadcasted_iota(jnp.int32, (2 * WIN, 2 * WIN), 0) % WIN
    col = lax.broadcasted_iota(jnp.int32, (2 * WIN, 2 * WIN), 1)
    return (col <= row + WIN) & (col > row), col


def window_kernel(rows, chunks, x_ref, wq_ref, wk_ref, v_ref, out_ref, head_ref, halo_ref):
    keys = project(x_ref, wk_ref, rows, chunks).astype(BF16)
    queries = project(x_ref, wq_ref, rows, chunks).astype(BF16)
    width = keys.shape[1]
    halo_ref[:, :width] = keys[rows - WIN :]
    halo_ref[:, width:] = v_ref[rows - WIN :, :]
    head_ref[:, :width] = queries[:WIN]
    head_ref[:, width : 2 * width] = keys[:WIN]
    head_ref[:, 2 * width :] = v_ref[:WIN, :]
    band, _ = window_band()
    places = [(t, p) for t in range(1, rows // WIN) for p in range(width // 128)]
    tiles = []
    for t, p in places:
        at, seen = slice(128 * p, 128 * p + 128), slice(WIN * (t - 1), WIN * (t + 1))
        tiles.append((queries[WIN * t : WIN * (t + 1), at], keys[seen, at], v_ref[seen, at]))
    for (t, p), out in zip(places, window_tiles(tiles, band)):
        out_ref[WIN * (t - 1) : WIN * t, 128 * p : 128 * p + 128] = out


def first_window_kernel(first_ref, head_ref, halo_ref, out_ref):
    width = out_ref.shape[1]
    band, col = window_band()
    valid = band & ((col >= WIN) | (first_ref[0] == 0))
    tiles = []
    for p in range(width // 128):
        at, at2, at3 = (slice(n * width + 128 * p, n * width + 128 * p + 128) for n in range(3))
        keys = jnp.concatenate([halo_ref[:, at], head_ref[:, at2]], axis=0)
        vals = jnp.concatenate([halo_ref[:, at2], head_ref[:, at3]], axis=0)
        tiles.append((head_ref[:, at], keys, vals))
    for p, out in enumerate(window_tiles(tiles, valid)):
        out_ref[:, 128 * p : 128 * p + 128] = out


def intra_kernel(rows, chunks, x_ref, wq_ref, wk_ref, v_ref, intra_ref, phi_ref):
    qt = project_transposed(wq_ref, x_ref, rows, chunks)
    kt = project_transposed(wk_ref, x_ref, rows, chunks)
    blocks = features(qt, 0.5, 1.0 / (FK // 2))
    heads = qt.shape[0] // FK
    pad = jnp.zeros((384 - 2 * PAIR_ROWS, rows), F32)
    q_hi = qt.astype(BF16).astype(F32)
    q_lo = qt - q_hi
    k_hi = kt.astype(BF16).astype(F32)
    k_lo = kt - k_hi
    zero = jnp.zeros((128 - 3 * FK, rows), F32)
    t = lax.broadcasted_iota(jnp.int32, (rows, rows), 0)
    s = lax.broadcasted_iota(jnp.int32, (rows, rows), 1)
    causal = t >= s
    for p in range(heads // 2):
        phi = jnp.concatenate([b[32 * p : 32 * p + 32].astype(F32) for b in blocks] + [pad], axis=0)
        phi_ref[:, 384 * p : 384 * (p + 1)] = phi.T.astype(BF16)
        vp = v_ref[:, 128 * p : 128 * p + 128]
        outs = []
        for h in (2 * p, 2 * p + 1):
            at = slice(FK * h, FK * (h + 1))
            left = jnp.concatenate([q_hi[at], q_hi[at], q_lo[at], zero], axis=0).T.astype(BF16)
            right = jnp.concatenate([k_hi[at], k_lo[at], k_hi[at], zero], axis=0).astype(BF16)
            a = dot(left, right)
            kern = jnp.where(causal, 1.0 + a + 0.5 * a * a, 0.0).astype(BF16)
            outs.append(dot(kern, vp))
        intra_ref[:, 128 * p : 128 * p + 128] = jnp.where(low_half((rows, 128)), outs[0], outs[1])


def total_kernel(slices_ref, out_ref):
    total = slices_ref[0].astype(F32)
    for i in range(1, slices_ref.shape[0]):
        total = total + slices_ref[i].astype(F32)
    total = total.astype(BF16)
    for z in range(out_ref.shape[0]):
        out_ref[z] = total


def prefix_kernel(plane_ref, slices_ref, totals_ref, out_hbm, out_ref, sem):
    plane = plane_ref[0]
    run = jnp.zeros(totals_ref.shape[1:], F32)
    for z in range(totals_ref.shape[0]):
        run = run + jnp.where(z < plane, totals_ref[z].astype(F32), 0.0)
    stores = []
    each = slices_ref.shape[0] // sem.shape[0]
    for n in range(sem.shape[0]):
        for i in range(each * n, each * (n + 1)):
            out_ref[i] = run.astype(BF16)
            run = run + slices_ref[i].astype(F32)
        at = pl.ds(each * n, each)
        stores.append(pltpu.make_async_copy(out_ref.at[at], out_hbm.at[at], sem.at[n]))
        stores[n].start()
    for store in stores:
        store.wait()


def final_kernel(
    rows, state_ref, phi_ref, intra_ref, early_ref, window_ref, gain_ref, mean_ref, out_hbm, out_ref, sem
):
    low_state = low_half((BLOCKS, FK, 128))
    pairs = [slice(128 * p, 128 * p + 128) for p in range(intra_ref.shape[1] // 128)]
    linears, squares = [], []
    for p, at in enumerate(pairs):
        state = state_ref[PAIR_ROWS * p : PAIR_ROWS * (p + 1), :].reshape(BLOCKS, FK, 128)
        none = jnp.zeros_like(state)
        even = jnp.where(low_state, state, none)[:, None]
        odd = jnp.where(low_state, none, state)[:, None]
        right = jnp.concatenate([even, odd], axis=1).reshape(2 * PAIR_ROWS, 128)
        right = jnp.concatenate([right, jnp.zeros((384 - 2 * PAIR_ROWS, 128), BF16)], axis=0)
        linears.append(intra_ref[:, at] + dot(phi_ref[:, 384 * p : 384 * (p + 1)], right))
    for linear in linears:
        square = (linear * SHRINK) * (linear * SHRINK)
        hi = square.astype(BF16)
        lo = (square - hi.astype(F32)).astype(BF16)
        squares.append(dot(jnp.concatenate([hi, lo], axis=1), mean_ref[...]))
    stores = []
    for p, at in enumerate(pairs):
        scale = lax.rsqrt(squares[p] + 1e-5 * SHRINK * SHRINK) * SHRINK
        normed = linears[p] * scale * gain_ref[at].reshape(1, 128)
        out_ref[p, :WIN, :] = (normed[:WIN] + early_ref[:, at]).astype(BF16)
        out_ref[p, WIN:, :] = (normed[WIN:] + window_ref[:, at]).astype(BF16)
        stores.append(pltpu.make_async_copy(out_ref.at[p], out_hbm.at[:, at], sem.at[p]))
        stores[p].start()
    for store in stores:
        store.wait()


def call(kernel, outs, args, nanoseconds, scratch=(), vmem=12):
    arrays = [a if space is pltpu.SMEM else pltpu.with_memory_space_constraint(a, space) for a, space in args]
    spaces = [space for _, space in args]
    size = sum(a.size * a.dtype.itemsize for a in arrays)

    def spec(space):
        return pl.BlockSpec(memory_space=pltpu.VMEM if space is pltpu.HBM and not scratch else space)

    return pl.pallas_call(
        kernel,
        out_shape=[space(shape, dtype) for shape, dtype, space in outs],
        in_specs=[spec(space) for space in spaces],
        out_specs=[spec(space) for _, _, space in outs],
        scratch_shapes=list(scratch),
        compiler_params=pltpu.CompilerParams(vmem_limit_bytes=vmem << 20),
        cost_estimate=pl.CostEstimate(
            flops=nanoseconds * FLOPS_PER_NS, bytes_accessed=size, transcendentals=0
        ),
    )(*arrays)


def exchange(x, axis):
    return lax.all_to_all(x, axis, split_axis=0, concat_axis=0, tiled=True)


def body(hidden_states, feature_q, feature_k, value_w, window_q, window_k, norm_gain):
    rows = hidden_states.shape[0]
    chunks = lax.axis_size("head")
    width = value_w.shape[1]
    model = value_w.shape[0]
    few = feature_k.shape[1]
    planes, members = lax.axis_size("seq_0"), lax.axis_size("seq_1") * lax.axis_size("seq_2")
    plane = lax.axis_index("seq_0").astype(jnp.int32).reshape(1)
    first = (lax.axis_index(SEQ) == 0).astype(jnp.int32).reshape(1)
    piece = FK * members
    held = -(-PAIR_ROWS * width // (128 * piece)) * piece

    vmem, hbm, smem = pltpu.VMEM, pltpu.HBM, pltpu.SMEM

    (mean,) = call(mean_kernel, [((256, 128), BF16, vmem)], [], 200)
    hidden_states, mean, plane, first = lax.optimization_barrier((hidden_states, mean, plane, first))
    whole = lax.all_gather(hidden_states, "head", tiled=True)
    state, v = call(
        functools.partial(state_kernel, rows, chunks),
        [((held, 128), BF16, vmem), ((rows, width), BF16, hbm)],
        [(whole, vmem), (feature_k.T, vmem), (value_w, vmem)],
        1500,
        scratch=[
            pltpu.VMEM((rows, width), BF16),
            pltpu.VMEM((width // 128, 2 * PAIR_ROWS, rows), BF16),
            pltpu.SemaphoreType.DMA(()),
        ],
    )
    slices = exchange(state.reshape(members, held // members, 128), PLANE)
    slices, v = lax.optimization_barrier((slices, v))
    (totals,) = call(
        total_kernel, [((planes, *slices.shape[1:]), BF16, vmem)], [(slices, vmem)], 300
    )
    totals = exchange(totals, "seq_0")
    (before,) = call(
        prefix_kernel,
        [(slices.shape, BF16, hbm)],
        [(plane, smem), (slices, vmem), (totals, vmem)],
        1000,
        scratch=[pltpu.VMEM(slices.shape, BF16), pltpu.SemaphoreType.DMA((4,))],
    )
    before, v = lax.optimization_barrier((before, v))
    prefix = exchange(before, PLANE).reshape(held, 128)
    window, head, halo = call(
        functools.partial(window_kernel, rows, chunks),
        [((rows - WIN, width), F32, hbm), ((WIN, 3 * width), BF16, hbm), ((WIN, 2 * width), BF16, hbm)],
        [(whole, vmem), (window_q, vmem), (window_k, vmem), (v, hbm)],
        1000,
    )
    devices = lax.axis_size(SEQ)
    halo = lax.ppermute(halo, SEQ, [(i, i + 1) for i in range(devices - 1)])
    intra, phi = call(
        functools.partial(intra_kernel, rows, chunks),
        [((rows, width), F32, vmem), ((rows, 3 * width), BF16, vmem)],
        [(whole, vmem), (feature_q.T, hbm), (feature_k.T, hbm), (v, hbm)],
        700,
    )
    (early,) = call(
        first_window_kernel,
        [((WIN, width), F32, vmem)],
        [(first, smem), (head, vmem), (halo, vmem)],
        1000,
    )
    (mixed,) = call(
        functools.partial(final_kernel, rows),
        [((rows, width), BF16, hbm)],
        [(a, vmem) for a in (prefix, phi, intra, early, window, norm_gain, mean)],
        1400,
        scratch=[pltpu.VMEM((width // 128, rows, 128), BF16), pltpu.SemaphoreType.DMA((width // 128,))],
    )
    return mixed


def solution(mesh):
    split = Mesh(
        mesh.devices.reshape(8, 8, 2, mesh.shape["head"]), ("seq_0", "seq_1", "seq_2", "head")
    )
    placed = (
        P(SEQ, "head"),
        P(None, "head"),
        P(None, "head"),
        P(None, "head"),
        P(None, "head"),
        P(None, "head"),
        P("head"),
    )
    return jax.shard_map(
        body, mesh=split, in_specs=placed, out_specs=P(SEQ, "head"), check_vma=False
    )
```

```python
import functools

import jax
import jax.numpy as jnp
from jax import lax
from jax.experimental import pallas as pl
from jax.experimental.pallas import tpu as pltpu
from jax.sharding import Mesh
from jax.sharding import PartitionSpec as P

FK = 16
HV = 64
WIN = 64
ROLLS = 8
BLOCKS = ROLLS + 2
PAIR_ROWS = BLOCKS * FK
SEQ = ("seq_0", "seq_1", "seq_2")
PLANE = ("seq_1", "seq_2")
F32 = jnp.float32
BF16 = jnp.bfloat16
SHRINK = 2.0**-30
FLOPS_PER_NS = 1_000_000
NT = (((1,), (1,)), ((), ()))


def dot(a, b):
    return jnp.dot(a, b, preferred_element_type=F32)


def project_transposed(w_ref, x_ref, rows, chunks):
    depth = x_ref.shape[1]
    total = None
    for c in range(chunks):
        part = lax.dot_general(
            w_ref[:, c * depth : (c + 1) * depth],
            x_ref[c * rows : (c + 1) * rows, :],
            NT,
            preferred_element_type=F32,
        )
        total = part if total is None else total + part
    return total * FK ** (-0.25)


def project(x_ref, w_ref, rows, chunks):
    depth = x_ref.shape[1]
    total = None
    for c in range(chunks):
        part = dot(x_ref[c * rows : (c + 1) * rows, :], w_ref[c * depth : (c + 1) * depth, :])
        total = part if total is None else total + part
    return total


def features(xt, weight, one):
    total, tokens = xt.shape
    x3 = xt.reshape(total // FK, FK, tokens)
    blocks = [(xt * xt * weight).astype(BF16)]
    for d in range(1, ROLLS):
        rolled = jnp.concatenate([x3[:, d:], x3[:, :d]], axis=1)
        blocks.append((x3 * rolled).reshape(total, tokens).astype(BF16))
    blocks.append(xt.astype(BF16))
    half = x3[:, : FK // 2] * x3[:, FK // 2 :]
    mixed = jnp.concatenate([half, jnp.full_like(half, one)], axis=1)
    blocks.append(mixed.reshape(total, tokens).astype(BF16))
    return blocks


def low_half(shape):
    return lax.broadcasted_iota(jnp.int32, shape, len(shape) - 1) < HV


def mean_kernel(out_ref):
    i = lax.broadcasted_iota(jnp.int32, out_ref.shape, 0) % 128
    j = lax.broadcasted_iota(jnp.int32, out_ref.shape, 1)
    out_ref[...] = jnp.where((i < HV) == (j < HV), 1.0 / HV, 0.0).astype(BF16)


def whole_rows(x_ref, rows, chunks):
    return jnp.concatenate([x_ref[c * rows : (c + 1) * rows, :] for c in range(chunks)], axis=1)


def state_kernel(rows, chunks, x_ref, wk_ref, wv_ref, state_ref, v_ref, left_ref):
    x = whole_rows(x_ref, rows, chunks)
    kt = lax.dot_general(wk_ref[...], x, NT, preferred_element_type=F32) * FK ** (-0.25)
    v_ref[...] = dot(x, wv_ref[...]).astype(BF16)
    blocks = features(kt, 1.0, 1.0)
    pairs = left_ref.shape[0]
    for p in range(pairs):
        for n, block in enumerate(blocks):
            left_ref[p, 32 * n : 32 * (n + 1), :] = block[32 * p : 32 * p + 32]
    for p in range(pairs):
        both = dot(left_ref[p], v_ref[:, 128 * p : 128 * p + 128]).reshape(BLOCKS, 2, FK, 128)
        one = jnp.where(low_half((BLOCKS, FK, 128)), both[:, 0], both[:, 1])
        state_ref[PAIR_ROWS * p : PAIR_ROWS * (p + 1), :] = one.reshape(PAIR_ROWS, 128).astype(BF16)
    used = PAIR_ROWS * pairs
    state_ref[used:, :] = jnp.zeros((state_ref.shape[0] - used, 128), BF16)


def window_tiles(tiles, valid):
    low = low_half((WIN, 128))
    logits = []
    for q, keys, _ in tiles:
        none = jnp.zeros_like(q)
        both = jnp.concatenate([jnp.where(low, q, none), jnp.where(low, none, q)], axis=0)
        score = lax.dot_general(both, keys, NT, preferred_element_type=F32)
        logits.append(jnp.where(valid, score * HV ** (-0.5), -1e30))
    logits = jnp.concatenate(logits, axis=0)
    expw = jnp.exp(logits - jnp.max(logits, axis=-1, keepdims=True))
    weights = (expw / jnp.sum(expw, axis=-1, keepdims=True)).astype(BF16)
    outs = []
    for n, (_, _, vals) in enumerate(tiles):
        mixed = dot(weights[2 * WIN * n : 2 * WIN * (n + 1)], vals)
        outs.append(jnp.where(low, mixed[:WIN], mixed[WIN:]))
    return outs


def window_band():
    row = lax.broadcasted_iota(jnp.int32, (2 * WIN, 2 * WIN), 0) % WIN
    col = lax.broadcasted_iota(jnp.int32, (2 * WIN, 2 * WIN), 1)
    return (col <= row + WIN) & (col > row), col


def window_kernel(rows, chunks, x_ref, wq_ref, wk_ref, wv_ref, out_ref, head_ref, halo_ref, v_ref):
    v_ref[...] = dot(whole_rows(x_ref, rows, chunks), wv_ref[...]).astype(BF16)
    keys = project(x_ref, wk_ref, rows, chunks).astype(BF16)
    queries = project(x_ref, wq_ref, rows, chunks).astype(BF16)
    width = keys.shape[1]
    halo_ref[:, :width] = keys[rows - WIN :]
    halo_ref[:, width:] = v_ref[rows - WIN :, :]
    head_ref[:, :width] = queries[:WIN]
    head_ref[:, width : 2 * width] = keys[:WIN]
    head_ref[:, 2 * width :] = v_ref[:WIN, :]
    band, _ = window_band()
    places = [(t, p) for t in range(1, rows // WIN) for p in range(width // 128)]
    tiles = []
    for t, p in places:
        at, seen = slice(128 * p, 128 * p + 128), slice(WIN * (t - 1), WIN * (t + 1))
        tiles.append((queries[WIN * t : WIN * (t + 1), at], keys[seen, at], v_ref[seen, at]))
    for (t, p), out in zip(places, window_tiles(tiles, band)):
        out_ref[WIN * (t - 1) : WIN * t, 128 * p : 128 * p + 128] = out


def first_window_kernel(first_ref, head_ref, halo_ref, out_ref):
    width = out_ref.shape[1]
    band, col = window_band()
    valid = band & ((col >= WIN) | (first_ref[0] == 0))
    tiles = []
    for p in range(width // 128):
        at, at2, at3 = (slice(n * width + 128 * p, n * width + 128 * p + 128) for n in range(3))
        keys = jnp.concatenate([halo_ref[:, at], head_ref[:, at2]], axis=0)
        vals = jnp.concatenate([halo_ref[:, at2], head_ref[:, at3]], axis=0)
        tiles.append((head_ref[:, at], keys, vals))
    for p, out in enumerate(window_tiles(tiles, valid)):
        out_ref[:, 128 * p : 128 * p + 128] = out


def intra_kernel(rows, chunks, x_ref, wq_ref, wk_ref, v_ref, intra_ref, phi_ref):
    qt = project_transposed(wq_ref, x_ref, rows, chunks)
    kt = project_transposed(wk_ref, x_ref, rows, chunks)
    blocks = features(qt, 0.5, 1.0 / (FK // 2))
    heads = qt.shape[0] // FK
    pad = jnp.zeros((384 - 2 * PAIR_ROWS, rows), F32)
    q_hi = qt.astype(BF16).astype(F32)
    q_lo = qt - q_hi
    k_hi = kt.astype(BF16).astype(F32)
    k_lo = kt - k_hi
    zero = jnp.zeros((128 - 3 * FK, rows), F32)
    t = lax.broadcasted_iota(jnp.int32, (rows, rows), 0)
    s = lax.broadcasted_iota(jnp.int32, (rows, rows), 1)
    causal = t >= s
    for p in range(heads // 2):
        phi = jnp.concatenate([b[32 * p : 32 * p + 32].astype(F32) for b in blocks] + [pad], axis=0)
        phi_ref[:, 384 * p : 384 * (p + 1)] = phi.T.astype(BF16)
        vp = v_ref[:, 128 * p : 128 * p + 128]
        outs = []
        for h in (2 * p, 2 * p + 1):
            at = slice(FK * h, FK * (h + 1))
            left = jnp.concatenate([q_hi[at], q_hi[at], q_lo[at], zero], axis=0).T.astype(BF16)
            right = jnp.concatenate([k_hi[at], k_lo[at], k_hi[at], zero], axis=0).astype(BF16)
            a = dot(left, right)
            kern = jnp.where(causal, 1.0 + a + 0.5 * a * a, 0.0).astype(BF16)
            outs.append(dot(kern, vp))
        intra_ref[:, 128 * p : 128 * p + 128] = jnp.where(low_half((rows, 128)), outs[0], outs[1])


def total_kernel(slices_ref, out_hbm, total_ref, sem):
    total = slices_ref[0].astype(F32)
    for i in range(1, slices_ref.shape[0]):
        total = total + slices_ref[i].astype(F32)
    total_ref[...] = total.astype(BF16)
    stores = [pltpu.make_async_copy(total_ref, out_hbm.at[z], sem.at[z]) for z in range(out_hbm.shape[0])]
    for store in stores:
        store.start()
    for store in stores:
        store.wait()


def prefix_kernel(plane_ref, slices_ref, totals_ref, out_hbm, out_ref, sem):
    plane = plane_ref[0]
    run = jnp.zeros(totals_ref.shape[1:], F32)
    for z in range(totals_ref.shape[0]):
        run = run + jnp.where(z < plane, totals_ref[z].astype(F32), 0.0)
    stores = []
    each = slices_ref.shape[0] // sem.shape[0]
    for n in range(sem.shape[0]):
        for i in range(each * n, each * (n + 1)):
            out_ref[i] = run.astype(BF16)
            run = run + slices_ref[i].astype(F32)
        at = pl.ds(each * n, each)
        stores.append(pltpu.make_async_copy(out_ref.at[at], out_hbm.at[at], sem.at[n]))
        stores[n].start()
    for store in stores:
        store.wait()


def final_kernel(
    rows, state_ref, phi_ref, intra_ref, early_ref, window_ref, gain_ref, mean_ref, out_hbm, out_ref, sem
):
    low_state = low_half((BLOCKS, FK, 128))
    pairs = [slice(128 * p, 128 * p + 128) for p in range(intra_ref.shape[1] // 128)]
    linears, squares = [], []
    for p, at in enumerate(pairs):
        state = state_ref[PAIR_ROWS * p : PAIR_ROWS * (p + 1), :].reshape(BLOCKS, FK, 128)
        none = jnp.zeros_like(state)
        even = jnp.where(low_state, state, none)[:, None]
        odd = jnp.where(low_state, none, state)[:, None]
        right = jnp.concatenate([even, odd], axis=1).reshape(2 * PAIR_ROWS, 128)
        right = jnp.concatenate([right, jnp.zeros((384 - 2 * PAIR_ROWS, 128), BF16)], axis=0)
        linears.append(intra_ref[:, at] + dot(phi_ref[:, 384 * p : 384 * (p + 1)], right))
    for linear in linears:
        square = (linear * SHRINK) * (linear * SHRINK)
        hi = square.astype(BF16)
        lo = (square - hi.astype(F32)).astype(BF16)
        squares.append(dot(jnp.concatenate([hi, lo], axis=1), mean_ref[...]))
    stores = []
    for p, at in enumerate(pairs):
        scale = lax.rsqrt(squares[p] + 1e-5 * SHRINK * SHRINK) * SHRINK
        normed = linears[p] * scale * gain_ref[at].reshape(1, 128)
        out_ref[p, :WIN, :] = (normed[:WIN] + early_ref[:, at]).astype(BF16)
        out_ref[p, WIN:, :] = (normed[WIN:] + window_ref[:, at]).astype(BF16)
        stores.append(pltpu.make_async_copy(out_ref.at[p], out_hbm.at[:, at], sem.at[p]))
        stores[p].start()
    for store in stores:
        store.wait()


def call(kernel, outs, args, nanoseconds, scratch=(), vmem=12):
    arrays = [a if space is pltpu.SMEM else pltpu.with_memory_space_constraint(a, space) for a, space in args]
    spaces = [space for _, space in args]
    size = sum(a.size * a.dtype.itemsize for a in arrays)

    def spec(space):
        return pl.BlockSpec(memory_space=pltpu.VMEM if space is pltpu.HBM and not scratch else space)

    return pl.pallas_call(
        kernel,
        out_shape=[space(shape, dtype) for shape, dtype, space in outs],
        in_specs=[spec(space) for space in spaces],
        out_specs=[spec(space) for _, _, space in outs],
        scratch_shapes=list(scratch),
        compiler_params=pltpu.CompilerParams(vmem_limit_bytes=vmem << 20),
        cost_estimate=pl.CostEstimate(
            flops=nanoseconds * FLOPS_PER_NS, bytes_accessed=size, transcendentals=0
        ),
    )(*arrays)


def exchange(x, axis):
    return lax.all_to_all(x, axis, split_axis=0, concat_axis=0, tiled=True)


def body(hidden_states, feature_q, feature_k, value_w, window_q, window_k, norm_gain):
    rows = hidden_states.shape[0]
    chunks = lax.axis_size("head")
    width = value_w.shape[1]
    model = value_w.shape[0]
    few = feature_k.shape[1]
    planes, members = lax.axis_size("seq_0"), lax.axis_size("seq_1") * lax.axis_size("seq_2")
    plane = lax.axis_index("seq_0").astype(jnp.int32).reshape(1)
    first = (lax.axis_index(SEQ) == 0).astype(jnp.int32).reshape(1)
    piece = FK * members
    held = -(-PAIR_ROWS * width // (128 * piece)) * piece

    vmem, hbm, smem = pltpu.VMEM, pltpu.HBM, pltpu.SMEM

    (mean,) = call(mean_kernel, [((256, 128), BF16, vmem)], [], 200)
    hidden_states, mean, plane, first = lax.optimization_barrier((hidden_states, mean, plane, first))
    whole = lax.all_gather(hidden_states, "head", tiled=True)
    (state,) = call(
        functools.partial(state_kernel, rows, chunks),
        [((held, 128), BF16, vmem)],
        [(whole, vmem), (feature_k.T, vmem), (value_w, vmem)],
        1500,
        scratch=[pltpu.VMEM((rows, width), BF16), pltpu.VMEM((width // 128, 2 * PAIR_ROWS, rows), BF16)],
    )
    slices = exchange(state.reshape(members, held // members, 128), PLANE)
    slices, whole = lax.optimization_barrier((slices, whole))
    piece_shape = slices.shape[1:]
    (totals,) = call(
        total_kernel,
        [((planes, *piece_shape), BF16, hbm)],
        [(slices, vmem)],
        600,
        scratch=[pltpu.VMEM(piece_shape, BF16), pltpu.SemaphoreType.DMA((planes,))],
    )
    totals = exchange(totals, "seq_0")
    window, head, halo, v = call(
        functools.partial(window_kernel, rows, chunks),
        [
            ((rows - WIN, width), F32, hbm),
            ((WIN, 3 * width), BF16, hbm),
            ((WIN, 2 * width), BF16, hbm),
            ((rows, width), BF16, hbm),
        ],
        [(whole, vmem), (window_q, vmem), (window_k, vmem), (value_w, vmem)],
        3900,
    )
    intra, phi = call(
        functools.partial(intra_kernel, rows, chunks),
        [((rows, width), F32, vmem), ((rows, 3 * width), BF16, vmem)],
        [(whole, vmem), (feature_q.T, hbm), (feature_k.T, hbm), (v, hbm)],
        2200,
    )
    totals, window, head, halo, intra, phi = lax.optimization_barrier(
        (totals, window, head, halo, intra, phi)
    )
    (before,) = call(
        prefix_kernel,
        [(slices.shape, BF16, hbm)],
        [(plane, smem), (slices, vmem), (totals, vmem)],
        1000,
        scratch=[pltpu.VMEM(slices.shape, BF16), pltpu.SemaphoreType.DMA((4,))],
    )
    prefix = exchange(before, PLANE).reshape(held, 128)
    devices = lax.axis_size(SEQ)
    halo = lax.ppermute(halo, SEQ, [(i, i + 1) for i in range(devices - 1)])
    (early,) = call(
        first_window_kernel,
        [((WIN, width), F32, vmem)],
        [(first, smem), (head, vmem), (halo, vmem)],
        1000,
    )
    (mixed,) = call(
        functools.partial(final_kernel, rows),
        [((rows, width), BF16, hbm)],
        [(a, vmem) for a in (prefix, phi, intra, early, window, norm_gain, mean)],
        1400,
        scratch=[pltpu.VMEM((width // 128, rows, 128), BF16), pltpu.SemaphoreType.DMA((width // 128,))],
    )
    return mixed


def solution(mesh):
    split = Mesh(
        mesh.devices.reshape(8, 8, 2, mesh.shape["head"]), ("seq_0", "seq_1", "seq_2", "head")
    )
    placed = (
        P(SEQ, "head"),
        P(None, "head"),
        P(None, "head"),
        P(None, "head"),
        P(None, "head"),
        P(None, "head"),
        P("head"),
    )
    return jax.shard_map(
        body, mesh=split, in_specs=placed, out_specs=P(SEQ, "head"), check_vma=False
    )
```

```python
import functools

import jax
import jax.numpy as jnp
from jax import lax
from jax.experimental import pallas as pl
from jax.experimental.pallas import tpu as pltpu
from jax.sharding import Mesh
from jax.sharding import PartitionSpec as P

FK = 16
HV = 64
WIN = 64
ROLLS = 8
BLOCKS = ROLLS + 2
PAIR_ROWS = BLOCKS * FK
SEQ = ("seq_0", "seq_1", "seq_2")
PLANE = ("seq_1", "seq_2")
F32 = jnp.float32
BF16 = jnp.bfloat16
SHRINK = 2.0**-30
FLOPS_PER_NS = 1_000_000
NT = (((1,), (1,)), ((), ()))


def dot(a, b):
    return jnp.dot(a, b, preferred_element_type=F32)


def project_transposed(w_ref, x_ref, rows, chunks):
    depth = x_ref.shape[1]
    total = None
    for c in range(chunks):
        part = lax.dot_general(
            w_ref[:, c * depth : (c + 1) * depth],
            x_ref[c * rows : (c + 1) * rows, :],
            NT,
            preferred_element_type=F32,
        )
        total = part if total is None else total + part
    return total * FK ** (-0.25)


def project(x_ref, w_ref, rows, chunks):
    depth = x_ref.shape[1]
    total = None
    for c in range(chunks):
        part = dot(x_ref[c * rows : (c + 1) * rows, :], w_ref[c * depth : (c + 1) * depth, :])
        total = part if total is None else total + part
    return total


def features(xt, weight, one):
    total, tokens = xt.shape
    x3 = xt.reshape(total // FK, FK, tokens)
    blocks = [(xt * xt * weight).astype(BF16)]
    for d in range(1, ROLLS):
        rolled = jnp.concatenate([x3[:, d:], x3[:, :d]], axis=1)
        blocks.append((x3 * rolled).reshape(total, tokens).astype(BF16))
    blocks.append(xt.astype(BF16))
    half = x3[:, : FK // 2] * x3[:, FK // 2 :]
    mixed = jnp.concatenate([half, jnp.full_like(half, one)], axis=1)
    blocks.append(mixed.reshape(total, tokens).astype(BF16))
    return blocks


def low_half(shape):
    return lax.broadcasted_iota(jnp.int32, shape, len(shape) - 1) < HV


def first_kernel(x_ref, copies_ref, out_ref):
    for c in range(copies_ref.shape[0]):
        copies_ref[c] = x_ref[...]
    i = lax.broadcasted_iota(jnp.int32, out_ref.shape, 0) % 128
    j = lax.broadcasted_iota(jnp.int32, out_ref.shape, 1)
    out_ref[...] = jnp.where((i < HV) == (j < HV), 1.0 / HV, 0.0).astype(BF16)


def whole_rows(x_ref, rows, chunks):
    return jnp.concatenate([x_ref[c * rows : (c + 1) * rows, :] for c in range(chunks)], axis=1)


def state_kernel(rows, chunks, x_ref, wk_ref, wv_ref, state_ref, v_ref, left_ref):
    x = whole_rows(x_ref, rows, chunks)
    kt = lax.dot_general(wk_ref[...], x, NT, preferred_element_type=F32) * FK ** (-0.25)
    v_ref[...] = dot(x, wv_ref[...]).astype(BF16)
    blocks = features(kt, 1.0, 1.0)
    pairs = left_ref.shape[0]
    for p in range(pairs):
        for n, block in enumerate(blocks):
            left_ref[p, 32 * n : 32 * (n + 1), :] = block[32 * p : 32 * p + 32]
    for p in range(pairs):
        both = dot(left_ref[p], v_ref[:, 128 * p : 128 * p + 128]).reshape(BLOCKS, 2, FK, 128)
        one = jnp.where(low_half((BLOCKS, FK, 128)), both[:, 0], both[:, 1])
        state_ref[PAIR_ROWS * p : PAIR_ROWS * (p + 1), :] = one.reshape(PAIR_ROWS, 128).astype(BF16)
    used = PAIR_ROWS * pairs
    state_ref[used:, :] = jnp.zeros((state_ref.shape[0] - used, 128), BF16)


def window_tiles(tiles, valid):
    low = low_half((WIN, 128))
    logits = []
    for q, keys, _ in tiles:
        none = jnp.zeros_like(q)
        both = jnp.concatenate([jnp.where(low, q, none), jnp.where(low, none, q)], axis=0)
        score = lax.dot_general(both, keys, NT, preferred_element_type=F32)
        logits.append(jnp.where(valid, score * HV ** (-0.5), -1e30))
    logits = jnp.concatenate(logits, axis=0)
    expw = jnp.exp(logits - jnp.max(logits, axis=-1, keepdims=True))
    weights = (expw / jnp.sum(expw, axis=-1, keepdims=True)).astype(BF16)
    outs = []
    for n, (_, _, vals) in enumerate(tiles):
        mixed = dot(weights[2 * WIN * n : 2 * WIN * (n + 1)], vals)
        outs.append(jnp.where(low, mixed[:WIN], mixed[WIN:]))
    return outs


def window_band():
    row = lax.broadcasted_iota(jnp.int32, (2 * WIN, 2 * WIN), 0) % WIN
    col = lax.broadcasted_iota(jnp.int32, (2 * WIN, 2 * WIN), 1)
    return (col <= row + WIN) & (col > row), col


def window_kernel(rows, chunks, x_ref, wq_ref, wk_ref, wv_ref, out_ref, head_ref, halo_ref, v_ref):
    v_ref[...] = dot(whole_rows(x_ref, rows, chunks), wv_ref[...]).astype(BF16)
    keys = project(x_ref, wk_ref, rows, chunks).astype(BF16)
    queries = project(x_ref, wq_ref, rows, chunks).astype(BF16)
    width = keys.shape[1]
    halo_ref[:, :width] = keys[rows - WIN :]
    halo_ref[:, width:] = v_ref[rows - WIN :, :]
    head_ref[:, :width] = queries[:WIN]
    head_ref[:, width : 2 * width] = keys[:WIN]
    head_ref[:, 2 * width :] = v_ref[:WIN, :]
    band, _ = window_band()
    places = [(t, p) for t in range(1, rows // WIN) for p in range(width // 128)]
    tiles = []
    for t, p in places:
        at, seen = slice(128 * p, 128 * p + 128), slice(WIN * (t - 1), WIN * (t + 1))
        tiles.append((queries[WIN * t : WIN * (t + 1), at], keys[seen, at], v_ref[seen, at]))
    for (t, p), out in zip(places, window_tiles(tiles, band)):
        out_ref[WIN * (t - 1) : WIN * t, 128 * p : 128 * p + 128] = out


def first_window_kernel(first_ref, head_ref, halo_ref, out_ref):
    width = out_ref.shape[1]
    band, col = window_band()
    valid = band & ((col >= WIN) | (first_ref[0] == 0))
    tiles = []
    for p in range(width // 128):
        at, at2, at3 = (slice(n * width + 128 * p, n * width + 128 * p + 128) for n in range(3))
        keys = jnp.concatenate([halo_ref[:, at], head_ref[:, at2]], axis=0)
        vals = jnp.concatenate([halo_ref[:, at2], head_ref[:, at3]], axis=0)
        tiles.append((head_ref[:, at], keys, vals))
    for p, out in enumerate(window_tiles(tiles, valid)):
        out_ref[:, 128 * p : 128 * p + 128] = out


def intra_kernel(rows, chunks, x_ref, wq_ref, wk_ref, v_ref, intra_ref, phi_ref):
    qt = project_transposed(wq_ref, x_ref, rows, chunks)
    kt = project_transposed(wk_ref, x_ref, rows, chunks)
    blocks = features(qt, 0.5, 1.0 / (FK // 2))
    heads = qt.shape[0] // FK
    pad = jnp.zeros((384 - 2 * PAIR_ROWS, rows), F32)
    q_hi = qt.astype(BF16).astype(F32)
    q_lo = qt - q_hi
    k_hi = kt.astype(BF16).astype(F32)
    k_lo = kt - k_hi
    zero = jnp.zeros((128 - 3 * FK, rows), F32)
    t = lax.broadcasted_iota(jnp.int32, (rows, rows), 0)
    s = lax.broadcasted_iota(jnp.int32, (rows, rows), 1)
    causal = t >= s
    for p in range(heads // 2):
        phi = jnp.concatenate([b[32 * p : 32 * p + 32].astype(F32) for b in blocks] + [pad], axis=0)
        phi_ref[:, 384 * p : 384 * (p + 1)] = phi.T.astype(BF16)
        vp = v_ref[:, 128 * p : 128 * p + 128]
        outs = []
        for h in (2 * p, 2 * p + 1):
            at = slice(FK * h, FK * (h + 1))
            left = jnp.concatenate([q_hi[at], q_hi[at], q_lo[at], zero], axis=0).T.astype(BF16)
            right = jnp.concatenate([k_hi[at], k_lo[at], k_hi[at], zero], axis=0).astype(BF16)
            a = dot(left, right)
            kern = jnp.where(causal, 1.0 + a + 0.5 * a * a, 0.0).astype(BF16)
            outs.append(dot(kern, vp))
        intra_ref[:, 128 * p : 128 * p + 128] = jnp.where(low_half((rows, 128)), outs[0], outs[1])


def total_kernel(slices_ref, out_hbm, total_ref, sem):
    total = slices_ref[0].astype(F32)
    for i in range(1, slices_ref.shape[0]):
        total = total + slices_ref[i].astype(F32)
    total_ref[...] = total.astype(BF16)
    stores = [pltpu.make_async_copy(total_ref, out_hbm.at[z], sem.at[z]) for z in range(out_hbm.shape[0])]
    for store in stores:
        store.start()
    for store in stores:
        store.wait()


def prefix_kernel(plane_ref, slices_ref, totals_ref, out_hbm, out_ref, sem):
    plane = plane_ref[0]
    run = jnp.zeros(totals_ref.shape[1:], F32)
    for z in range(totals_ref.shape[0]):
        run = run + jnp.where(z < plane, totals_ref[z].astype(F32), 0.0)
    stores = []
    each = slices_ref.shape[0] // sem.shape[0]
    for n in range(sem.shape[0]):
        for i in range(each * n, each * (n + 1)):
            out_ref[i] = run.astype(BF16)
            run = run + slices_ref[i].astype(F32)
        at = pl.ds(each * n, each)
        stores.append(pltpu.make_async_copy(out_ref.at[at], out_hbm.at[at], sem.at[n]))
        stores[n].start()
    for store in stores:
        store.wait()


def final_kernel(
    rows, state_ref, phi_ref, intra_ref, early_ref, window_ref, gain_ref, mean_ref, out_hbm, out_ref, sem
):
    low_state = low_half((BLOCKS, FK, 128))
    pairs = [slice(128 * p, 128 * p + 128) for p in range(intra_ref.shape[1] // 128)]
    linears, squares = [], []
    for p, at in enumerate(pairs):
        state = state_ref[PAIR_ROWS * p : PAIR_ROWS * (p + 1), :].reshape(BLOCKS, FK, 128)
        none = jnp.zeros_like(state)
        even = jnp.where(low_state, state, none)[:, None]
        odd = jnp.where(low_state, none, state)[:, None]
        right = jnp.concatenate([even, odd], axis=1).reshape(2 * PAIR_ROWS, 128)
        right = jnp.concatenate([right, jnp.zeros((384 - 2 * PAIR_ROWS, 128), BF16)], axis=0)
        linears.append(intra_ref[:, at] + dot(phi_ref[:, 384 * p : 384 * (p + 1)], right))
    for linear in linears:
        square = (linear * SHRINK) * (linear * SHRINK)
        hi = square.astype(BF16)
        lo = (square - hi.astype(F32)).astype(BF16)
        squares.append(dot(jnp.concatenate([hi, lo], axis=1), mean_ref[...]))
    stores = []
    for p, at in enumerate(pairs):
        scale = lax.rsqrt(squares[p] + 1e-5 * SHRINK * SHRINK) * SHRINK
        normed = linears[p] * scale * gain_ref[at].reshape(1, 128)
        out_ref[p, :WIN, :] = (normed[:WIN] + early_ref[:, at]).astype(BF16)
        out_ref[p, WIN:, :] = (normed[WIN:] + window_ref[:, at]).astype(BF16)
        stores.append(pltpu.make_async_copy(out_ref.at[p], out_hbm.at[:, at], sem.at[p]))
        stores[p].start()
    for store in stores:
        store.wait()


def call(kernel, outs, args, nanoseconds, scratch=(), vmem=12):
    arrays = [a if space is pltpu.SMEM else pltpu.with_memory_space_constraint(a, space) for a, space in args]
    spaces = [space for _, space in args]
    size = sum(a.size * a.dtype.itemsize for a in arrays)

    def spec(space):
        return pl.BlockSpec(memory_space=pltpu.VMEM if space is pltpu.HBM and not scratch else space)

    return pl.pallas_call(
        kernel,
        out_shape=[space(shape, dtype) for shape, dtype, space in outs],
        in_specs=[spec(space) for space in spaces],
        out_specs=[spec(space) for _, _, space in outs],
        scratch_shapes=list(scratch),
        compiler_params=pltpu.CompilerParams(vmem_limit_bytes=vmem << 20),
        cost_estimate=pl.CostEstimate(
            flops=nanoseconds * FLOPS_PER_NS, bytes_accessed=size, transcendentals=0
        ),
    )(*arrays)


def exchange(x, axis):
    return lax.all_to_all(x, axis, split_axis=0, concat_axis=0, tiled=True)


def body(hidden_states, feature_q, feature_k, value_w, window_q, window_k, norm_gain):
    rows = hidden_states.shape[0]
    chunks = lax.axis_size("head")
    width = value_w.shape[1]
    model = value_w.shape[0]
    few = feature_k.shape[1]
    planes, members = lax.axis_size("seq_0"), lax.axis_size("seq_1") * lax.axis_size("seq_2")
    plane = lax.axis_index("seq_0").astype(jnp.int32).reshape(1)
    first = (lax.axis_index(SEQ) == 0).astype(jnp.int32).reshape(1)
    piece = FK * members
    held = -(-PAIR_ROWS * width // (128 * piece)) * piece

    vmem, hbm, smem = pltpu.VMEM, pltpu.HBM, pltpu.SMEM

    copies, mean = call(
        first_kernel,
        [((chunks, *hidden_states.shape), BF16, vmem), ((256, 128), BF16, vmem)],
        [(hidden_states, hbm)],
        1000,
    )
    copies, mean, plane, first = lax.optimization_barrier((copies, mean, plane, first))
    whole = exchange(copies, "head").reshape(chunks * rows, hidden_states.shape[1])
    (state,) = call(
        functools.partial(state_kernel, rows, chunks),
        [((held, 128), BF16, vmem)],
        [(whole, vmem), (feature_k.T, vmem), (value_w, vmem)],
        1500,
        scratch=[pltpu.VMEM((rows, width), BF16), pltpu.VMEM((width // 128, 2 * PAIR_ROWS, rows), BF16)],
    )
    slices = exchange(state.reshape(members, held // members, 128), PLANE)
    slices, whole = lax.optimization_barrier((slices, whole))
    piece_shape = slices.shape[1:]
    (totals,) = call(
        total_kernel,
        [((planes, *piece_shape), BF16, hbm)],
        [(slices, vmem)],
        600,
        scratch=[pltpu.VMEM(piece_shape, BF16), pltpu.SemaphoreType.DMA((planes,))],
    )
    totals = exchange(totals, "seq_0")
    window, head, halo, v = call(
        functools.partial(window_kernel, rows, chunks),
        [
            ((rows - WIN, width), F32, hbm),
            ((WIN, 3 * width), BF16, hbm),
            ((WIN, 2 * width), BF16, hbm),
            ((rows, width), BF16, hbm),
        ],
        [(whole, vmem), (window_q, vmem), (window_k, vmem), (value_w, vmem)],
        3900,
    )
    intra, phi = call(
        functools.partial(intra_kernel, rows, chunks),
        [((rows, width), F32, vmem), ((rows, 3 * width), BF16, vmem)],
        [(whole, vmem), (feature_q.T, hbm), (feature_k.T, hbm), (v, hbm)],
        2200,
    )
    totals, window, head, halo, intra, phi = lax.optimization_barrier(
        (totals, window, head, halo, intra, phi)
    )
    (before,) = call(
        prefix_kernel,
        [(slices.shape, BF16, hbm)],
        [(plane, smem), (slices, vmem), (totals, vmem)],
        1000,
        scratch=[pltpu.VMEM(slices.shape, BF16), pltpu.SemaphoreType.DMA((4,))],
    )
    prefix = exchange(before, PLANE).reshape(held, 128)
    devices = lax.axis_size(SEQ)
    halo = lax.ppermute(halo, SEQ, [(i, i + 1) for i in range(devices - 1)])
    (early,) = call(
        first_window_kernel,
        [((WIN, width), F32, vmem)],
        [(first, smem), (head, vmem), (halo, vmem)],
        1000,
    )
    (mixed,) = call(
        functools.partial(final_kernel, rows),
        [((rows, width), BF16, hbm)],
        [(a, vmem) for a in (prefix, phi, intra, early, window, norm_gain, mean)],
        1400,
        scratch=[pltpu.VMEM((width // 128, rows, 128), BF16), pltpu.SemaphoreType.DMA((width // 128,))],
    )
    return mixed


def solution(mesh):
    split = Mesh(
        mesh.devices.reshape(8, 8, 2, mesh.shape["head"]), ("seq_0", "seq_1", "seq_2", "head")
    )
    placed = (
        P(SEQ, "head"),
        P(None, "head"),
        P(None, "head"),
        P(None, "head"),
        P(None, "head"),
        P(None, "head"),
        P("head"),
    )
    return jax.shard_map(
        body, mesh=split, in_specs=placed, out_specs=P(SEQ, "head"), check_vma=False
    )
```

```python
import functools

import jax
import jax.numpy as jnp
from jax import lax
from jax.experimental import pallas as pl
from jax.experimental.pallas import tpu as pltpu
from jax.sharding import Mesh
from jax.sharding import PartitionSpec as P

FK = 16
HV = 64
WIN = 64
ROLLS = 8
BLOCKS = ROLLS + 2
PAIR_ROWS = BLOCKS * FK
SEQ = ("seq_0", "seq_1", "seq_2")
PLANE = ("seq_1", "seq_2")
F32 = jnp.float32
BF16 = jnp.bfloat16
SHRINK = 2.0**-30
FLOPS_PER_NS = 1_000_000
NT = (((1,), (1,)), ((), ()))


def dot(a, b):
    return jnp.dot(a, b, preferred_element_type=F32)


def project_transposed(w_ref, x_ref, rows, chunks):
    depth = x_ref.shape[1]
    total = None
    for c in range(chunks):
        part = lax.dot_general(
            w_ref[:, c * depth : (c + 1) * depth],
            x_ref[c * rows : (c + 1) * rows, :],
            NT,
            preferred_element_type=F32,
        )
        total = part if total is None else total + part
    return total * FK ** (-0.25)


def project(x_ref, w_ref, rows, chunks):
    depth = x_ref.shape[1]
    total = None
    for c in range(chunks):
        part = dot(x_ref[c * rows : (c + 1) * rows, :], w_ref[c * depth : (c + 1) * depth, :])
        total = part if total is None else total + part
    return total


def features(xt, weight, one):
    total, tokens = xt.shape
    x3 = xt.reshape(total // FK, FK, tokens)
    blocks = [(xt * xt * weight).astype(BF16)]
    for d in range(1, ROLLS):
        rolled = jnp.concatenate([x3[:, d:], x3[:, :d]], axis=1)
        blocks.append((x3 * rolled).reshape(total, tokens).astype(BF16))
    blocks.append(xt.astype(BF16))
    half = x3[:, : FK // 2] * x3[:, FK // 2 :]
    mixed = jnp.concatenate([half, jnp.full_like(half, one)], axis=1)
    blocks.append(mixed.reshape(total, tokens).astype(BF16))
    return blocks


def low_half(shape):
    return lax.broadcasted_iota(jnp.int32, shape, len(shape) - 1) < HV


def mean_kernel(out_ref):
    i = lax.broadcasted_iota(jnp.int32, out_ref.shape, 0) % 128
    j = lax.broadcasted_iota(jnp.int32, out_ref.shape, 1)
    out_ref[...] = jnp.where((i < HV) == (j < HV), 1.0 / HV, 0.0).astype(BF16)


def whole_rows(x_ref, rows, chunks):
    return jnp.concatenate([x_ref[c * rows : (c + 1) * rows, :] for c in range(chunks)], axis=1)


def state_kernel(rows, chunks, x_ref, wk_ref, wv_ref, state_ref, v_ref, left_ref):
    x = whole_rows(x_ref, rows, chunks)
    kt = lax.dot_general(wk_ref[...], x, NT, preferred_element_type=F32) * FK ** (-0.25)
    v_ref[...] = dot(x, wv_ref[...]).astype(BF16)
    blocks = features(kt, 1.0, 1.0)
    pairs = left_ref.shape[0]
    for p in range(pairs):
        for n, block in enumerate(blocks):
            left_ref[p, 32 * n : 32 * (n + 1), :] = block[32 * p : 32 * p + 32]
    for p in range(pairs):
        both = dot(left_ref[p], v_ref[:, 128 * p : 128 * p + 128]).reshape(BLOCKS, 2, FK, 128)
        one = jnp.where(low_half((BLOCKS, FK, 128)), both[:, 0], both[:, 1])
        state_ref[PAIR_ROWS * p : PAIR_ROWS * (p + 1), :] = one.reshape(PAIR_ROWS, 128).astype(BF16)
    used = PAIR_ROWS * pairs
    state_ref[used:, :] = jnp.zeros((state_ref.shape[0] - used, 128), BF16)


def window_tiles(tiles, valid):
    low = low_half((WIN, 128))
    logits = []
    for q, keys, _ in tiles:
        none = jnp.zeros_like(q)
        both = jnp.concatenate([jnp.where(low, q, none), jnp.where(low, none, q)], axis=0)
        score = lax.dot_general(both, keys, NT, preferred_element_type=F32)
        logits.append(jnp.where(valid, score * HV ** (-0.5), -1e30))
    logits = jnp.concatenate(logits, axis=0)
    expw = jnp.exp(logits - jnp.max(logits, axis=-1, keepdims=True))
    weights = (expw / jnp.sum(expw, axis=-1, keepdims=True)).astype(BF16)
    outs = []
    for n, (_, _, vals) in enumerate(tiles):
        mixed = dot(weights[2 * WIN * n : 2 * WIN * (n + 1)], vals)
        outs.append(jnp.where(low, mixed[:WIN], mixed[WIN:]))
    return outs


def window_band():
    row = lax.broadcasted_iota(jnp.int32, (2 * WIN, 2 * WIN), 0) % WIN
    col = lax.broadcasted_iota(jnp.int32, (2 * WIN, 2 * WIN), 1)
    return (col <= row + WIN) & (col > row), col


def window_kernel(
    rows, chunks, x_ref, wq_hbm, wk_ref, wv_ref, out_hbm, head_hbm, halo_hbm, v_hbm,
    wq_ref, out_ref, head_ref, halo_ref, v_ref, key_ref, sem
):
    load = pltpu.make_async_copy(wq_hbm, wq_ref, sem.at[0])
    load.start()
    x = whole_rows(x_ref, rows, chunks)
    width = key_ref.shape[1]
    v_ref[...] = dot(x, wv_ref[...]).astype(BF16)
    stores = [pltpu.make_async_copy(v_ref, v_hbm, sem.at[1])]
    stores[0].start()
    key_ref[...] = dot(x, wk_ref[...]).astype(BF16)
    halo_ref[:, :width] = key_ref[rows - WIN :, :]
    halo_ref[:, width:] = v_ref[rows - WIN :, :]
    stores.append(pltpu.make_async_copy(halo_ref, halo_hbm, sem.at[2]))
    stores[1].start()
    load.wait()
    queries = dot(x, wq_ref[...]).astype(BF16)
    head_ref[:, :width] = queries[:WIN]
    head_ref[:, width : 2 * width] = key_ref[:WIN, :]
    head_ref[:, 2 * width :] = v_ref[:WIN, :]
    stores.append(pltpu.make_async_copy(head_ref, head_hbm, sem.at[3]))
    stores[2].start()
    band, _ = window_band()
    places = [(t, p) for t in range(1, rows // WIN) for p in range(width // 128)]
    tiles = []
    for t, p in places:
        at, seen = slice(128 * p, 128 * p + 128), slice(WIN * (t - 1), WIN * (t + 1))
        tiles.append((queries[WIN * t : WIN * (t + 1), at], key_ref[seen, at], v_ref[seen, at]))
    for (t, p), out in zip(places, window_tiles(tiles, band)):
        out_ref[WIN * (t - 1) : WIN * t, 128 * p : 128 * p + 128] = out
    stores.append(pltpu.make_async_copy(out_ref, out_hbm, sem.at[4]))
    stores[3].start()
    for store in stores:
        store.wait()


def first_window_kernel(first_ref, head_ref, halo_ref, out_ref):
    width = out_ref.shape[1]
    band, col = window_band()
    valid = band & ((col >= WIN) | (first_ref[0] == 0))
    tiles = []
    for p in range(width // 128):
        at, at2, at3 = (slice(n * width + 128 * p, n * width + 128 * p + 128) for n in range(3))
        keys = jnp.concatenate([halo_ref[:, at], head_ref[:, at2]], axis=0)
        vals = jnp.concatenate([halo_ref[:, at2], head_ref[:, at3]], axis=0)
        tiles.append((head_ref[:, at], keys, vals))
    for p, out in enumerate(window_tiles(tiles, valid)):
        out_ref[:, 128 * p : 128 * p + 128] = out


def intra_kernel(rows, chunks, x_ref, wq_ref, wk_ref, v_ref, intra_ref, phi_ref):
    qt = project_transposed(wq_ref, x_ref, rows, chunks)
    kt = project_transposed(wk_ref, x_ref, rows, chunks)
    blocks = features(qt, 0.5, 1.0 / (FK // 2))
    heads = qt.shape[0] // FK
    pad = jnp.zeros((384 - 2 * PAIR_ROWS, rows), F32)
    q_hi = qt.astype(BF16).astype(F32)
    q_lo = qt - q_hi
    k_hi = kt.astype(BF16).astype(F32)
    k_lo = kt - k_hi
    zero = jnp.zeros((128 - 3 * FK, rows), F32)
    t = lax.broadcasted_iota(jnp.int32, (rows, rows), 0)
    s = lax.broadcasted_iota(jnp.int32, (rows, rows), 1)
    causal = t >= s
    for p in range(heads // 2):
        phi = jnp.concatenate([b[32 * p : 32 * p + 32].astype(F32) for b in blocks] + [pad], axis=0)
        phi_ref[:, 384 * p : 384 * (p + 1)] = phi.T.astype(BF16)
        vp = v_ref[:, 128 * p : 128 * p + 128]
        outs = []
        for h in (2 * p, 2 * p + 1):
            at = slice(FK * h, FK * (h + 1))
            left = jnp.concatenate([q_hi[at], q_hi[at], q_lo[at], zero], axis=0).T.astype(BF16)
            right = jnp.concatenate([k_hi[at], k_lo[at], k_hi[at], zero], axis=0).astype(BF16)
            a = dot(left, right)
            kern = jnp.where(causal, 1.0 + a + 0.5 * a * a, 0.0).astype(BF16)
            outs.append(dot(kern, vp))
        intra_ref[:, 128 * p : 128 * p + 128] = jnp.where(low_half((rows, 128)), outs[0], outs[1])


def total_kernel(slices_ref, out_hbm, total_ref, sem):
    total = slices_ref[0].astype(F32)
    for i in range(1, slices_ref.shape[0]):
        total = total + slices_ref[i].astype(F32)
    total_ref[...] = total.astype(BF16)
    stores = [pltpu.make_async_copy(total_ref, out_hbm.at[z], sem.at[z]) for z in range(out_hbm.shape[0])]
    for store in stores:
        store.start()
    for store in stores:
        store.wait()


def prefix_kernel(plane_ref, slices_ref, totals_ref, out_hbm, out_ref, sem):
    plane = plane_ref[0]
    run = jnp.zeros(totals_ref.shape[1:], F32)
    for z in range(totals_ref.shape[0]):
        run = run + jnp.where(z < plane, totals_ref[z].astype(F32), 0.0)
    stores = []
    each = slices_ref.shape[0] // sem.shape[0]
    for n in range(sem.shape[0]):
        for i in range(each * n, each * (n + 1)):
            out_ref[i] = run.astype(BF16)
            run = run + slices_ref[i].astype(F32)
        at = pl.ds(each * n, each)
        stores.append(pltpu.make_async_copy(out_ref.at[at], out_hbm.at[at], sem.at[n]))
        stores[n].start()
    for store in stores:
        store.wait()


def final_kernel(
    rows, state_ref, phi_ref, intra_ref, early_ref, window_ref, gain_ref, mean_ref, out_hbm, out_ref, sem
):
    low_state = low_half((BLOCKS, FK, 128))
    pairs = [slice(128 * p, 128 * p + 128) for p in range(intra_ref.shape[1] // 128)]
    linears, squares = [], []
    for p, at in enumerate(pairs):
        state = state_ref[PAIR_ROWS * p : PAIR_ROWS * (p + 1), :].reshape(BLOCKS, FK, 128)
        none = jnp.zeros_like(state)
        even = jnp.where(low_state, state, none)[:, None]
        odd = jnp.where(low_state, none, state)[:, None]
        right = jnp.concatenate([even, odd], axis=1).reshape(2 * PAIR_ROWS, 128)
        right = jnp.concatenate([right, jnp.zeros((384 - 2 * PAIR_ROWS, 128), BF16)], axis=0)
        linears.append(intra_ref[:, at] + dot(phi_ref[:, 384 * p : 384 * (p + 1)], right))
    for linear in linears:
        square = (linear * SHRINK) * (linear * SHRINK)
        hi = square.astype(BF16)
        lo = (square - hi.astype(F32)).astype(BF16)
        squares.append(dot(jnp.concatenate([hi, lo], axis=1), mean_ref[...]))
    stores = []
    for p, at in enumerate(pairs):
        scale = lax.rsqrt(squares[p] + 1e-5 * SHRINK * SHRINK) * SHRINK
        normed = linears[p] * scale * gain_ref[at].reshape(1, 128)
        out_ref[p, :WIN, :] = (normed[:WIN] + early_ref[:, at]).astype(BF16)
        out_ref[p, WIN:, :] = (normed[WIN:] + window_ref[:, at]).astype(BF16)
        stores.append(pltpu.make_async_copy(out_ref.at[p], out_hbm.at[:, at], sem.at[p]))
        stores[p].start()
    for store in stores:
        store.wait()


def call(kernel, outs, args, nanoseconds, scratch=(), vmem=12):
    arrays = [a if space is pltpu.SMEM else pltpu.with_memory_space_constraint(a, space) for a, space in args]
    spaces = [space for _, space in args]
    size = sum(a.size * a.dtype.itemsize for a in arrays)

    def spec(space):
        return pl.BlockSpec(memory_space=pltpu.VMEM if space is pltpu.HBM and not scratch else space)

    return pl.pallas_call(
        kernel,
        out_shape=[space(shape, dtype) for shape, dtype, space in outs],
        in_specs=[spec(space) for space in spaces],
        out_specs=[spec(space) for _, _, space in outs],
        scratch_shapes=list(scratch),
        compiler_params=pltpu.CompilerParams(vmem_limit_bytes=vmem << 20),
        cost_estimate=pl.CostEstimate(
            flops=nanoseconds * FLOPS_PER_NS, bytes_accessed=size, transcendentals=0
        ),
    )(*arrays)


def exchange(x, axis):
    return lax.all_to_all(x, axis, split_axis=0, concat_axis=0, tiled=True)


def body(hidden_states, feature_q, feature_k, value_w, window_q, window_k, norm_gain):
    rows = hidden_states.shape[0]
    chunks = lax.axis_size("head")
    width = value_w.shape[1]
    model = value_w.shape[0]
    few = feature_k.shape[1]
    planes, members = lax.axis_size("seq_0"), lax.axis_size("seq_1") * lax.axis_size("seq_2")
    plane = lax.axis_index("seq_0").astype(jnp.int32).reshape(1)
    first = (lax.axis_index(SEQ) == 0).astype(jnp.int32).reshape(1)
    piece = FK * members
    held = -(-PAIR_ROWS * width // (128 * piece)) * piece

    vmem, hbm, smem = pltpu.VMEM, pltpu.HBM, pltpu.SMEM

    (mean,) = call(mean_kernel, [((256, 128), BF16, vmem)], [], 200)
    hidden_states, mean, plane, first = lax.optimization_barrier((hidden_states, mean, plane, first))
    whole = lax.all_gather(hidden_states, "head", tiled=True)
    (state,) = call(
        functools.partial(state_kernel, rows, chunks),
        [((held, 128), BF16, vmem)],
        [(whole, vmem), (feature_k.T, vmem), (value_w, vmem)],
        1500,
        scratch=[pltpu.VMEM((rows, width), BF16), pltpu.VMEM((width // 128, 2 * PAIR_ROWS, rows), BF16)],
    )
    slices = exchange(state.reshape(members, held // members, 128), PLANE)
    slices, whole = lax.optimization_barrier((slices, whole))
    piece_shape = slices.shape[1:]
    (totals,) = call(
        total_kernel,
        [((planes, *piece_shape), BF16, hbm)],
        [(slices, vmem)],
        600,
        scratch=[pltpu.VMEM(piece_shape, BF16), pltpu.SemaphoreType.DMA((planes,))],
    )
    totals = exchange(totals, "seq_0")
    window, head, halo, v = call(
        functools.partial(window_kernel, rows, chunks),
        [
            ((rows - WIN, width), F32, hbm),
            ((WIN, 3 * width), BF16, hbm),
            ((WIN, 2 * width), BF16, hbm),
            ((rows, width), BF16, hbm),
        ],
        [(whole, vmem), (window_q, hbm), (window_k, vmem), (value_w, vmem)],
        3900,
        scratch=[
            pltpu.VMEM((model, width), BF16),
            pltpu.VMEM((rows - WIN, width), F32),
            pltpu.VMEM((WIN, 3 * width), BF16),
            pltpu.VMEM((WIN, 2 * width), BF16),
            pltpu.VMEM((rows, width), BF16),
            pltpu.VMEM((rows, width), BF16),
            pltpu.SemaphoreType.DMA((5,)),
        ],
    )
    intra, phi = call(
        functools.partial(intra_kernel, rows, chunks),
        [((rows, width), F32, vmem), ((rows, 3 * width), BF16, vmem)],
        [(whole, vmem), (feature_q.T, hbm), (feature_k.T, hbm), (v, hbm)],
        2200,
    )
    totals, window, head, halo, intra, phi = lax.optimization_barrier(
        (totals, window, head, halo, intra, phi)
    )
    (before,) = call(
        prefix_kernel,
        [(slices.shape, BF16, hbm)],
        [(plane, smem), (slices, vmem), (totals, vmem)],
        1000,
        scratch=[pltpu.VMEM(slices.shape, BF16), pltpu.SemaphoreType.DMA((4,))],
    )
    prefix = exchange(before, PLANE).reshape(held, 128)
    devices = lax.axis_size(SEQ)
    halo = lax.ppermute(halo, SEQ, [(i, i + 1) for i in range(devices - 1)])
    (early,) = call(
        first_window_kernel,
        [((WIN, width), F32, vmem)],
        [(first, smem), (head, vmem), (halo, vmem)],
        1000,
    )
    (mixed,) = call(
        functools.partial(final_kernel, rows),
        [((rows, width), BF16, hbm)],
        [(a, vmem) for a in (prefix, phi, intra, early, window, norm_gain, mean)],
        1400,
        scratch=[pltpu.VMEM((width // 128, rows, 128), BF16), pltpu.SemaphoreType.DMA((width // 128,))],
    )
    return mixed


def solution(mesh):
    split = Mesh(
        mesh.devices.reshape(8, 8, 2, mesh.shape["head"]), ("seq_0", "seq_1", "seq_2", "head")
    )
    placed = (
        P(SEQ, "head"),
        P(None, "head"),
        P(None, "head"),
        P(None, "head"),
        P(None, "head"),
        P(None, "head"),
        P("head"),
    )
    return jax.shard_map(
        body, mesh=split, in_specs=placed, out_specs=P(SEQ, "head"), check_vma=False
    )
```

```python
import functools

import jax
import jax.numpy as jnp
from jax import lax
from jax.experimental import pallas as pl
from jax.experimental.pallas import tpu as pltpu
from jax.sharding import Mesh
from jax.sharding import PartitionSpec as P

FK = 16
HV = 64
WIN = 64
ROLLS = 8
BLOCKS = ROLLS + 2
PAIR_ROWS = BLOCKS * FK
SEQ = ("seq_0", "seq_1", "seq_2")
PLANE = ("seq_1", "seq_2")
F32 = jnp.float32
BF16 = jnp.bfloat16
SHRINK = 2.0**-30
FLOPS_PER_NS = 1_000_000
NT = (((1,), (1,)), ((), ()))


def dot(a, b):
    return jnp.dot(a, b, preferred_element_type=F32)


def project_transposed(w_ref, x_ref, rows, chunks):
    depth = x_ref.shape[1]
    total = None
    for c in range(chunks):
        part = lax.dot_general(
            w_ref[:, c * depth : (c + 1) * depth],
            x_ref[c * rows : (c + 1) * rows, :],
            NT,
            preferred_element_type=F32,
        )
        total = part if total is None else total + part
    return total * FK ** (-0.25)


def project(x_ref, w_ref, rows, chunks):
    depth = x_ref.shape[1]
    total = None
    for c in range(chunks):
        part = dot(x_ref[c * rows : (c + 1) * rows, :], w_ref[c * depth : (c + 1) * depth, :])
        total = part if total is None else total + part
    return total


def features(xt, weight, one):
    total, tokens = xt.shape
    x3 = xt.reshape(total // FK, FK, tokens)
    blocks = [(xt * xt * weight).astype(BF16)]
    for d in range(1, ROLLS):
        rolled = jnp.concatenate([x3[:, d:], x3[:, :d]], axis=1)
        blocks.append((x3 * rolled).reshape(total, tokens).astype(BF16))
    blocks.append(xt.astype(BF16))
    half = x3[:, : FK // 2] * x3[:, FK // 2 :]
    mixed = jnp.concatenate([half, jnp.full_like(half, one)], axis=1)
    blocks.append(mixed.reshape(total, tokens).astype(BF16))
    return blocks


def low_half(shape):
    return lax.broadcasted_iota(jnp.int32, shape, len(shape) - 1) < HV


def mean_kernel(out_ref):
    i = lax.broadcasted_iota(jnp.int32, out_ref.shape, 0) % 128
    j = lax.broadcasted_iota(jnp.int32, out_ref.shape, 1)
    out_ref[...] = jnp.where((i < HV) == (j < HV), 1.0 / HV, 0.0).astype(BF16)


def whole_rows(x_ref, rows, chunks):
    return jnp.concatenate([x_ref[c * rows : (c + 1) * rows, :] for c in range(chunks)], axis=1)


def state_kernel(rows, chunks, x_ref, wk_ref, wv_ref, state_ref, v_ref, left_ref):
    x = whole_rows(x_ref, rows, chunks)
    kt = lax.dot_general(wk_ref[...], x, NT, preferred_element_type=F32) * FK ** (-0.25)
    v_ref[...] = dot(x, wv_ref[...]).astype(BF16)
    blocks = features(kt, 1.0, 1.0)
    pairs = left_ref.shape[0]
    for p in range(pairs):
        for n, block in enumerate(blocks):
            left_ref[p, 32 * n : 32 * (n + 1), :] = block[32 * p : 32 * p + 32]
    for p in range(pairs):
        both = dot(left_ref[p], v_ref[:, 128 * p : 128 * p + 128]).reshape(BLOCKS, 2, FK, 128)
        one = jnp.where(low_half((BLOCKS, FK, 128)), both[:, 0], both[:, 1])
        state_ref[PAIR_ROWS * p : PAIR_ROWS * (p + 1), :] = one.reshape(PAIR_ROWS, 128).astype(BF16)
    used = PAIR_ROWS * pairs
    state_ref[used:, :] = jnp.zeros((state_ref.shape[0] - used, 128), BF16)


def window_tiles(tiles, valid):
    low = low_half((WIN, 128))
    logits = []
    for q, keys, _ in tiles:
        none = jnp.zeros_like(q)
        both = jnp.concatenate([jnp.where(low, q, none), jnp.where(low, none, q)], axis=0)
        score = lax.dot_general(both, keys, NT, preferred_element_type=F32)
        logits.append(jnp.where(valid, score * HV ** (-0.5), -1e30))
    logits = jnp.concatenate(logits, axis=0)
    expw = jnp.exp(logits - jnp.max(logits, axis=-1, keepdims=True))
    weights = (expw / jnp.sum(expw, axis=-1, keepdims=True)).astype(BF16)
    outs = []
    for n, (_, _, vals) in enumerate(tiles):
        mixed = dot(weights[2 * WIN * n : 2 * WIN * (n + 1)], vals)
        outs.append(jnp.where(low, mixed[:WIN], mixed[WIN:]))
    return outs


def window_band():
    row = lax.broadcasted_iota(jnp.int32, (2 * WIN, 2 * WIN), 0) % WIN
    col = lax.broadcasted_iota(jnp.int32, (2 * WIN, 2 * WIN), 1)
    return (col <= row + WIN) & (col > row), col


def window_kernel(
    rows, chunks, x_ref, wq_hbm, wk_ref, wv_ref, out_hbm, head_hbm, halo_hbm, v_hbm,
    wq_ref, out_ref, head_ref, halo_ref, v_ref, key_ref, sem
):
    load = pltpu.make_async_copy(wq_hbm, wq_ref, sem.at[0])
    load.start()
    x = whole_rows(x_ref, rows, chunks)
    width = key_ref.shape[1]
    v_ref[...] = dot(x, wv_ref[...]).astype(BF16)
    stores = [pltpu.make_async_copy(v_ref, v_hbm, sem.at[1])]
    stores[0].start()
    key_ref[...] = dot(x, wk_ref[...]).astype(BF16)
    halo_ref[:, :width] = key_ref[rows - WIN :, :]
    halo_ref[:, width:] = v_ref[rows - WIN :, :]
    stores.append(pltpu.make_async_copy(halo_ref, halo_hbm, sem.at[2]))
    stores[1].start()
    load.wait()
    queries = dot(x, wq_ref[...]).astype(BF16)
    head_ref[:, :width] = queries[:WIN]
    head_ref[:, width : 2 * width] = key_ref[:WIN, :]
    head_ref[:, 2 * width :] = v_ref[:WIN, :]
    stores.append(pltpu.make_async_copy(head_ref, head_hbm, sem.at[3]))
    stores[2].start()
    band, _ = window_band()
    places = [(t, p) for t in range(1, rows // WIN) for p in range(width // 128)]
    tiles = []
    for t, p in places:
        at, seen = slice(128 * p, 128 * p + 128), slice(WIN * (t - 1), WIN * (t + 1))
        tiles.append((queries[WIN * t : WIN * (t + 1), at], key_ref[seen, at], v_ref[seen, at]))
    for (t, p), out in zip(places, window_tiles(tiles, band)):
        out_ref[WIN * (t - 1) : WIN * t, 128 * p : 128 * p + 128] = out
    stores.append(pltpu.make_async_copy(out_ref, out_hbm, sem.at[4]))
    stores[3].start()
    for store in stores:
        store.wait()


def first_window_kernel(first_ref, head_ref, halo_ref, out_ref):
    width = out_ref.shape[1]
    band, col = window_band()
    valid = band & ((col >= WIN) | (first_ref[0] == 0))
    tiles = []
    for p in range(width // 128):
        at, at2, at3 = (slice(n * width + 128 * p, n * width + 128 * p + 128) for n in range(3))
        keys = jnp.concatenate([halo_ref[:, at], head_ref[:, at2]], axis=0)
        vals = jnp.concatenate([halo_ref[:, at2], head_ref[:, at3]], axis=0)
        tiles.append((head_ref[:, at], keys, vals))
    for p, out in enumerate(window_tiles(tiles, valid)):
        out_ref[:, 128 * p : 128 * p + 128] = out


def intra_kernel(rows, chunks, x_ref, wq_ref, wk_ref, v_ref, intra_ref, phi_ref):
    qt = project_transposed(wq_ref, x_ref, rows, chunks)
    kt = project_transposed(wk_ref, x_ref, rows, chunks)
    blocks = features(qt, 0.5, 1.0 / (FK // 2))
    heads = qt.shape[0] // FK
    pad = jnp.zeros((384 - 2 * PAIR_ROWS, rows), F32)
    q_hi = qt.astype(BF16).astype(F32)
    q_lo = qt - q_hi
    k_hi = kt.astype(BF16).astype(F32)
    k_lo = kt - k_hi
    zero = jnp.zeros((128 - 3 * FK, rows), F32)
    t = lax.broadcasted_iota(jnp.int32, (rows, rows), 0)
    s = lax.broadcasted_iota(jnp.int32, (rows, rows), 1)
    causal = t >= s
    for p in range(heads // 2):
        phi = jnp.concatenate([b[32 * p : 32 * p + 32].astype(F32) for b in blocks] + [pad], axis=0)
        phi_ref[:, 384 * p : 384 * (p + 1)] = phi.T.astype(BF16)
        vp = v_ref[:, 128 * p : 128 * p + 128]
        outs = []
        for h in (2 * p, 2 * p + 1):
            at = slice(FK * h, FK * (h + 1))
            left = jnp.concatenate([q_hi[at], q_hi[at], q_lo[at], zero], axis=0).T.astype(BF16)
            right = jnp.concatenate([k_hi[at], k_lo[at], k_hi[at], zero], axis=0).astype(BF16)
            a = dot(left, right)
            kern = jnp.where(causal, 1.0 + a + 0.5 * a * a, 0.0).astype(BF16)
            outs.append(dot(kern, vp))
        intra_ref[:, 128 * p : 128 * p + 128] = jnp.where(low_half((rows, 128)), outs[0], outs[1])


def total_kernel(slices_ref, out_hbm, total_ref, sem):
    total = slices_ref[0].astype(F32)
    for i in range(1, slices_ref.shape[0]):
        total = total + slices_ref[i].astype(F32)
    total_ref[...] = total.astype(BF16)
    stores = [pltpu.make_async_copy(total_ref, out_hbm.at[z], sem.at[z]) for z in range(out_hbm.shape[0])]
    for store in stores:
        store.start()
    for store in stores:
        store.wait()


def prefix_kernel(plane_ref, slices_ref, totals_ref, out_hbm, out_ref, sem):
    plane = plane_ref[0]
    run = jnp.zeros(totals_ref.shape[1:], F32)
    for z in range(totals_ref.shape[0]):
        run = run + jnp.where(z < plane, totals_ref[z].astype(F32), 0.0)
    stores = []
    each = slices_ref.shape[0] // sem.shape[0]
    for n in range(sem.shape[0]):
        for i in range(each * n, each * (n + 1)):
            out_ref[i] = run.astype(BF16)
            run = run + slices_ref[i].astype(F32)
        at = pl.ds(each * n, each)
        stores.append(pltpu.make_async_copy(out_ref.at[at], out_hbm.at[at], sem.at[n]))
        stores[n].start()
    for store in stores:
        store.wait()


def final_kernel(
    rows, state_ref, phi_ref, intra_ref, early_ref, window_ref, gain_ref, mean_ref, out_hbm, out_ref, sem
):
    low_state = low_half((BLOCKS, FK, 128))
    pairs = [slice(128 * p, 128 * p + 128) for p in range(intra_ref.shape[1] // 128)]
    linears, squares = [], []
    for p, at in enumerate(pairs):
        state = state_ref[PAIR_ROWS * p : PAIR_ROWS * (p + 1), :].reshape(BLOCKS, FK, 128)
        none = jnp.zeros_like(state)
        even = jnp.where(low_state, state, none)[:, None]
        odd = jnp.where(low_state, none, state)[:, None]
        right = jnp.concatenate([even, odd], axis=1).reshape(2 * PAIR_ROWS, 128)
        right = jnp.concatenate([right, jnp.zeros((384 - 2 * PAIR_ROWS, 128), BF16)], axis=0)
        linears.append(intra_ref[:, at] + dot(phi_ref[:, 384 * p : 384 * (p + 1)], right))
    for linear in linears:
        square = (linear * SHRINK) * (linear * SHRINK)
        hi = square.astype(BF16)
        lo = (square - hi.astype(F32)).astype(BF16)
        squares.append(dot(jnp.concatenate([hi, lo], axis=1), mean_ref[...]))
    stores = []
    for p, at in enumerate(pairs):
        scale = lax.rsqrt(squares[p] + 1e-5 * SHRINK * SHRINK) * SHRINK
        normed = linears[p] * scale * gain_ref[at].reshape(1, 128)
        out_ref[p, :WIN, :] = (normed[:WIN] + early_ref[:, at]).astype(BF16)
        out_ref[p, WIN:, :] = (normed[WIN:] + window_ref[:, at]).astype(BF16)
        stores.append(pltpu.make_async_copy(out_ref.at[p], out_hbm.at[:, at], sem.at[p]))
        stores[p].start()
    for store in stores:
        store.wait()


def call(kernel, outs, args, nanoseconds, scratch=(), vmem=12):
    arrays = [a if space is pltpu.SMEM else pltpu.with_memory_space_constraint(a, space) for a, space in args]
    spaces = [space for _, space in args]
    size = sum(a.size * a.dtype.itemsize for a in arrays)

    def spec(space):
        return pl.BlockSpec(memory_space=pltpu.VMEM if space is pltpu.HBM and not scratch else space)

    return pl.pallas_call(
        kernel,
        out_shape=[space(shape, dtype) for shape, dtype, space in outs],
        in_specs=[spec(space) for space in spaces],
        out_specs=[spec(space) for _, _, space in outs],
        scratch_shapes=list(scratch),
        compiler_params=pltpu.CompilerParams(vmem_limit_bytes=vmem << 20),
        cost_estimate=pl.CostEstimate(
            flops=nanoseconds * FLOPS_PER_NS, bytes_accessed=size, transcendentals=0
        ),
    )(*arrays)


def exchange(x, axis):
    return lax.all_to_all(x, axis, split_axis=0, concat_axis=0, tiled=True)


def body(hidden_states, feature_q, feature_k, value_w, window_q, window_k, norm_gain):
    rows = hidden_states.shape[0]
    chunks = lax.axis_size("head")
    width = value_w.shape[1]
    model = value_w.shape[0]
    few = feature_k.shape[1]
    planes, members = lax.axis_size("seq_0"), lax.axis_size("seq_1") * lax.axis_size("seq_2")
    plane = lax.axis_index("seq_0").astype(jnp.int32).reshape(1)
    first = (lax.axis_index(SEQ) == 0).astype(jnp.int32).reshape(1)
    piece = FK * members
    held = -(-PAIR_ROWS * width // (128 * piece)) * piece

    vmem, hbm, smem = pltpu.VMEM, pltpu.HBM, pltpu.SMEM

    (mean,) = call(mean_kernel, [((256, 128), BF16, vmem)], [], 200)
    hidden_states, mean, plane, first = lax.optimization_barrier((hidden_states, mean, plane, first))
    whole = lax.all_gather(hidden_states, "head", tiled=True)
    (state,) = call(
        functools.partial(state_kernel, rows, chunks),
        [((held, 128), BF16, vmem)],
        [(whole, vmem), (feature_k.T, vmem), (value_w, vmem)],
        1500,
        scratch=[pltpu.VMEM((rows, width), BF16), pltpu.VMEM((width // 128, 2 * PAIR_ROWS, rows), BF16)],
    )
    slices = exchange(state.reshape(members, held // members, 128), PLANE)
    slices, whole = lax.optimization_barrier((slices, whole))
    piece_shape = slices.shape[1:]
    (totals,) = call(
        total_kernel,
        [((planes, *piece_shape), BF16, hbm)],
        [(slices, vmem)],
        600,
        scratch=[pltpu.VMEM(piece_shape, BF16), pltpu.SemaphoreType.DMA((planes,))],
    )
    totals = exchange(totals, "seq_0")
    window, head, halo, v = call(
        functools.partial(window_kernel, rows, chunks),
        [
            ((rows - WIN, width), F32, hbm),
            ((WIN, 3 * width), BF16, hbm),
            ((WIN, 2 * width), BF16, hbm),
            ((rows, width), BF16, hbm),
        ],
        [(whole, vmem), (window_q, hbm), (window_k, vmem), (value_w, vmem)],
        3900,
        scratch=[
            pltpu.VMEM((model, width), BF16),
            pltpu.VMEM((rows - WIN, width), F32),
            pltpu.VMEM((WIN, 3 * width), BF16),
            pltpu.VMEM((WIN, 2 * width), BF16),
            pltpu.VMEM((rows, width), BF16),
            pltpu.VMEM((rows, width), BF16),
            pltpu.SemaphoreType.DMA((5,)),
        ],
    )
    totals, window, head, halo, v = lax.optimization_barrier((totals, window, head, halo, v))
    (before,) = call(
        prefix_kernel,
        [(slices.shape, BF16, hbm)],
        [(plane, smem), (slices, vmem), (totals, vmem)],
        1000,
        scratch=[pltpu.VMEM(slices.shape, BF16), pltpu.SemaphoreType.DMA((4,))],
    )
    prefix = exchange(before, PLANE).reshape(held, 128)
    devices = lax.axis_size(SEQ)
    halo = lax.ppermute(halo, SEQ, [(i, i + 1) for i in range(devices - 1)])
    intra, phi = call(
        functools.partial(intra_kernel, rows, chunks),
        [((rows, width), F32, vmem), ((rows, 3 * width), BF16, vmem)],
        [(whole, vmem), (feature_q.T, hbm), (feature_k.T, hbm), (v, hbm)],
        700,
    )
    (early,) = call(
        first_window_kernel,
        [((WIN, width), F32, vmem)],
        [(first, smem), (head, vmem), (halo, vmem)],
        1000,
    )
    (mixed,) = call(
        functools.partial(final_kernel, rows),
        [((rows, width), BF16, hbm)],
        [(a, vmem) for a in (prefix, phi, intra, early, window, norm_gain, mean)],
        1400,
        scratch=[pltpu.VMEM((width // 128, rows, 128), BF16), pltpu.SemaphoreType.DMA((width // 128,))],
    )
    return mixed


def solution(mesh):
    split = Mesh(
        mesh.devices.reshape(8, 8, 2, mesh.shape["head"]), ("seq_0", "seq_1", "seq_2", "head")
    )
    placed = (
        P(SEQ, "head"),
        P(None, "head"),
        P(None, "head"),
        P(None, "head"),
        P(None, "head"),
        P(None, "head"),
        P("head"),
    )
    return jax.shard_map(
        body, mesh=split, in_specs=placed, out_specs=P(SEQ, "head"), check_vma=False
    )
```

```python
import functools

import jax
import jax.numpy as jnp
from jax import lax
from jax.experimental import pallas as pl
from jax.experimental.pallas import tpu as pltpu
from jax.sharding import Mesh
from jax.sharding import PartitionSpec as P

FK = 16
HV = 64
WIN = 64
ROLLS = 8
BLOCKS = ROLLS + 2
PAIR_ROWS = BLOCKS * FK
SEQ = ("seq_0", "seq_1", "seq_2")
PLANE = ("seq_1", "seq_2")
F32 = jnp.float32
BF16 = jnp.bfloat16
SHRINK = 2.0**-30
FLOPS_PER_NS = 1_000_000
NT = (((1,), (1,)), ((), ()))


def dot(a, b):
    return jnp.dot(a, b, preferred_element_type=F32)


def project_transposed(w_ref, x_ref, rows, chunks):
    depth = x_ref.shape[1]
    total = None
    for c in range(chunks):
        part = lax.dot_general(
            w_ref[:, c * depth : (c + 1) * depth],
            x_ref[c * rows : (c + 1) * rows, :],
            NT,
            preferred_element_type=F32,
        )
        total = part if total is None else total + part
    return total * FK ** (-0.25)


def project(x_ref, w_ref, rows, chunks):
    depth = x_ref.shape[1]
    total = None
    for c in range(chunks):
        part = dot(x_ref[c * rows : (c + 1) * rows, :], w_ref[c * depth : (c + 1) * depth, :])
        total = part if total is None else total + part
    return total


def features(xt, weight, one):
    total, tokens = xt.shape
    x3 = xt.reshape(total // FK, FK, tokens)
    blocks = [(xt * xt * weight).astype(BF16)]
    for d in range(1, ROLLS):
        rolled = jnp.concatenate([x3[:, d:], x3[:, :d]], axis=1)
        blocks.append((x3 * rolled).reshape(total, tokens).astype(BF16))
    blocks.append(xt.astype(BF16))
    half = x3[:, : FK // 2] * x3[:, FK // 2 :]
    mixed = jnp.concatenate([half, jnp.full_like(half, one)], axis=1)
    blocks.append(mixed.reshape(total, tokens).astype(BF16))
    return blocks


def low_half(shape):
    return lax.broadcasted_iota(jnp.int32, shape, len(shape) - 1) < HV


def mean_kernel(out_ref):
    i = lax.broadcasted_iota(jnp.int32, out_ref.shape, 0) % 128
    j = lax.broadcasted_iota(jnp.int32, out_ref.shape, 1)
    out_ref[...] = jnp.where((i < HV) == (j < HV), 1.0 / HV, 0.0).astype(BF16)


def whole_rows(x_ref, rows, chunks):
    return jnp.concatenate([x_ref[c * rows : (c + 1) * rows, :] for c in range(chunks)], axis=1)


def state_kernel(rows, chunks, x_ref, wk_ref, wv_ref, state_ref, v_ref, left_ref):
    x = whole_rows(x_ref, rows, chunks)
    kt = lax.dot_general(wk_ref[...], x, NT, preferred_element_type=F32) * FK ** (-0.25)
    v_ref[...] = dot(x, wv_ref[...]).astype(BF16)
    blocks = features(kt, 1.0, 1.0)
    pairs = left_ref.shape[0]
    for p in range(pairs):
        for n, block in enumerate(blocks):
            left_ref[p, 32 * n : 32 * (n + 1), :] = block[32 * p : 32 * p + 32]
    for p in range(pairs):
        both = dot(left_ref[p], v_ref[:, 128 * p : 128 * p + 128]).reshape(BLOCKS, 2, FK, 128)
        one = jnp.where(low_half((BLOCKS, FK, 128)), both[:, 0], both[:, 1])
        state_ref[PAIR_ROWS * p : PAIR_ROWS * (p + 1), :] = one.reshape(PAIR_ROWS, 128).astype(BF16)
    used = PAIR_ROWS * pairs
    state_ref[used:, :] = jnp.zeros((state_ref.shape[0] - used, 128), BF16)


def window_tiles(tiles, valid):
    low = low_half((WIN, 128))
    logits = []
    for q, keys, _ in tiles:
        none = jnp.zeros_like(q)
        both = jnp.concatenate([jnp.where(low, q, none), jnp.where(low, none, q)], axis=0)
        score = lax.dot_general(both, keys, NT, preferred_element_type=F32)
        logits.append(jnp.where(valid, score * HV ** (-0.5), -1e30))
    logits = jnp.concatenate(logits, axis=0)
    expw = jnp.exp(logits - jnp.max(logits, axis=-1, keepdims=True))
    weights = (expw / jnp.sum(expw, axis=-1, keepdims=True)).astype(BF16)
    outs = []
    for n, (_, _, vals) in enumerate(tiles):
        mixed = dot(weights[2 * WIN * n : 2 * WIN * (n + 1)], vals)
        outs.append(jnp.where(low, mixed[:WIN], mixed[WIN:]))
    return outs


def window_band():
    row = lax.broadcasted_iota(jnp.int32, (2 * WIN, 2 * WIN), 0) % WIN
    col = lax.broadcasted_iota(jnp.int32, (2 * WIN, 2 * WIN), 1)
    return (col <= row + WIN) & (col > row), col


def window_kernel(
    rows, chunks, x_ref, wq_hbm, wk_ref, wv_ref, out_hbm, head_hbm, halo_hbm, v_hbm,
    wq_ref, out_ref, head_ref, halo_ref, v_ref, key_ref, sem
):
    load = pltpu.make_async_copy(wq_hbm, wq_ref, sem.at[0])
    load.start()
    x = whole_rows(x_ref, rows, chunks)
    width = key_ref.shape[1]
    v_ref[...] = dot(x, wv_ref[...]).astype(BF16)
    stores = [pltpu.make_async_copy(v_ref, v_hbm, sem.at[1])]
    stores[0].start()
    key_ref[...] = dot(x, wk_ref[...]).astype(BF16)
    halo_ref[:, :width] = key_ref[rows - WIN :, :]
    halo_ref[:, width:] = v_ref[rows - WIN :, :]
    stores.append(pltpu.make_async_copy(halo_ref, halo_hbm, sem.at[2]))
    stores[1].start()
    load.wait()
    queries = dot(x, wq_ref[...]).astype(BF16)
    head_ref[:, :width] = queries[:WIN]
    head_ref[:, width : 2 * width] = key_ref[:WIN, :]
    head_ref[:, 2 * width :] = v_ref[:WIN, :]
    stores.append(pltpu.make_async_copy(head_ref, head_hbm, sem.at[3]))
    stores[2].start()
    band, _ = window_band()
    places = [(t, p) for t in range(1, rows // WIN) for p in range(width // 128)]
    tiles = []
    for t, p in places:
        at, seen = slice(128 * p, 128 * p + 128), slice(WIN * (t - 1), WIN * (t + 1))
        tiles.append((queries[WIN * t : WIN * (t + 1), at], key_ref[seen, at], v_ref[seen, at]))
    for (t, p), out in zip(places, window_tiles(tiles, band)):
        out_ref[WIN * (t - 1) : WIN * t, 128 * p : 128 * p + 128] = out
    stores.append(pltpu.make_async_copy(out_ref, out_hbm, sem.at[4]))
    stores[3].start()
    for store in stores:
        store.wait()


def first_window_kernel(first_ref, head_ref, halo_ref, out_ref):
    width = out_ref.shape[1]
    band, col = window_band()
    valid = band & ((col >= WIN) | (first_ref[0] == 0))
    tiles = []
    for p in range(width // 128):
        at, at2, at3 = (slice(n * width + 128 * p, n * width + 128 * p + 128) for n in range(3))
        keys = jnp.concatenate([halo_ref[:, at], head_ref[:, at2]], axis=0)
        vals = jnp.concatenate([halo_ref[:, at2], head_ref[:, at3]], axis=0)
        tiles.append((head_ref[:, at], keys, vals))
    for p, out in enumerate(window_tiles(tiles, valid)):
        out_ref[:, 128 * p : 128 * p + 128] = out


def intra_kernel(rows, chunks, x_ref, wq_ref, wk_ref, v_ref, intra_ref, phi_ref):
    qt = project_transposed(wq_ref, x_ref, rows, chunks)
    kt = project_transposed(wk_ref, x_ref, rows, chunks)
    blocks = features(qt, 0.5, 1.0 / (FK // 2))
    heads = qt.shape[0] // FK
    pad = jnp.zeros((384 - 2 * PAIR_ROWS, rows), F32)
    q_hi = qt.astype(BF16).astype(F32)
    q_lo = qt - q_hi
    k_hi = kt.astype(BF16).astype(F32)
    k_lo = kt - k_hi
    zero = jnp.zeros((128 - 3 * FK, rows), F32)
    t = lax.broadcasted_iota(jnp.int32, (rows, rows), 0)
    s = lax.broadcasted_iota(jnp.int32, (rows, rows), 1)
    causal = t >= s
    for p in range(heads // 2):
        phi = jnp.concatenate([b[32 * p : 32 * p + 32].astype(F32) for b in blocks] + [pad], axis=0)
        phi_ref[:, 384 * p : 384 * (p + 1)] = phi.T.astype(BF16)
        vp = v_ref[:, 128 * p : 128 * p + 128]
        outs = []
        for h in (2 * p, 2 * p + 1):
            at = slice(FK * h, FK * (h + 1))
            left = jnp.concatenate([q_hi[at], q_hi[at], q_lo[at], zero], axis=0).T.astype(BF16)
            right = jnp.concatenate([k_hi[at], k_lo[at], k_hi[at], zero], axis=0).astype(BF16)
            a = dot(left, right)
            kern = jnp.where(causal, 1.0 + a + 0.5 * a * a, 0.0).astype(BF16)
            outs.append(dot(kern, vp))
        intra_ref[:, 128 * p : 128 * p + 128] = jnp.where(low_half((rows, 128)), outs[0], outs[1])


def total_kernel(slices_ref, out_hbm, total_ref, sem):
    total = slices_ref[0].astype(F32)
    for i in range(1, slices_ref.shape[0]):
        total = total + slices_ref[i].astype(F32)
    total = total.astype(BF16)
    for z in range(total_ref.shape[0]):
        total_ref[z] = total
    store = pltpu.make_async_copy(total_ref, out_hbm, sem)
    store.start()
    store.wait()


def prefix_kernel(plane_ref, slices_ref, totals_ref, out_hbm, out_ref, sem):
    plane = plane_ref[0]
    run = jnp.zeros(totals_ref.shape[1:], F32)
    for z in range(totals_ref.shape[0]):
        run = run + jnp.where(z < plane, totals_ref[z].astype(F32), 0.0)
    stores = []
    each = slices_ref.shape[0] // sem.shape[0]
    for n in range(sem.shape[0]):
        for i in range(each * n, each * (n + 1)):
            out_ref[i] = run.astype(BF16)
            run = run + slices_ref[i].astype(F32)
        at = pl.ds(each * n, each)
        stores.append(pltpu.make_async_copy(out_ref.at[at], out_hbm.at[at], sem.at[n]))
        stores[n].start()
    for store in stores:
        store.wait()


def final_kernel(
    rows, state_ref, phi_ref, intra_ref, early_ref, window_ref, gain_ref, mean_ref, out_hbm, out_ref, sem
):
    low_state = low_half((BLOCKS, FK, 128))
    pairs = [slice(128 * p, 128 * p + 128) for p in range(intra_ref.shape[1] // 128)]
    linears, squares = [], []
    for p, at in enumerate(pairs):
        state = state_ref[PAIR_ROWS * p : PAIR_ROWS * (p + 1), :].reshape(BLOCKS, FK, 128)
        none = jnp.zeros_like(state)
        even = jnp.where(low_state, state, none)[:, None]
        odd = jnp.where(low_state, none, state)[:, None]
        right = jnp.concatenate([even, odd], axis=1).reshape(2 * PAIR_ROWS, 128)
        right = jnp.concatenate([right, jnp.zeros((384 - 2 * PAIR_ROWS, 128), BF16)], axis=0)
        linears.append(intra_ref[:, at] + dot(phi_ref[:, 384 * p : 384 * (p + 1)], right))
    for linear in linears:
        square = (linear * SHRINK) * (linear * SHRINK)
        hi = square.astype(BF16)
        lo = (square - hi.astype(F32)).astype(BF16)
        squares.append(dot(jnp.concatenate([hi, lo], axis=1), mean_ref[...]))
    stores = []
    for p, at in enumerate(pairs):
        scale = lax.rsqrt(squares[p] + 1e-5 * SHRINK * SHRINK) * SHRINK
        normed = linears[p] * scale * gain_ref[at].reshape(1, 128)
        out_ref[p, :WIN, :] = (normed[:WIN] + early_ref[:, at]).astype(BF16)
        out_ref[p, WIN:, :] = (normed[WIN:] + window_ref[:, at]).astype(BF16)
        stores.append(pltpu.make_async_copy(out_ref.at[p], out_hbm.at[:, at], sem.at[p]))
        stores[p].start()
    for store in stores:
        store.wait()


def call(kernel, outs, args, nanoseconds, scratch=(), vmem=12):
    arrays = [a if space is pltpu.SMEM else pltpu.with_memory_space_constraint(a, space) for a, space in args]
    spaces = [space for _, space in args]
    size = sum(a.size * a.dtype.itemsize for a in arrays)

    def spec(space):
        return pl.BlockSpec(memory_space=pltpu.VMEM if space is pltpu.HBM and not scratch else space)

    return pl.pallas_call(
        kernel,
        out_shape=[space(shape, dtype) for shape, dtype, space in outs],
        in_specs=[spec(space) for space in spaces],
        out_specs=[spec(space) for _, _, space in outs],
        scratch_shapes=list(scratch),
        compiler_params=pltpu.CompilerParams(vmem_limit_bytes=vmem << 20),
        cost_estimate=pl.CostEstimate(
            flops=nanoseconds * FLOPS_PER_NS, bytes_accessed=size, transcendentals=0
        ),
    )(*arrays)


def exchange(x, axis):
    return lax.all_to_all(x, axis, split_axis=0, concat_axis=0, tiled=True)


def body(hidden_states, feature_q, feature_k, value_w, window_q, window_k, norm_gain):
    rows = hidden_states.shape[0]
    chunks = lax.axis_size("head")
    width = value_w.shape[1]
    model = value_w.shape[0]
    few = feature_k.shape[1]
    planes, members = lax.axis_size("seq_0"), lax.axis_size("seq_1") * lax.axis_size("seq_2")
    plane = lax.axis_index("seq_0").astype(jnp.int32).reshape(1)
    first = (lax.axis_index(SEQ) == 0).astype(jnp.int32).reshape(1)
    piece = FK * members
    held = -(-PAIR_ROWS * width // (128 * piece)) * piece

    vmem, hbm, smem = pltpu.VMEM, pltpu.HBM, pltpu.SMEM

    (mean,) = call(mean_kernel, [((256, 128), BF16, vmem)], [], 200)
    hidden_states, mean, plane, first = lax.optimization_barrier((hidden_states, mean, plane, first))
    whole = lax.all_gather(hidden_states, "head", tiled=True)
    (state,) = call(
        functools.partial(state_kernel, rows, chunks),
        [((held, 128), BF16, vmem)],
        [(whole, vmem), (feature_k.T, vmem), (value_w, vmem)],
        1500,
        scratch=[pltpu.VMEM((rows, width), BF16), pltpu.VMEM((width // 128, 2 * PAIR_ROWS, rows), BF16)],
    )
    slices = exchange(state.reshape(members, held // members, 128), PLANE)
    slices, whole = lax.optimization_barrier((slices, whole))
    piece_shape = slices.shape[1:]
    (totals,) = call(
        total_kernel,
        [((planes, *piece_shape), BF16, hbm)],
        [(slices, vmem)],
        600,
        scratch=[pltpu.VMEM((planes, *piece_shape), BF16), pltpu.SemaphoreType.DMA(())],
    )
    totals = exchange(totals, "seq_0")
    window, head, halo, v = call(
        functools.partial(window_kernel, rows, chunks),
        [
            ((rows - WIN, width), F32, hbm),
            ((WIN, 3 * width), BF16, hbm),
            ((WIN, 2 * width), BF16, hbm),
            ((rows, width), BF16, hbm),
        ],
        [(whole, vmem), (window_q, hbm), (window_k, vmem), (value_w, vmem)],
        3900,
        scratch=[
            pltpu.VMEM((model, width), BF16),
            pltpu.VMEM((rows - WIN, width), F32),
            pltpu.VMEM((WIN, 3 * width), BF16),
            pltpu.VMEM((WIN, 2 * width), BF16),
            pltpu.VMEM((rows, width), BF16),
            pltpu.VMEM((rows, width), BF16),
            pltpu.SemaphoreType.DMA((5,)),
        ],
    )
    intra, phi = call(
        functools.partial(intra_kernel, rows, chunks),
        [((rows, width), F32, vmem), ((rows, 3 * width), BF16, vmem)],
        [(whole, vmem), (feature_q.T, hbm), (feature_k.T, hbm), (v, hbm)],
        2200,
    )
    totals, window, head, halo, intra, phi = lax.optimization_barrier(
        (totals, window, head, halo, intra, phi)
    )
    (before,) = call(
        prefix_kernel,
        [(slices.shape, BF16, hbm)],
        [(plane, smem), (slices, vmem), (totals, vmem)],
        1000,
        scratch=[pltpu.VMEM(slices.shape, BF16), pltpu.SemaphoreType.DMA((2,))],
    )
    prefix = exchange(before, PLANE).reshape(held, 128)
    devices = lax.axis_size(SEQ)
    halo = lax.ppermute(halo, SEQ, [(i, i + 1) for i in range(devices - 1)])
    (early,) = call(
        first_window_kernel,
        [((WIN, width), F32, vmem)],
        [(first, smem), (head, vmem), (halo, vmem)],
        1000,
    )
    (mixed,) = call(
        functools.partial(final_kernel, rows),
        [((rows, width), BF16, hbm)],
        [(a, vmem) for a in (prefix, phi, intra, early, window, norm_gain, mean)],
        1400,
        scratch=[pltpu.VMEM((width // 128, rows, 128), BF16), pltpu.SemaphoreType.DMA((width // 128,))],
    )
    return mixed


def solution(mesh):
    split = Mesh(
        mesh.devices.reshape(8, 8, 2, mesh.shape["head"]), ("seq_0", "seq_1", "seq_2", "head")
    )
    placed = (
        P(SEQ, "head"),
        P(None, "head"),
        P(None, "head"),
        P(None, "head"),
        P(None, "head"),
        P(None, "head"),
        P("head"),
    )
    return jax.shard_map(
        body, mesh=split, in_specs=placed, out_specs=P(SEQ, "head"), check_vma=False
    )
```
